32 devices in a mesh: region: 4 (over x, core), dom: 8 (over z, y).
Axes of the slice: x: 2, y: 2, z: 4, core: 2. Of those that a mesh axis runs over, the one named last changes fastest.
Arguments:
- params: float32 [59, 32768], P(None, ('region', 'dom')), may hold values from -6.4 to 6.4, as said below
- first_moment: float32 [59, 32768], P(None, ('region', 'dom')), may hold values from -0.3 to 0.3
- second_moment: float32 [59, 32768], P(None, ('region', 'dom')), may hold values from 0.0001 to 0.01
- piece_blocks: int32 [32, 32, 2], P(('region', 'dom')), may hold values from 0 to 9, all different within a row
- piece_live: int32 [32, 32], P(('region', 'dom')), may hold values from 1 to 2
- piece_owner: int32 [32, 32], P(('region', 'dom')), may hold values from 0 to 7, as said below
- piece_cell: int32 [32, 32], P(('region', 'dom')), may hold values from 0 to 63, as said below
- target: float32 [32, 8, 3, 256], P(('region', 'dom')), may hold values from 0 to 1
- background: float32 [3], replicated, may hold values from 0 to 1
Outputs:
- gradient: float32 [59, 32768], P(None, ('region', 'dom'))
- new_params: float32 [59, 32768], P(None, ('region', 'dom'))
- new_first: float32 [59, 32768], P(None, ('region', 'dom'))
- new_second: float32 [59, 32768], P(None, ('region', 'dom'))
The draws below stay inside these ranges and needn't reach their ends.
Inputs may be any that keep to these rules, and one draw needn't show every extreme that they name: `params`: rows 0 to 2: z in [2, 4], x / z and y / z in [-1.6, 1.6]; rows 3 to 5 in [-0.9, 0.2]; row 6 in [0.5, 1.5]; rows 7 to 9 in [-1, 1]; row 10 in [-5.5, -1.8]; rows 11 to 58 in [-2, 2]. `piece_blocks`: the entries of one list are different pool blocks. `piece_owner`: each part sends at most 8 pieces to one owner; in every region some owner receives exactly 8 pieces from every part. `piece_cell`: the pieces that one owner receives have different cells.
All inputs are finite; a program needn't handle non-finite values.
Results may differ from the reference program's by a relative error of at most 0.0003.
Values sent between devices are 32-bit elements; how exact they have to be, the bound alone decides.
No kernel may reach another device: no remote copies, remote signals or barrier semaphores. Data moves between devices by JAX's collectives and lax.ppermute only.
A program may use at most 64 MiB of HBM per device.

```python
import math
import jax
import jax.numpy as jnp
from jax import lax

PARAMS = 59
TSIDE = 16
WIN = 8
BLOCK = 128
BLOCKS = 8
KB = 2
MAXD = 8
PIECES = 32
PIX = 256
TILE_DEV = 8
CELLS = 64
POOL = 10
SENDERS = 32
GAUSS = 32768
N_REGION = 4
N_DOM = 8


def draw_params(key, part):
    keys = jax.random.split(jax.random.fold_in(key, 11), 7)
    depth_z = jax.random.uniform(keys[0], (1, GAUSS), minval=2.0, maxval=4.0)
    across = jax.random.uniform(keys[1], (2, GAUSS), minval=-1.6, maxval=1.6) * depth_z
    quat_w = jax.random.uniform(keys[3], (1, GAUSS), minval=0.5, maxval=1.5)
    quat_rest = jax.random.uniform(keys[4], (3, GAUSS), minval=-1.0, maxval=1.0)
    degree_scale = jnp.concatenate([jnp.full((1,), 0.6), jnp.full((15,), 0.25)])[None, :, None]
    log_scales = jax.random.uniform(keys[2], (3, GAUSS), minval=-0.7, maxval=0.0)
    logits = jax.random.uniform(keys[5], (1, GAUSS), minval=-5.0, maxval=-2.0)
    coeffs = jax.random.normal(keys[6], (3, 16, GAUSS)) * degree_scale
    coeffs = jnp.clip(coeffs, -2.0, 2.0).reshape(48, GAUSS)
    return jnp.concatenate([across, depth_z, log_scales, quat_w, quat_rest, logits, coeffs], axis=0).astype(jnp.float32)


def routing_draw(key):
    base = jax.random.fold_in(key, 29)
    regions = SENDERS // N_DOM
    capacity = 2 * PIECES // N_DOM
    slot_total = N_DOM * capacity
    region_keys = jax.random.split(jax.random.fold_in(base, 1), regions)
    full_owner = jax.vmap(lambda one_key: jax.random.randint(one_key, (), 0, N_DOM))(region_keys)
    full_each = jnp.repeat(full_owner, N_DOM)
    sender_keys = jax.random.split(jax.random.fold_in(base, 2), SENDERS)

    def choose(one_key, full_dest):
        scores = jax.random.permutation(one_key, slot_total)
        slot_ids = jnp.arange(slot_total)
        scores = jnp.where(slot_ids // capacity == full_dest, slot_ids - slot_total, scores)
        picked = jnp.argsort(scores, stable=True)[:PIECES]
        mixed = jax.random.permutation(jax.random.fold_in(one_key, 3), picked)
        return mixed // capacity
    owners = jax.vmap(choose)(sender_keys, full_each)
    onehot = (owners[:, :, None] == jnp.arange(N_DOM)[None, None, :]).astype(jnp.int32)
    position = jnp.sum((jnp.cumsum(onehot, axis=1) - onehot) * onehot, axis=2)
    owner_keys = jax.random.split(jax.random.fold_in(base, 4), SENDERS)
    perms = jax.vmap(lambda one_key: jax.random.permutation(one_key, slot_total))(owner_keys).reshape(regions, N_DOM, slot_total)
    region_of = jnp.arange(SENDERS) // N_DOM
    dom_of = jnp.arange(SENDERS) % N_DOM
    cells = perms[region_of[:, None], owners, dom_of[:, None] * capacity + position]
    return (owners.astype(jnp.int32), cells.astype(jnp.int32))


def draw_piece_owner(key, part):
    return routing_draw(key)[0]


def draw_piece_cell(key, part):
    return routing_draw(key)[1]


def place_ends(result, rng, smallest, high):
    longest = result.shape.index(max(result.shape))
    spots = []
    for shift in (0, 1):
        where = [jax.random.randint(jax.random.fold_in(rng, axis), (), 0, length) for axis, length in enumerate(result.shape)]
        where[longest] = (where[longest] + shift) % result.shape[longest]
        spots.append(tuple(where))
    return result.at[spots[0]].set(smallest).at[spots[1]].set(high)


def block_scale(rng, extent, cuts, low, top_value):
    def one(axis_at, shards_of):
        draws = jax.random.uniform(jax.random.fold_in(jax.random.fold_in(rng, 6), axis_at), (shards_of,), jnp.float32, low / len(cuts), top_value / len(cuts))
        return jnp.repeat(jnp.exp(draws), extent[axis_at] // shards_of).reshape((-1,) + (1,) * (len(extent) - axis_at - 1))

    factor_of = one(*cuts[0])
    for cut in cuts[1:]:
        factor_of = factor_of * one(*cut)
    return factor_of


def picks_of(stream_key, rows, count, top, lift):
    sequence = jax.random.permutation(jax.random.fold_in(stream_key, 1), count)
    pull = sequence
    for power in range(3):
        pull = pull * pull // count
    pull = pull * lift // count
    lots = jax.random.randint(jax.random.fold_in(stream_key, 2), (rows, count), 0, 4096) + pull
    holders = jax.random.permutation(jax.random.fold_in(stream_key, 3), rows)[jnp.arange(count) % rows]
    lots = jnp.where(jnp.arange(rows)[:, None] == holders[None, :], 1 << 14, lots)
    priority = lots * count + jnp.arange(count)
    return lax.top_k(priority.astype(jnp.int32), top)[1].astype(jnp.int32)


def gaussian(rng, dims, scale, reach, cuts=(), kind=jnp.bfloat16):
    result = jax.random.normal(rng, dims, jnp.float32) * scale
    if len(cuts) > 0:
        result = block_scale(rng, dims, cuts, -0.22, 0.18) * result
    return jnp.clip(result, min=-reach, max=reach).astype(kind)


def setup_inputs(seed: int = 0) -> dict:
    key_list = jax.random.split(jax.random.key(seed), 10)
    return {
        "params": draw_params(jax.random.fold_in(key_list[9], 71), 0),
        "first_moment": gaussian(key_list[1], (PARAMS, GAUSS), 0.05, 0.3, ((1, 32),), jnp.float32),
        "second_moment": jnp.clip(jnp.exp(math.log(0.01) - 4.6051702 * jax.random.uniform(key_list[2], (PARAMS, GAUSS), jnp.float32) ** block_scale(key_list[2], (PARAMS, GAUSS), ((1, 32),), -0.2, 0.2)), 0.0001, 0.01),
        "piece_blocks": picks_of(key_list[3], SENDERS * PIECES, POOL, KB, 0).reshape((SENDERS, PIECES, KB)),
        "piece_live": place_ends(jax.random.randint(key_list[4], (SENDERS, PIECES), 1, KB + 1), jax.random.fold_in(key_list[4], 1), 1, KB).astype(jnp.int32),
        "piece_owner": draw_piece_owner(jax.random.fold_in(key_list[9], 71), 0),
        "piece_cell": draw_piece_cell(jax.random.fold_in(key_list[9], 71), 0),
        "target": jnp.clip(1.0 * jax.random.uniform(key_list[7], (SENDERS, TILE_DEV, 3, PIX), jnp.float32) ** block_scale(key_list[7], (SENDERS, TILE_DEV, 3, PIX), ((0, 32),), -0.2, 0.2), 0.0, 1.0),
        "background": jnp.clip(jax.random.uniform(key_list[8], (3,), jnp.float32, 0.0, 1.0), 0.0, 1.0),
    }


harmonic_zero = 0.28209479177387814
harmonic_one = 0.4886025119029199
harmonic_two = (1.0925484305920792, -1.0925484305920792, 0.31539156525252005, -1.0925484305920792, 0.5462742152960396)
harmonic_three = (-0.5900435899266435, 2.890611442640554, -0.4570457994644658, 0.3731763325901154, -0.4570457994644658, 1.445305721320277, -0.5900435899266435)
beta_one = 0.9
beta_two = 0.999
rate = 0.001
adam_step = 100
tiny = 1e-08

def splat_table(block, screen_px):
    mean_x, mean_y, mean_z = (block[0], block[1], block[2])
    scales = jnp.exp(block[3:6])
    quat_raw = block[6:10]
    quat_norm = quat_raw / jnp.sqrt(lax.optimization_barrier(jnp.sum(quat_raw * quat_raw, axis=0)))
    quat_w, quat_x, quat_y, quat_z = (quat_norm[0], quat_norm[1], quat_norm[2], quat_norm[3])
    rotation = [[1 - 2 * (quat_y * quat_y + quat_z * quat_z), 2 * (quat_x * quat_y - quat_w * quat_z), 2 * (quat_x * quat_z + quat_w * quat_y)], [2 * (quat_x * quat_y + quat_w * quat_z), 1 - 2 * (quat_x * quat_x + quat_z * quat_z), 2 * (quat_y * quat_z - quat_w * quat_x)], [2 * (quat_x * quat_z - quat_w * quat_y), 2 * (quat_y * quat_z + quat_w * quat_x), 1 - 2 * (quat_x * quat_x + quat_y * quat_y)]]
    focal_px = 0.3125 * screen_px
    inv_z = 1.0 / mean_z
    jac_rows = [[focal_px * inv_z, 0.0 * inv_z, -focal_px * mean_x * inv_z * inv_z], [0.0 * inv_z, focal_px * inv_z, -focal_px * mean_y * inv_z * inv_z]]
    projected = []
    for out_row in range(2):
        entries = []
        for out_col in range(3):
            acc_term = jac_rows[out_row][0] * rotation[0][out_col]
            acc_term = acc_term + jac_rows[out_row][1] * rotation[1][out_col]
            acc_term = acc_term + jac_rows[out_row][2] * rotation[2][out_col]
            entries.append(acc_term * scales[out_col])
        projected.append(entries)
    sigma_xx = projected[0][0] * projected[0][0] + projected[0][1] * projected[0][1] + projected[0][2] * projected[0][2] + 0.3
    sigma_xy = projected[0][0] * projected[1][0] + projected[0][1] * projected[1][1] + projected[0][2] * projected[1][2]
    sigma_yy = projected[1][0] * projected[1][0] + projected[1][1] * projected[1][1] + projected[1][2] * projected[1][2] + 0.3
    determinant = sigma_xx * sigma_yy - sigma_xy * sigma_xy
    conic_xx = sigma_yy / determinant
    conic_xy = -sigma_xy / determinant
    conic_yy = sigma_xx / determinant
    centre_u = 0.5 * screen_px + focal_px * mean_x * inv_z
    centre_v = 0.5 * screen_px + focal_px * mean_y * inv_z
    opacity = jax.nn.sigmoid(block[10])
    length = jnp.sqrt(mean_x * mean_x + mean_y * mean_y + mean_z * mean_z)
    dir_x, dir_y, dir_z = (mean_x / length, mean_y / length, mean_z / length)
    sq_x, sq_y, sq_z = (dir_x * dir_x, dir_y * dir_y, dir_z * dir_z)
    harmonics = [harmonic_zero + 0.0 * dir_x, -harmonic_one * dir_y, harmonic_one * dir_z, -harmonic_one * dir_x, harmonic_two[0] * dir_x * dir_y, harmonic_two[1] * dir_y * dir_z, harmonic_two[2] * (2 * sq_z - sq_x - sq_y), harmonic_two[3] * dir_x * dir_z, harmonic_two[4] * (sq_x - sq_y), harmonic_three[0] * dir_y * (3 * sq_x - sq_y), harmonic_three[1] * dir_x * dir_y * dir_z, harmonic_three[2] * dir_y * (4 * sq_z - sq_x - sq_y), harmonic_three[3] * dir_z * (2 * sq_z - 3 * sq_x - 3 * sq_y), harmonic_three[4] * dir_x * (4 * sq_z - sq_x - sq_y), harmonic_three[5] * dir_z * (sq_x - sq_y), harmonic_three[6] * dir_x * (sq_x - 3 * sq_y)]
    basis = jnp.stack(harmonics, axis=0)
    coeffs = block[11:59].reshape(3, 16, block.shape[1])
    colour = jnp.maximum(lax.optimization_barrier(jnp.sum(coeffs * basis[None], axis=1)) + 0.5, 0.0)
    return jnp.stack([centre_u, centre_v, conic_xx, conic_xy, conic_yy, opacity, colour[0], colour[1], colour[2]], axis=0)

def pool_terms(table, present):
    screen_px = float(WIN * TSIDE)
    flat = table.reshape(table.shape[0], table.shape[1] * table.shape[2])
    terms = splat_table(flat, screen_px).reshape(9, table.shape[1], table.shape[2])
    return jnp.where(present[None, :, None] > 0, terms, jnp.zeros_like(terms))

def render_piece(chosen, slot_flags, tile_index):
    pixels = jnp.arange(TSIDE * TSIDE, dtype=jnp.int32)
    column = tile_index % WIN
    tile_row = tile_index // WIN
    pixel_x = (TSIDE * column + pixels % TSIDE).astype(chosen.dtype) + 0.5
    pixel_y = (TSIDE * tile_row + pixels // TSIDE).astype(chosen.dtype) + 0.5
    carry_log = jnp.zeros((TSIDE * TSIDE,), chosen.dtype)
    colour_sum = jnp.zeros((3, TSIDE * TSIDE), chosen.dtype)
    for slot_no in range(chosen.shape[1]):
        terms = chosen[:, slot_no]
        centre_u, centre_v, conic_xx, conic_xy, conic_yy, opacity = (terms[0], terms[1], terms[2], terms[3], terms[4], terms[5])
        colour = terms[6:9]
        offset_x = pixel_x[None, :] - centre_u[:, None]
        offset_y = pixel_y[None, :] - centre_v[:, None]
        quadratic = conic_xx[:, None] * offset_x * offset_x + 2.0 * conic_xy[:, None] * offset_x * offset_y + conic_yy[:, None] * offset_y * offset_y
        alphas = (opacity * slot_flags[slot_no])[:, None] * jnp.exp(-0.5 * quadratic)
        log_keep = jnp.log1p(-alphas)
        before = carry_log[None, :] + jnp.cumsum(log_keep, axis=0) - log_keep
        weight = alphas * jnp.exp(before)
        colour_sum = colour_sum + jnp.dot(colour, weight, precision=lax.Precision.HIGHEST)
        carry_log = carry_log + lax.optimization_barrier(jnp.sum(log_keep, axis=0))
    return jnp.concatenate([colour_sum, jnp.exp(carry_log)[None, :]], axis=0)

def render_listed(terms, present, blocks_row, live_row, tile_index):
    chosen = terms[:, blocks_row]
    slot_ids = jnp.arange(blocks_row.shape[0], dtype=jnp.int32)
    slot_flags = present[blocks_row] * (slot_ids < live_row).astype(present.dtype)
    return render_piece(chosen, slot_flags, tile_index)

def build_pools(params):
    own_cols = params.reshape(PARAMS, N_REGION, N_DOM, BLOCKS * BLOCK)
    blank = jnp.zeros_like(own_cols[:, :1, :, :BLOCK])
    lower = jnp.concatenate([blank, own_cols[:, :-1, :, -BLOCK:]], axis=1)
    upper = jnp.concatenate([own_cols[:, 1:, :, :BLOCK], blank], axis=1)
    pooled = jnp.concatenate([lower, own_cols, upper], axis=3)
    pooled = pooled.reshape(PARAMS, N_REGION * N_DOM, POOL, BLOCK)
    return jnp.transpose(pooled, (1, 0, 2, 3))

def build_present(dtype_like):
    region_of = jnp.arange(N_REGION * N_DOM, dtype=jnp.int32) // N_DOM
    low_flag = (region_of > 0).astype(dtype_like.dtype)[:, None]
    high_flag = (region_of < N_REGION - 1).astype(dtype_like.dtype)[:, None]
    middle = jnp.ones((N_REGION * N_DOM, BLOCKS), dtype_like.dtype)
    return jnp.concatenate([low_flag, middle, high_flag], axis=1)

def total_loss(params, piece_blocks, piece_live, piece_owner, piece_cell, target, background):
    pools = build_pools(params)
    present = build_present(params)
    tile_ids = jnp.arange(PIECES, dtype=jnp.int32)

    def one_part(items):
        table, flags, blocks_part, live_part = items
        terms = pool_terms(table, flags)
        return jax.vmap(render_listed, in_axes=(None, None, 0, 0, 0))(terms, flags, blocks_part, live_part, tile_ids)
    pieces = lax.map(jax.checkpoint(one_part), (pools, present, piece_blocks, piece_live))
    pieces = pieces.reshape(N_REGION, N_DOM * PIECES, 4, PIX)
    cell_index = (piece_owner * CELLS + piece_cell).reshape(N_REGION, N_DOM * PIECES)
    empty = jnp.concatenate([jnp.zeros((N_DOM * CELLS, 3, PIX), pieces.dtype), jnp.ones((N_DOM * CELLS, 1, PIX), pieces.dtype)], axis=1)
    cell_grid = jax.vmap(lambda where_to, values: empty.at[where_to].set(values))(cell_index, pieces)
    cell_grid = cell_grid.reshape(N_REGION, N_DOM, TILE_DEV, MAXD, 4, PIX)
    in_front = jnp.ones((N_REGION, N_DOM, TILE_DEV, PIX), pieces.dtype)
    composite = jnp.zeros((N_REGION, N_DOM, TILE_DEV, 3, PIX), pieces.dtype)
    for depth_slot in range(MAXD):
        composite = composite + in_front[:, :, :, None, :] * cell_grid[:, :, :, depth_slot, :3]
        in_front = in_front * cell_grid[:, :, :, depth_slot, 3]
    composite = composite + in_front[:, :, :, None, :] * background[:, None]
    residual = composite - target.reshape(N_REGION, N_DOM, TILE_DEV, 3, PIX)
    return 0.5 * jnp.sum(residual * residual)

def reference(params, first_moment, second_moment, piece_blocks, piece_live, piece_owner, piece_cell, target, background):
    gradient = jax.grad(total_loss)(params, piece_blocks, piece_live, piece_owner, piece_cell, target, background)
    new_first = beta_one * first_moment + (1 - beta_one) * gradient
    new_second = beta_two * second_moment + (1 - beta_two) * gradient * gradient
    update = new_first / (1 - beta_one ** adam_step) / (jnp.sqrt(new_second / (1 - beta_two ** adam_step)) + tiny)
    new_params = params - rate * update
    return (gradient, new_params, new_first, new_second)
```

```python
import math

import numpy as np
import jax
import jax.numpy as jnp
from jax import lax
from jax.experimental import pallas as pl
from jax.experimental.pallas import tpu as pltpu
from jax.sharding import PartitionSpec as P

PARAMS = 59
TSIDE = 16
WIN = 8
BLOCK = 128
MAXD = 8
PIX = 256

harmonic_zero = 0.28209479177387814
harmonic_one = 0.4886025119029199
harmonic_two = (
    1.0925484305920792,
    -1.0925484305920792,
    0.31539156525252005,
    -1.0925484305920792,
    0.5462742152960396,
)
harmonic_three = (
    -0.5900435899266435,
    2.890611442640554,
    -0.4570457994644658,
    0.3731763325901154,
    -0.4570457994644658,
    1.445305721320277,
    -0.5900435899266435,
)
beta_one = 0.9
beta_two = 0.999
rate = 0.001
adam_step = 100
tiny = 1e-08
log2_e = math.log2(math.e)
ln_2 = math.log(2.0)

LANES = 128
SUBL = 8
ROWS = BLOCK // SUBL
GROUP = LANES // 4
BASIS = 16
KE = 3 * BASIS
KC = 6 * SUBL
SLOTS = 16
f32 = jnp.float32
bf16 = jnp.bfloat16


def splat_rows(rows):
    mean_x, mean_y, mean_z = rows[0], rows[1], rows[2]
    scales = [jnp.exp(rows[3]), jnp.exp(rows[4]), jnp.exp(rows[5])]
    norm_sq = rows[6] * rows[6] + rows[7] * rows[7] + rows[8] * rows[8] + rows[9] * rows[9]
    inv_norm = 1.0 / jnp.sqrt(norm_sq)
    quat_w, quat_x, quat_y, quat_z = [rows[6 + i] * inv_norm for i in range(4)]
    rotation = [
        [
            1 - 2 * (quat_y * quat_y + quat_z * quat_z),
            2 * (quat_x * quat_y - quat_w * quat_z),
            2 * (quat_x * quat_z + quat_w * quat_y),
        ],
        [
            2 * (quat_x * quat_y + quat_w * quat_z),
            1 - 2 * (quat_x * quat_x + quat_z * quat_z),
            2 * (quat_y * quat_z - quat_w * quat_x),
        ],
        [
            2 * (quat_x * quat_z - quat_w * quat_y),
            2 * (quat_y * quat_z + quat_w * quat_x),
            1 - 2 * (quat_x * quat_x + quat_y * quat_y),
        ],
    ]
    focal_px = 0.3125 * float(WIN * TSIDE)
    inv_z = 1.0 / mean_z
    scale_z = focal_px * inv_z
    off_u = scale_z * mean_x
    off_v = scale_z * mean_y
    slope_u = off_u * inv_z
    slope_v = off_v * inv_z
    proj_u = [(scale_z * rotation[0][i] - slope_u * rotation[2][i]) * scales[i] for i in range(3)]
    proj_v = [(scale_z * rotation[1][i] - slope_v * rotation[2][i]) * scales[i] for i in range(3)]
    sigma_xx = proj_u[0] * proj_u[0] + proj_u[1] * proj_u[1] + proj_u[2] * proj_u[2] + 0.3
    sigma_xy = proj_u[0] * proj_v[0] + proj_u[1] * proj_v[1] + proj_u[2] * proj_v[2]
    sigma_yy = proj_v[0] * proj_v[0] + proj_v[1] * proj_v[1] + proj_v[2] * proj_v[2] + 0.3
    determinant = sigma_xx * sigma_yy - sigma_xy * sigma_xy
    inv_det = log2_e / determinant
    con_xx = sigma_yy * inv_det
    con_xy = -sigma_xy * inv_det
    con_yy = sigma_xx * inv_det
    lin_x = con_xx * off_u + con_xy * off_v
    lin_y = con_xy * off_u + con_yy * off_v
    logit = rows[10]
    log_opacity = (logit - jnp.log(1.0 + jnp.exp(logit))) * log2_e
    const = log_opacity - 0.5 * (lin_x * off_u + lin_y * off_v)
    coefs = [const, lin_x, lin_y, -0.5 * con_xx, -con_xy, -0.5 * con_yy]
    inv_len = 1.0 / jnp.sqrt(mean_x * mean_x + mean_y * mean_y + mean_z * mean_z)
    dir_x, dir_y, dir_z = mean_x * inv_len, mean_y * inv_len, mean_z * inv_len
    sq_x, sq_y, sq_z = dir_x * dir_x, dir_y * dir_y, dir_z * dir_z
    harmonics = [
        None,
        -harmonic_one * dir_y,
        harmonic_one * dir_z,
        -harmonic_one * dir_x,
        harmonic_two[0] * dir_x * dir_y,
        harmonic_two[1] * dir_y * dir_z,
        harmonic_two[2] * (2 * sq_z - sq_x - sq_y),
        harmonic_two[3] * dir_x * dir_z,
        harmonic_two[4] * (sq_x - sq_y),
        harmonic_three[0] * dir_y * (3 * sq_x - sq_y),
        harmonic_three[1] * dir_x * dir_y * dir_z,
        harmonic_three[2] * dir_y * (4 * sq_z - sq_x - sq_y),
        harmonic_three[3] * dir_z * (2 * sq_z - 3 * sq_x - 3 * sq_y),
        harmonic_three[4] * dir_x * (4 * sq_z - sq_x - sq_y),
        harmonic_three[5] * dir_z * (sq_x - sq_y),
        harmonic_three[6] * dir_x * (sq_x - 3 * sq_y),
    ]
    colours = []
    for colour_no in range(3):
        base = 11 + 16 * colour_no
        total = rows[base] * harmonic_zero
        for k in range(1, 16):
            total = total + rows[base + k] * harmonics[k]
        colours.append(jnp.maximum(total + 0.5, 0.0))
    return coefs, colours


def split3(value):
    high = value.astype(bf16).astype(f32)
    rest = value - high
    middle = rest.astype(bf16).astype(f32)
    return high, middle, rest - middle


def split2(value):
    high = value.astype(bf16)
    return high, (value - high.astype(f32)).astype(bf16)


def pixel_basis(pieces):
    tiles = np.arange(pieces)[:, None]
    pixels = np.arange(PIX)[None, :]
    half = WIN * TSIDE / 2
    pos_x = TSIDE * (tiles % WIN) + pixels % TSIDE + 0.5 - half
    pos_y = TSIDE * (tiles // WIN) + pixels // TSIDE + 0.5 - half
    rows = [np.ones_like(pos_x), pos_x, pos_y]
    for product in (pos_x * pos_x, pos_x * pos_y, pos_y * pos_y):
        high = product.astype(bf16).astype(np.float64)
        rows += [high, product - high]
    table = np.zeros((pieces, BASIS, PIX))
    for row_no, row in enumerate(rows):
        table[:, row_no] = row
    return table.astype(bf16)


def basis_coefs(coefs):
    return [coefs[i] for i in (0, 1, 2, 3, 3, 4, 4, 5, 5)]


def lane_order(shape, inverse):
    lane = lax.broadcasted_iota(jnp.int32, shape, 1)
    if inverse:
        return (lane % ROWS) * SUBL + lane // ROWS
    return (lane % SUBL) * ROWS + lane // SUBL


def prefix_product(total):
    sub = lax.broadcasted_iota(jnp.int32, total.shape, 0)
    run = total
    for step in (1, 2, 4):
        run = jnp.where(sub >= step, run * pltpu.roll(run, step, 0), run)
    before = jnp.where(sub >= 1, pltpu.roll(run, 1, 0), 1.0)
    return before, run[SUBL - 1 :]


def suffix_affine(total, keep, behind):
    sub = lax.broadcasted_iota(jnp.int32, total.shape, 0)
    value, gain = total, keep
    for step in (1, 2, 4):
        inside = sub < SUBL - step
        next_value = jnp.where(inside, pltpu.roll(value, SUBL - step, 0), 0.0)
        next_gain = jnp.where(inside, pltpu.roll(gain, SUBL - step, 0), 1.0)
        value = value + gain * next_value
        gain = gain * next_gain
    whole = value + gain * behind
    after = jnp.where(sub < SUBL - 1, pltpu.roll(whole, SUBL - 1, 0), behind)
    return after, whole[:1]


def slot_blocks(blocks_ref, live_ref, piece, own_blocks):
    found = []
    for slot in range(2):
        block = blocks_ref[piece, slot]
        index = jnp.where(
            block == 0, own_blocks, jnp.where(block > own_blocks, own_blocks + 1, block - 1)
        )
        found.append(jnp.where(slot < live_ref[piece], index, own_blocks + 2))
    return found


def forward_kernel(
    blocks_ref,
    live_ref,
    place_ref,
    params_ref,
    low_ref,
    high_ref,
    target_ref,
    labels_ref,
    basis_ref,
    out_ref,
    tab_e_ref,
    tab_c_ref,
    rows_ref,
    stage_e_ref,
    stage_c_ref,
    stage_t_ref,
    colour_ref,
    result_ref,
):
    doms, pieces = out_ref.shape[0], basis_ref.shape[0]
    own_blocks = params_ref.shape[1] // BLOCK
    region_idx, regions = place_ref[0], place_ref[1]
    for block in range(own_blocks):
        rows_ref[pl.ds(block, PARAMS, stride=SLOTS), :] = params_ref[
            :, block * BLOCK : (block + 1) * BLOCK
        ]
    rows_ref[pl.ds(own_blocks, PARAMS, stride=SLOTS), :] = low_ref[...]
    rows_ref[pl.ds(own_blocks + 1, PARAMS, stride=SLOTS), :] = high_ref[...]
    coefs, colours = splat_rows(
        [rows_ref[i * SLOTS : (i + 1) * SLOTS, :] for i in range(PARAMS)]
    )
    shape = (SLOTS, LANES)
    slot = lax.broadcasted_iota(jnp.int32, shape, 0)
    present = (
        (slot < own_blocks)
        | ((slot == own_blocks) & (region_idx > 0))
        | ((slot == own_blocks + 1) & (region_idx < regions - 1))
    )
    order = lane_order(shape, False)

    def settled(value, absent):
        return jnp.take_along_axis(jnp.where(present, value, absent), order, axis=1)

    coefs = [settled(value, -1e9 if i == 0 else 0.0) for i, value in enumerate(coefs)]
    colours = [settled(value, 0.0) for value in colours]
    stage_e_ref[...] = jnp.zeros_like(stage_e_ref)
    stage_c_ref[...] = jnp.zeros_like(stage_c_ref)
    stage_t_ref[...] = jnp.zeros_like(stage_t_ref)
    parts = basis_coefs([split3(value) for value in coefs])
    for row_no, triple in enumerate(parts):
        for level in range(3):
            stage_e_ref[pl.ds(level * BASIS + row_no, SLOTS, stride=KE), :] = triple[level]
    for colour_no, value in enumerate(colours):
        triple = split3(value)
        for group, level in enumerate((0, 1, 2, 0, 1, 0)):
            stage_c_ref[pl.ds(group * SUBL + colour_no, SLOTS, stride=KC), :] = triple[level]
        for level in range(2):
            stage_t_ref[pl.ds(level * SUBL + colour_no, SLOTS, stride=BASIS), :] = triple[level]
    for block in range(own_blocks + 3):
        span = slice(block * BLOCK, (block + 1) * BLOCK)
        tab_e_ref[span, :] = stage_e_ref[block * KE : (block + 1) * KE, :].T.astype(bf16)
        tab_c_ref[span, :] = stage_c_ref[block * KC : (block + 1) * KC, :].T.astype(bf16)
        colour_ref[block] = stage_t_ref[block * BASIS : (block + 1) * BASIS, :].astype(bf16)

    def render(piece):
        unit = basis_ref[piece]
        rhs = jnp.concatenate([unit, unit, unit], axis=0)
        carry = None
        weights, left = [], []
        for index in slot_blocks(blocks_ref, live_ref, piece, own_blocks):
            start = pl.multiple_of(index * BLOCK, BLOCK)
            alphas = jnp.exp2(
                jnp.dot(tab_e_ref[pl.ds(start, BLOCK), :], rhs, preferred_element_type=f32)
            )
            keep, local = None, []
            for row in range(ROWS):
                alpha = alphas[row * SUBL : (row + 1) * SUBL]
                weight = alpha if keep is None else alpha * keep
                keep = 1.0 - alpha if keep is None else keep - weight
                local.append(weight)
            before, total = prefix_product(keep)
            if carry is not None:
                before, total = before * carry, total * carry
            carry = total
            weights += [weight * before for weight in local]
            left.append(colour_ref[index])
        high, low = split2(jnp.concatenate(weights, axis=0))
        lhs = jnp.concatenate(left, axis=1)
        sums = jnp.dot(lhs, high, preferred_element_type=f32)
        sums = sums + jnp.dot(lhs, low, preferred_element_type=f32)
        sums = sums[:SUBL] + sums[SUBL:]
        row_no = lax.broadcasted_iota(jnp.int32, sums.shape, 0)
        sums = jnp.where(row_no == 3, 1.0 - carry, sums)
        for half in range(PIX // LANES):
            span = pl.ds(half * SUBL * pieces + piece, SUBL, stride=pieces)
            result_ref[span, :] = sums[:, half * LANES : (half + 1) * LANES]

    def step(pair, carry):
        render(2 * pair)
        render(2 * pair + 1)
        return carry

    lax.fori_loop(0, pieces // 2, step, 0)
    width = PIX // doms
    lane = lax.broadcasted_iota(jnp.int32, (pieces, LANES), 1)
    tile_lane = lax.broadcasted_iota(jnp.int32, (SUBL, LANES), 1)
    labels = jnp.broadcast_to(labels_ref[...], (SUBL, LANES))
    tiles = target_ref.shape[0]
    for dom in range(doms):
        half, offset = divmod(dom * width, LANES)
        span = slice(half * LANES, (half + 1) * LANES)
        packed, aimed = None, None
        for channel in range(4):
            shift = (channel * GROUP - offset) % LANES
            first = (half * SUBL + channel) * pieces
            value = result_ref[first : first + pieces, :]
            value = pltpu.roll(value, shift, 1) if shift else value
            packed = value if packed is None else jnp.where(lane >= channel * GROUP, value, packed)
            if channel < 3:
                value = target_ref[:, channel, span]
                value = pltpu.roll(value, shift, 1) if shift else value
            else:
                value = labels
            aimed = value if aimed is None else jnp.where(tile_lane >= channel * GROUP, value, aimed)
        out_ref[dom, :pieces, :] = packed
        out_ref[dom, pieces : pieces + tiles, :] = aimed


def composite_kernel(background_ref, arrived_ref, out_ref):
    doms, pieces = out_ref.shape[0], out_ref.shape[1]
    tiles = arrived_ref.shape[1] - pieces
    all_pieces, all_tiles = doms * pieces, doms * tiles
    per_row = LANES // GROUP
    lane = lax.broadcasted_iota(jnp.int32, (1, LANES), 1)
    label_rows = []
    for dom in range(doms):
        place = dom % per_row
        value = arrived_ref[dom, pieces : pieces + 1, :]
        shift = ((place - 3) * GROUP) % LANES
        value = pltpu.roll(value, shift, 1) if shift else value
        if place == 0:
            label_rows.append(value)
        else:
            label_rows[-1] = jnp.where(lane >= place * GROUP, value, label_rows[-1])
    cell_no = lax.broadcasted_iota(jnp.int32, (MAXD * all_tiles, LANES), 0).astype(f32)
    chosen = jnp.concatenate(
        [jnp.where(cell_no == row, 1.0, 0.0).astype(bf16) for row in label_rows], axis=1
    )

    def moved(matrix, values, dims):
        triple = jnp.concatenate([part.astype(bf16) for part in split3(values)], axis=1)
        wide = lax.dot_general(matrix, triple, (dims, ((), ())), preferred_element_type=f32)
        return wide[:, :LANES] + wide[:, LANES : 2 * LANES] + wide[:, 2 * LANES :]

    data = arrived_ref[:, :pieces, :].reshape(all_pieces, LANES)
    cells = moved(chosen, data, ((1,), (0,)))
    goal = arrived_ref[:, pieces:, :].reshape(all_tiles, LANES)
    lane = lax.broadcasted_iota(jnp.int32, (all_tiles, LANES), 1)
    last = lane >= 3 * GROUP
    backdrop = jnp.where(
        lane < GROUP,
        background_ref[0],
        jnp.where(lane < 2 * GROUP, background_ref[1], background_ref[2]),
    )

    def spread(value):
        return pltpu.roll(value, GROUP, 1) + pltpu.roll(value, 2 * GROUP, 1) + pltpu.roll(
            value, 3 * GROUP, 1
        )

    fronts, through, layers = [], [], []
    front = jnp.ones((all_tiles, LANES), f32)
    composite = jnp.zeros((all_tiles, LANES), f32)
    for depth in range(MAXD):
        layer = cells[depth * all_tiles : (depth + 1) * all_tiles]
        passed = jnp.where(last, 1.0 - layer, 0.0)
        passed = passed + spread(passed)
        fronts.append(front)
        through.append(passed)
        layers.append(layer)
        composite = composite + front * layer
        front = front * passed
    residual = jnp.where(last, 0.0, composite + front * backdrop - goal)
    behind = backdrop
    grads = [None] * MAXD
    for depth in reversed(range(MAXD)):
        grads[depth] = fronts[depth] * jnp.where(last, spread(residual * behind), residual)
        behind = layers[depth] + through[depth] * behind
    back = moved(chosen, jnp.concatenate(grads, axis=0), ((0,), (0,)))
    out_ref[...] = back.reshape(out_ref.shape)


def backward_kernel(
    blocks_ref,
    live_ref,
    place_ref,
    back_ref,
    tab_e_ref,
    tab_c_ref,
    basis_ref,
    own_ref,
    low_ref,
    high_ref,
    grad_ref,
    sums_ref,
):
    doms, pieces = back_ref.shape[0], back_ref.shape[1]
    own_blocks = own_ref.shape[1]
    width = PIX // doms
    lane = lax.broadcasted_iota(jnp.int32, (pieces, LANES), 1)
    for channel in range(4):
        for half in range(PIX // LANES):
            gathered = None
            for dom in range(half * LANES // width, (half + 1) * LANES // width):
                offset = dom * width - half * LANES
                shift = (offset - channel * GROUP) % LANES
                value = back_ref[dom]
                value = pltpu.roll(value, shift, 1) if shift else value
                gathered = value if gathered is None else jnp.where(lane >= offset, value, gathered)
            first = (half * SUBL + channel) * pieces
            grad_ref[first : first + pieces, :] = gathered
            first = (half * SUBL + 4 + channel) * pieces
            grad_ref[first : first + pieces, :] = jnp.zeros_like(gathered)
    sums_ref[...] = jnp.zeros_like(sums_ref)

    def pull(piece):
        unit = basis_ref[piece]
        rhs = jnp.concatenate([unit, unit, unit], axis=0)
        halves = [
            grad_ref[pl.ds(half * SUBL * pieces + piece, SUBL, stride=pieces), :]
            for half in range(PIX // LANES)
        ]
        grads = jnp.concatenate(halves, axis=1)
        g_high, g_mid, g_low = split3(grads)
        g_rhs = jnp.concatenate([g_high, g_high, g_high, g_mid, g_mid, g_low], axis=0).astype(bf16)
        g_lhs = jnp.concatenate([g_high, g_mid], axis=0).astype(bf16)
        indices = slot_blocks(blocks_ref, live_ref, piece, own_blocks)
        carry, slots = None, []
        for index in indices:
            start = pl.multiple_of(index * BLOCK, BLOCK)
            alphas = jnp.exp2(
                jnp.dot(tab_e_ref[pl.ds(start, BLOCK), :], rhs, preferred_element_type=f32)
            )
            shades = jnp.dot(tab_c_ref[pl.ds(start, BLOCK), :], g_rhs, preferred_element_type=f32)
            keep, total, local = None, None, []
            for row in range(ROWS):
                alpha = alphas[row * SUBL : (row + 1) * SUBL]
                weight = alpha if keep is None else alpha * keep
                keep = 1.0 - alpha if keep is None else keep - weight
                value = weight * shades[row * SUBL : (row + 1) * SUBL]
                total = value if total is None else total + value
                local.append(weight)
            before, whole = prefix_product(keep)
            if carry is not None:
                before, whole = before * carry, whole * carry
            carry = whole
            slots.append((alphas, shades, local, before, total, keep))
        behind = grads[3:4]
        for index, (alphas, shades, local, before, total, keep) in zip(
            reversed(indices), reversed(slots)
        ):
            hidden, behind = suffix_affine(total, keep, behind)
            pulls, weights = [None] * ROWS, [None] * ROWS
            for row in reversed(range(ROWS)):
                span = slice(row * SUBL, (row + 1) * SUBL)
                weight = local[row] * before
                gap = shades[span] - hidden
                weights[row] = weight
                pulls[row] = weight * gap
                hidden = hidden + alphas[span] * gap
            along = (((1,), (1,)), ((), ()))
            added = []
            for left, right in ((unit, pulls), (g_lhs, weights)):
                high, low = split2(jnp.concatenate(right, axis=0))
                part = lax.dot_general(left, high, along, preferred_element_type=f32)
                added.append(
                    part + lax.dot_general(left, low, along, preferred_element_type=f32)
                )
            start = pl.multiple_of(index * 2 * BASIS, 2 * BASIS)
            span = pl.ds(start, 2 * BASIS)
            sums_ref[span, :] = sums_ref[span, :] + jnp.concatenate(added, axis=0)

    def step(pair, carry):
        pull(2 * pair)
        pull(2 * pair + 1)
        return carry

    lax.fori_loop(0, pieces // 2, step, 0)

    def rows_of(row):
        return sums_ref[pl.ds(row, SLOTS, stride=2 * BASIS), :]

    moments = [rows_of(0), rows_of(1), rows_of(2)]
    moments += [rows_of(3 + 2 * i) + rows_of(4 + 2 * i) for i in range(3)]
    terms = [value * ln_2 for value in moments]
    terms += [rows_of(BASIS + i) + rows_of(BASIS + SUBL + i) for i in range(3)]
    order = lane_order((SLOTS, LANES), True)
    low_ref[...] = jnp.zeros_like(low_ref)
    high_ref[...] = jnp.zeros_like(high_ref)
    for term_no, value in enumerate(terms):
        value = jnp.take_along_axis(value, order, axis=1)
        own_ref[term_no] = value[:own_blocks]
        low_ref[term_no : term_no + 1, :] = value[own_blocks : own_blocks + 1]
        high_ref[term_no : term_no + 1, :] = value[own_blocks + 1 : own_blocks + 2]


def update_kernel(
    params_ref,
    first_ref,
    second_ref,
    own_ref,
    from_low_ref,
    from_high_ref,
    gradient_ref,
    new_params_ref,
    new_first_ref,
    new_second_ref,
    rows_ref,
    grads_ref,
):
    own_blocks = own_ref.shape[1]
    for block in range(own_blocks):
        rows_ref[pl.ds(block, PARAMS, stride=own_blocks), :] = params_ref[
            :, block * BLOCK : (block + 1) * BLOCK
        ]
    rows = [rows_ref[i * own_blocks : (i + 1) * own_blocks, :] for i in range(PARAMS)]
    slot = lax.broadcasted_iota(jnp.int32, (own_blocks, LANES), 0)
    cots = []
    for term_no in range(9):
        low = jnp.where(slot == 0, from_low_ref[term_no : term_no + 1, :], 0.0)
        high = jnp.where(slot == own_blocks - 1, from_high_ref[term_no : term_no + 1, :], 0.0)
        cots.append(own_ref[term_no] + low + high)
    _, pull_back = jax.vjp(splat_rows, rows)
    pulled = pull_back((cots[:6], cots[6:]))[0]
    for i in range(PARAMS):
        grads_ref[i * own_blocks : (i + 1) * own_blocks, :] = pulled[i]
    for block in range(own_blocks):
        span = slice(block * BLOCK, (block + 1) * BLOCK)
        gradient = grads_ref[pl.ds(block, PARAMS, stride=own_blocks), :]
        new_first = beta_one * first_ref[:, span] + (1 - beta_one) * gradient
        new_second = beta_two * second_ref[:, span] + (1 - beta_two) * gradient * gradient
        update = (
            new_first
            / (1 - beta_one**adam_step)
            / (jnp.sqrt(new_second / (1 - beta_two**adam_step)) + tiny)
        )
        gradient_ref[:, span] = gradient
        new_params_ref[:, span] = params_ref[:, span] - rate * update
        new_first_ref[:, span] = new_first
        new_second_ref[:, span] = new_second


def swap_neighbours(to_lower, to_upper):
    count = lax.axis_size("region")
    even = lax.axis_index("region") % 2 == 0
    inner = [(i, i ^ 1) for i in range(count) if (i ^ 1) < count]
    outer = [(i, i + 1) for i in range(1, count - 1, 2)]
    outer += [(target, source) for source, target in outer]
    first = lax.ppermute(jnp.where(even, to_upper, to_lower), "region", inner)
    second = lax.ppermute(jnp.where(even, to_lower, to_upper), "region", outer)
    return jnp.where(even, second, first), jnp.where(even, first, second)


def on_device(
    params,
    first_moment,
    second_moment,
    piece_blocks,
    piece_live,
    piece_owner,
    piece_cell,
    target,
    background,
):
    own_blocks = params.shape[1] // BLOCK
    doms = lax.axis_size("dom")
    pieces = piece_live.shape[1]
    tiles = target.shape[1]
    low, high = swap_neighbours(params[:, :BLOCK], params[:, -BLOCK:])
    cell = piece_cell[0]
    label = (cell % MAXD) * (doms * tiles) + piece_owner[0] * tiles + cell // MAXD
    labels = jnp.pad(label.astype(f32)[None], ((0, 0), (LANES - GROUP, GROUP - pieces)))
    place = jnp.stack([lax.axis_index("region"), jnp.int32(lax.axis_size("region"))])
    basis = jnp.asarray(pixel_basis(pieces))
    smem = pl.BlockSpec(memory_space=pltpu.SMEM)
    vmem = pl.BlockSpec(memory_space=pltpu.VMEM)
    table_rows = (own_blocks + 3) * BLOCK
    payload, tab_e, tab_c = pl.pallas_call(
        forward_kernel,
        out_shape=(
            jax.ShapeDtypeStruct((doms, pieces + tiles, LANES), f32),
            jax.ShapeDtypeStruct((table_rows, KE), bf16),
            jax.ShapeDtypeStruct((table_rows, KC), bf16),
        ),
        in_specs=[smem] * 3 + [vmem] * 6,
        out_specs=(vmem, vmem, vmem),
        scratch_shapes=[
            pltpu.VMEM((64 * SLOTS, LANES), f32),
            pltpu.VMEM((SLOTS * KE, LANES), f32),
            pltpu.VMEM((SLOTS * KC, LANES), f32),
            pltpu.VMEM((SLOTS * BASIS, LANES), f32),
            pltpu.VMEM((own_blocks + 3, BASIS, LANES), bf16),
            pltpu.VMEM((PIX // LANES * SUBL * pieces, LANES), f32),
        ],
        name="forward",
    )(piece_blocks[0], piece_live[0], place, params, low, high, target[0], labels, basis)
    arrived = lax.all_to_all(payload, "dom", split_axis=0, concat_axis=0, tiled=True)
    back = pl.pallas_call(
        composite_kernel,
        out_shape=jax.ShapeDtypeStruct((doms, pieces, LANES), f32),
        in_specs=[smem, vmem],
        out_specs=vmem,
        name="composite",
    )(background, arrived)
    returned = lax.all_to_all(back, "dom", split_axis=0, concat_axis=0, tiled=True)
    own, to_lower, to_upper = pl.pallas_call(
        backward_kernel,
        out_shape=(
            jax.ShapeDtypeStruct((9, own_blocks, LANES), f32),
            jax.ShapeDtypeStruct((SLOTS, LANES), f32),
            jax.ShapeDtypeStruct((SLOTS, LANES), f32),
        ),
        in_specs=[smem] * 3 + [vmem] * 4,
        out_specs=(vmem, vmem, vmem),
        scratch_shapes=[
            pltpu.VMEM((PIX // LANES * SUBL * pieces, LANES), f32),
            pltpu.VMEM((SLOTS * 2 * BASIS, LANES), f32),
        ],
        name="backward",
    )(piece_blocks[0], piece_live[0], place, returned, tab_e, tab_c, basis)
    from_low, from_high = swap_neighbours(to_lower, to_upper)
    shape = jax.ShapeDtypeStruct(params.shape, f32)
    return pl.pallas_call(
        update_kernel,
        out_shape=(shape, shape, shape, shape),
        in_specs=[vmem] * 6,
        out_specs=(vmem,) * 4,
        scratch_shapes=[
            pltpu.VMEM((64 * own_blocks, LANES), f32),
            pltpu.VMEM((64 * own_blocks, LANES), f32),
        ],
        name="update",
    )(params, first_moment, second_moment, own, from_low, from_high)


def solution(mesh):
    in_specs = (
        P(None, ("region", "dom")),
        P(None, ("region", "dom")),
        P(None, ("region", "dom")),
        P(("region", "dom"), None, None),
        P(("region", "dom"), None),
        P(("region", "dom"), None),
        P(("region", "dom"), None),
        P(("region", "dom"), None, None, None),
        P(),
    )
    out_specs = (P(None, ("region", "dom")),) * 4
    return jax.shard_map(
        on_device, mesh=mesh, in_specs=in_specs, out_specs=out_specs, check_vma=False
    )
```

```python
import math

import numpy as np
import jax
import jax.numpy as jnp
from jax import lax
from jax.experimental import pallas as pl
from jax.experimental.pallas import tpu as pltpu
from jax.sharding import PartitionSpec as P

PARAMS = 59
TSIDE = 16
WIN = 8
BLOCK = 128
MAXD = 8
PIX = 256

harmonic_zero = 0.28209479177387814
harmonic_one = 0.4886025119029199
harmonic_two = (
    1.0925484305920792,
    -1.0925484305920792,
    0.31539156525252005,
    -1.0925484305920792,
    0.5462742152960396,
)
harmonic_three = (
    -0.5900435899266435,
    2.890611442640554,
    -0.4570457994644658,
    0.3731763325901154,
    -0.4570457994644658,
    1.445305721320277,
    -0.5900435899266435,
)
beta_one = 0.9
beta_two = 0.999
rate = 0.001
adam_step = 100
tiny = 1e-08
log2_e = math.log2(math.e)
ln_2 = math.log(2.0)

LANES = 128
SUBL = 8
ROWS = BLOCK // SUBL
GROUP = LANES // 4
BASIS = 9
KE = 32
KC = 2 * SUBL
KT = KE + KC
TOP = 16
SLOTS = 16
f32 = jnp.float32
bf16 = jnp.bfloat16


def splat_rows(rows):
    mean_x, mean_y, mean_z = rows[0], rows[1], rows[2]
    scales = [jnp.exp(rows[3]), jnp.exp(rows[4]), jnp.exp(rows[5])]
    norm_sq = rows[6] * rows[6] + rows[7] * rows[7] + rows[8] * rows[8] + rows[9] * rows[9]
    inv_norm = 1.0 / jnp.sqrt(norm_sq)
    quat_w, quat_x, quat_y, quat_z = [rows[6 + i] * inv_norm for i in range(4)]
    rotation = [
        [
            1 - 2 * (quat_y * quat_y + quat_z * quat_z),
            2 * (quat_x * quat_y - quat_w * quat_z),
            2 * (quat_x * quat_z + quat_w * quat_y),
        ],
        [
            2 * (quat_x * quat_y + quat_w * quat_z),
            1 - 2 * (quat_x * quat_x + quat_z * quat_z),
            2 * (quat_y * quat_z - quat_w * quat_x),
        ],
        [
            2 * (quat_x * quat_z - quat_w * quat_y),
            2 * (quat_y * quat_z + quat_w * quat_x),
            1 - 2 * (quat_x * quat_x + quat_y * quat_y),
        ],
    ]
    focal_px = 0.3125 * float(WIN * TSIDE)
    inv_z = 1.0 / mean_z
    scale_z = focal_px * inv_z
    off_u = scale_z * mean_x
    off_v = scale_z * mean_y
    slope_u = off_u * inv_z
    slope_v = off_v * inv_z
    proj_u = [(scale_z * rotation[0][i] - slope_u * rotation[2][i]) * scales[i] for i in range(3)]
    proj_v = [(scale_z * rotation[1][i] - slope_v * rotation[2][i]) * scales[i] for i in range(3)]
    sigma_xx = proj_u[0] * proj_u[0] + proj_u[1] * proj_u[1] + proj_u[2] * proj_u[2] + 0.3
    sigma_xy = proj_u[0] * proj_v[0] + proj_u[1] * proj_v[1] + proj_u[2] * proj_v[2]
    sigma_yy = proj_v[0] * proj_v[0] + proj_v[1] * proj_v[1] + proj_v[2] * proj_v[2] + 0.3
    determinant = sigma_xx * sigma_yy - sigma_xy * sigma_xy
    inv_det = log2_e / determinant
    con_xx = sigma_yy * inv_det
    con_xy = -sigma_xy * inv_det
    con_yy = sigma_xx * inv_det
    lin_x = con_xx * off_u + con_xy * off_v
    lin_y = con_xy * off_u + con_yy * off_v
    logit = rows[10]
    log_opacity = (logit - jnp.log(1.0 + jnp.exp(logit))) * log2_e
    const = log_opacity - 0.5 * (lin_x * off_u + lin_y * off_v)
    coefs = [const, lin_x, lin_y, -0.5 * con_xx, -con_xy, -0.5 * con_yy]
    inv_len = 1.0 / jnp.sqrt(mean_x * mean_x + mean_y * mean_y + mean_z * mean_z)
    dir_x, dir_y, dir_z = mean_x * inv_len, mean_y * inv_len, mean_z * inv_len
    sq_x, sq_y, sq_z = dir_x * dir_x, dir_y * dir_y, dir_z * dir_z
    harmonics = [
        None,
        -harmonic_one * dir_y,
        harmonic_one * dir_z,
        -harmonic_one * dir_x,
        harmonic_two[0] * dir_x * dir_y,
        harmonic_two[1] * dir_y * dir_z,
        harmonic_two[2] * (2 * sq_z - sq_x - sq_y),
        harmonic_two[3] * dir_x * dir_z,
        harmonic_two[4] * (sq_x - sq_y),
        harmonic_three[0] * dir_y * (3 * sq_x - sq_y),
        harmonic_three[1] * dir_x * dir_y * dir_z,
        harmonic_three[2] * dir_y * (4 * sq_z - sq_x - sq_y),
        harmonic_three[3] * dir_z * (2 * sq_z - 3 * sq_x - 3 * sq_y),
        harmonic_three[4] * dir_x * (4 * sq_z - sq_x - sq_y),
        harmonic_three[5] * dir_z * (sq_x - sq_y),
        harmonic_three[6] * dir_x * (sq_x - 3 * sq_y),
    ]
    colours = []
    for colour_no in range(3):
        base = 11 + 16 * colour_no
        total = rows[base] * harmonic_zero
        for k in range(1, 16):
            total = total + rows[base + k] * harmonics[k]
        colours.append(jnp.maximum(total + 0.5, 0.0))
    return coefs, colours


def split3(value):
    high = value.astype(bf16).astype(f32)
    rest = value - high
    middle = rest.astype(bf16).astype(f32)
    return high, middle, rest - middle


def split2(value):
    high = value.astype(bf16)
    return high, (value - high.astype(f32)).astype(bf16)


def pixel_basis(pieces):
    tiles = np.arange(pieces)[:, None]
    pixels = np.arange(PIX)[None, :]
    half = WIN * TSIDE / 2
    pos_x = TSIDE * (tiles % WIN) + pixels % TSIDE + 0.5 - half
    pos_y = TSIDE * (tiles // WIN) + pixels // TSIDE + 0.5 - half
    rows = [np.ones_like(pos_x), pos_x, pos_y]
    for product in (pos_x * pos_x, pos_x * pos_y, pos_y * pos_y):
        high = product.astype(bf16).astype(np.float64)
        rows += [high, product - high]
    table = np.zeros((pieces, KE, PIX))
    for row_no, row in enumerate(rows * 3):
        table[:, row_no] = row
    return table.astype(bf16)


def basis_coefs(coefs):
    return [coefs[i] for i in (0, 1, 2, 3, 3, 4, 4, 5, 5)]


def lane_order(shape, inverse):
    lane = lax.broadcasted_iota(jnp.int32, shape, 1)
    if inverse:
        return (lane % ROWS) * SUBL + lane // ROWS
    return (lane % SUBL) * ROWS + lane // SUBL


def prefix_product(total):
    sub = lax.broadcasted_iota(jnp.int32, total.shape, 0)
    run = total
    for step in (1, 2, 4):
        run = jnp.where(sub >= step, run * pltpu.roll(run, step, 0), run)
    before = jnp.where(sub >= 1, pltpu.roll(run, 1, 0), 1.0)
    return before, run[SUBL - 1 :]


def suffix_affine(total, keep, behind):
    sub = lax.broadcasted_iota(jnp.int32, total.shape, 0)
    value, gain = total, keep
    for step in (1, 2, 4):
        inside = sub < SUBL - step
        next_value = jnp.where(inside, pltpu.roll(value, SUBL - step, 0), 0.0)
        next_gain = jnp.where(inside, pltpu.roll(gain, SUBL - step, 0), 1.0)
        value = value + gain * next_value
        gain = gain * next_gain
    whole = value + gain * behind
    after = jnp.where(sub < SUBL - 1, pltpu.roll(whole, SUBL - 1, 0), behind)
    return after, whole[:1]


def list_items(blocks_ref, live_ref, items_ref, pieces, own_blocks):
    room = pieces + SUBL
    doubles, singles = jnp.int32(0), jnp.int32(0)
    for piece in range(pieces):
        entries = []
        for slot in range(2):
            block = blocks_ref[slot, piece]
            place = jnp.where(block == 0, own_blocks + 1, block - 1)
            entries.append(place * 64 + piece)
        items_ref[doubles] = entries[0]
        items_ref[room + doubles] = entries[1]
        items_ref[2 * room + singles] = entries[0]
        second = live_ref[0, piece] - 1
        doubles = doubles + second
        singles = singles + 1 - second
    for spare in range(6):
        items_ref[2 * room + singles + spare] = (own_blocks + 2) * 64 + pieces
    items_ref[3 * room] = doubles
    items_ref[3 * room + 1] = (doubles + (singles + 1) // 2 + 1) // 2


def item_slots(items_ref, item, pieces):
    room = pieces + SUBL
    doubles = items_ref[3 * room]
    chained = item < doubles
    single = 2 * (room + item - doubles)
    first = items_ref[jnp.where(chained, item, single)]
    second = items_ref[jnp.where(chained, room + item, single + 1)]
    slots = []
    for entry in (first, second):
        slots.append((entry % 64, pl.multiple_of(entry // 64 * BLOCK, BLOCK)))
    return chained, slots


def pipelined(pairs, front, back):
    front(0, 0)

    def step(pair, carry):
        for side in range(2):
            front(2 * pair + side + 1, 1 - side)
            back(2 * pair + side, side)
        return carry

    lax.fori_loop(0, pairs, step, 0)


def exponents(table_ref, basis_ref, piece, start, pieces):
    unit = basis_ref[jnp.minimum(piece, pieces - 1)]
    rhs = jnp.concatenate([unit, jnp.zeros((KC, PIX), bf16)], axis=0)
    return jnp.dot(table_ref[pl.ds(start, BLOCK), :], rhs, preferred_element_type=f32)


def forward_kernel(
    blocks_ref,
    live_ref,
    owner_ref,
    cell_ref,
    params_ref,
    inner_ref,
    outer_ref,
    target_ref,
    basis_ref,
    out_ref,
    table_ref,
    items_ref,
    own_rows_ref,
    copy_rows_ref,
    stage_ref,
    colour_ref,
    result_ref,
    local_refs,
    before_refs,
    left_refs,
):
    doms, pieces = out_ref.shape[0], basis_ref.shape[0]
    own_blocks = params_ref.shape[1] // BLOCK
    region_idx, regions = lax.axis_index("region"), lax.axis_size("region")
    even = region_idx % 2 == 0
    list_items(blocks_ref, live_ref, items_ref, pieces, own_blocks)
    for block in range(own_blocks):
        own_rows_ref[pl.ds(block, PARAMS, stride=SUBL), :] = params_ref[
            :, block * BLOCK : (block + 1) * BLOCK
        ]
    inner, outer = inner_ref[...], outer_ref[...]
    copy_rows_ref[pl.ds(0, PARAMS, stride=SUBL), :] = jnp.where(even, inner, outer)
    copy_rows_ref[pl.ds(1, PARAMS, stride=SUBL), :] = jnp.where(even, outer, inner)
    rows = []
    for i in range(PARAMS):
        span = slice(i * SUBL, (i + 1) * SUBL)
        rows.append(jnp.concatenate([own_rows_ref[span, :], copy_rows_ref[span, :]], axis=0))
    coefs, colours = splat_rows(rows)
    shape = (SLOTS, LANES)
    slot_no = lax.broadcasted_iota(jnp.int32, shape, 0)
    present = (
        (slot_no < own_blocks)
        | ((slot_no == own_blocks) & (region_idx < regions - 1))
        | ((slot_no == own_blocks + 1) & (region_idx > 0))
    )
    order = lane_order(shape, False)

    def settled(value, absent):
        return jnp.take_along_axis(jnp.where(present, value, absent), order, axis=1)

    coefs = [settled(value, -1e9 if i == 0 else 0.0) for i, value in enumerate(coefs)]
    colours = [settled(value, 0.0) for value in colours]
    nothing = jnp.zeros(shape, f32)
    parts = basis_coefs([split3(value) for value in coefs])
    lines = [parts[row % BASIS][row // BASIS] for row in range(3 * BASIS)]
    lines += [nothing] * (KE - 3 * BASIS)
    triples = [split3(value) for value in colours]
    for level in (0, 0, 1, 0, 0, 1):
        lines += [triple[level] for triple in triples] + [nothing]
    for row, value in enumerate(lines):
        group, place = divmod(row, SUBL)
        base = group * SLOTS * SUBL + place
        stage_ref[pl.ds(base, SUBL, stride=SUBL), :] = value[:SUBL]
        stage_ref[pl.ds(base + SUBL * SUBL, 4, stride=SUBL), :] = value[SUBL : SUBL + 4]
    for block in range(own_blocks + 3):
        tiles = [
            stage_ref[(group * SLOTS + block) * SUBL : (group * SLOTS + block + 1) * SUBL, :]
            for group in range(len(lines) // SUBL)
        ]
        span = slice(block * BLOCK, (block + 1) * BLOCK)
        table_ref[span, :] = jnp.concatenate(tiles[: KT // SUBL], axis=0).T.astype(bf16)
        colour_ref[block] = jnp.concatenate(tiles[KT // SUBL :] * 2, axis=0).astype(bf16)

    def front(item, side):
        chained, slots = item_slots(items_ref, item, pieces)
        carry = None
        for slot, (piece, start) in enumerate(slots):
            alphas = jnp.exp2(exponents(table_ref, basis_ref, piece, start, pieces))
            keep = None
            for row in range(ROWS):
                alpha = alphas[row * SUBL : (row + 1) * SUBL]
                weight = alpha if keep is None else alpha * keep
                keep = 1.0 - alpha if keep is None else keep - weight
                first = slot * BLOCK + row * SUBL
                local_refs[side][first : first + SUBL, :] = weight
            before, total = prefix_product(keep)
            if slot == 1:
                carry = jnp.where(chained, carry, 1.0)
                before, total = before * carry, total * carry
            carry = total
            before_refs[side][slot * SUBL : (slot + 1) * SUBL, :] = before
            left_refs[side][slot : slot + 1, :] = total

    def back(item, side):
        chained, slots = item_slots(items_ref, item, pieces)
        sums = None
        for slot, (piece, start) in enumerate(slots):
            before = before_refs[side][slot * SUBL : (slot + 1) * SUBL, :]
            weights = []
            for row in range(ROWS):
                first = slot * BLOCK + row * SUBL
                weights.append(local_refs[side][first : first + SUBL, :] * before)
            high, low = split2(jnp.concatenate(weights, axis=0))
            left = colour_ref[start // BLOCK]
            wide = jnp.dot(left, high, preferred_element_type=f32)
            wide = (wide + jnp.dot(left, low, preferred_element_type=f32))[:SUBL]
            wide = wide + pltpu.roll(wide, 4, 0)
            sums = wide + jnp.where(chained, sums, 0.0) if slot else wide
            row_no = lax.broadcasted_iota(jnp.int32, sums.shape, 0)
            value = jnp.where(row_no == 3, 1.0 - left_refs[side][slot : slot + 1, :], sums)
            for half in range(PIX // LANES):
                first = pl.multiple_of((half * (pieces + 1) + piece) * SUBL, SUBL)
                result_ref[pl.ds(first, SUBL), :] = value[:, half * LANES : (half + 1) * LANES]

    pipelined(items_ref[3 * (pieces + SUBL) + 1], front, back)
    width = PIX // doms
    lane = lax.broadcasted_iota(jnp.int32, (pieces, LANES), 1)
    tile_lane = lax.broadcasted_iota(jnp.int32, (SUBL, LANES), 1)
    tiles = target_ref.shape[1]
    cell = cell_ref[...]
    labels = (cell % MAXD) * (doms * tiles) + owner_ref[...] * tiles + cell // MAXD
    labels = jnp.concatenate(
        [jnp.zeros((1, LANES - pieces), f32), labels.astype(f32)], axis=1
    )
    labels = jnp.broadcast_to(labels, (SUBL, LANES))
    for dom in range(doms):
        half, offset = divmod(dom * width, LANES)
        span = slice(half * LANES, (half + 1) * LANES)
        packed, aimed = None, None
        for channel in range(4):
            shift = (channel * GROUP - offset) % LANES
            first = half * (pieces + 1) * SUBL + channel
            value = result_ref[pl.ds(first, pieces, stride=SUBL), :]
            value = pltpu.roll(value, shift, 1) if shift else value
            packed = value if packed is None else jnp.where(lane >= channel * GROUP, value, packed)
            if channel < 3:
                value = target_ref[channel, :, span]
                value = pltpu.roll(value, shift, 1) if shift else value
            else:
                value = labels
            aimed = value if aimed is None else jnp.where(tile_lane >= channel * GROUP, value, aimed)
        out_ref[dom, :pieces, :] = packed
        out_ref[dom, pieces : pieces + tiles, :] = aimed


def composite_kernel(background_ref, arrived_ref, out_ref):
    doms, pieces = out_ref.shape[0], out_ref.shape[1]
    tiles = arrived_ref.shape[1] - pieces
    all_pieces, all_tiles = doms * pieces, doms * tiles
    per_row = LANES // GROUP
    lane = lax.broadcasted_iota(jnp.int32, (1, LANES), 1)
    label_rows = []
    for dom in range(doms):
        place = dom % per_row
        value = arrived_ref[dom, pieces : pieces + 1, :]
        shift = ((place - 3) * GROUP) % LANES
        value = pltpu.roll(value, shift, 1) if shift else value
        if place == 0:
            label_rows.append(value)
        else:
            label_rows[-1] = jnp.where(lane >= place * GROUP, value, label_rows[-1])
    cells_all = MAXD * all_tiles
    cell_no = lax.broadcasted_iota(jnp.int32, (cells_all, LANES), 0).astype(f32)
    to_cells = jnp.concatenate(
        [jnp.where(cell_no == row, 1.0, 0.0).astype(bf16) for row in label_rows], axis=1
    )
    upright = jnp.concatenate([jnp.broadcast_to(row, (SUBL, LANES)).T for row in label_rows], axis=0)
    cell_no = lax.broadcasted_iota(jnp.int32, (all_pieces, cells_all), 1).astype(f32)
    to_pieces = jnp.where(cell_no == upright[:, :1], 1.0, 0.0).astype(bf16)

    def moved(matrix, values):
        triple = jnp.concatenate([part.astype(bf16) for part in split3(values)], axis=1)
        wide = jnp.dot(matrix, triple, preferred_element_type=f32)
        return wide[:, :LANES] + wide[:, LANES : 2 * LANES] + wide[:, 2 * LANES :]

    data = arrived_ref[:, :pieces, :].reshape(all_pieces, LANES)
    cells = moved(to_cells, data)
    goal = arrived_ref[:, pieces:, :].reshape(all_tiles, LANES)
    lane = lax.broadcasted_iota(jnp.int32, (all_tiles, LANES), 1)
    last = lane >= 3 * GROUP
    backdrop = jnp.where(
        lane < GROUP,
        background_ref[0],
        jnp.where(lane < 2 * GROUP, background_ref[1], background_ref[2]),
    )

    def spread(value):
        return pltpu.roll(value, GROUP, 1) + pltpu.roll(value, 2 * GROUP, 1) + pltpu.roll(
            value, 3 * GROUP, 1
        )

    fronts, through, layers = [], [], []
    front = jnp.ones((all_tiles, LANES), f32)
    composite = jnp.zeros((all_tiles, LANES), f32)
    for depth in range(MAXD):
        layer = cells[depth * all_tiles : (depth + 1) * all_tiles]
        passed = jnp.where(last, 1.0 - layer, 0.0)
        passed = passed + spread(passed)
        fronts.append(front)
        through.append(passed)
        layers.append(layer)
        composite = composite + front * layer
        front = front * passed
    residual = jnp.where(last, 0.0, composite + front * backdrop - goal)
    behind = backdrop
    grads = [None] * MAXD
    for depth in reversed(range(MAXD)):
        grads[depth] = fronts[depth] * jnp.where(last, spread(residual * behind), residual)
        behind = layers[depth] + through[depth] * behind
    back = moved(to_pieces, jnp.concatenate(grads, axis=0))
    out_ref[...] = back.reshape(out_ref.shape)


def backward_kernel(
    items_ref,
    back_ref,
    table_ref,
    basis_ref,
    own_ref,
    inner_ref,
    outer_ref,
    grad_ref,
    sums_ref,
    alpha_refs,
    shade_refs,
    local_refs,
    before_refs,
    hidden_refs,
):
    doms, pieces = back_ref.shape[0], back_ref.shape[1]
    own_blocks = own_ref.shape[1]
    width = PIX // doms
    lane = lax.broadcasted_iota(jnp.int32, (pieces, LANES), 1)
    grad_ref[...] = jnp.zeros_like(grad_ref)
    sums_ref[...] = jnp.zeros_like(sums_ref)
    for half in range(PIX // LANES):
        for channel in range(4):
            gathered = None
            for dom in range(half * LANES // width, (half + 1) * LANES // width):
                offset = dom * width - half * LANES
                shift = (offset - channel * GROUP) % LANES
                value = back_ref[dom]
                value = pltpu.roll(value, shift, 1) if shift else value
                gathered = value if gathered is None else jnp.where(lane >= offset, value, gathered)
            first = half * (pieces + 1) * SUBL + channel
            grad_ref[pl.ds(first, pieces, stride=SUBL), :] = gathered

    def grads_of(piece):
        halves = []
        for half in range(PIX // LANES):
            first = pl.multiple_of((half * (pieces + 1) + piece) * SUBL, SUBL)
            halves.append(grad_ref[pl.ds(first, SUBL), :])
        grads = jnp.concatenate(halves, axis=1)
        upper = lax.broadcasted_iota(jnp.int32, grads.shape, 0) < 4
        high, middle, low = split3(grads)
        first = jnp.where(upper, high, pltpu.roll(middle, 4, 0))
        return grads, first, jnp.where(upper, high, pltpu.roll(low, 4, 0))

    def front(item, side):
        chained, slots = item_slots(items_ref, item, pieces)
        carry, ends = None, []
        for slot, (piece, start) in enumerate(slots):
            alphas = jnp.exp2(exponents(table_ref, basis_ref, piece, start, pieces))
            grads, first, second = grads_of(piece)
            rhs = jnp.concatenate([first, second], axis=0).astype(bf16)
            rhs = jnp.concatenate([jnp.zeros((KE, PIX), bf16), rhs], axis=0)
            shades = jnp.dot(table_ref[pl.ds(start, BLOCK), :], rhs, preferred_element_type=f32)
            span = slice(slot * BLOCK, (slot + 1) * BLOCK)
            alpha_refs[side][span, :] = alphas
            shade_refs[side][span, :] = shades
            keep, total = None, None
            for row in range(ROWS):
                alpha = alphas[row * SUBL : (row + 1) * SUBL]
                weight = alpha if keep is None else alpha * keep
                keep = 1.0 - alpha if keep is None else keep - weight
                value = weight * shades[row * SUBL : (row + 1) * SUBL]
                total = value if total is None else total + value
                first = slot * BLOCK + row * SUBL
                local_refs[side][first : first + SUBL, :] = weight
            before, whole = prefix_product(keep)
            if slot == 1:
                before = before * jnp.where(chained, carry, 1.0)
            carry = whole
            before_refs[side][slot * SUBL : (slot + 1) * SUBL, :] = before
            ends.append((total, keep, grads[3:4]))
        behind = None
        for slot in (1, 0):
            total, keep, final = ends[slot]
            behind = jnp.where(chained, behind, final) if slot == 0 else final
            hidden, behind = suffix_affine(total, keep, behind)
            hidden_refs[side][slot * SUBL : (slot + 1) * SUBL, :] = hidden

    def back(item, side):
        along = (((1,), (1,)), ((), ()))
        _, slots = item_slots(items_ref, item, pieces)
        for slot, (piece, start) in enumerate(slots):
            before = before_refs[side][slot * SUBL : (slot + 1) * SUBL, :]
            hidden = hidden_refs[side][slot * SUBL : (slot + 1) * SUBL, :]
            pulls, weights = [None] * ROWS, [None] * ROWS
            for row in reversed(range(ROWS)):
                first = slot * BLOCK + row * SUBL
                span = slice(first, first + SUBL)
                weight = local_refs[side][span, :] * before
                gap = shade_refs[side][span, :] - hidden
                weights[row] = weight
                pulls[row] = weight * gap
                hidden = hidden + alpha_refs[side][span, :] * gap
            unit = basis_ref[jnp.minimum(piece, pieces - 1)][:TOP]
            _, first, second = grads_of(piece)
            g_lhs = jnp.concatenate([first, second], axis=0).astype(bf16)
            for base, left, values in ((0, unit, pulls), (2, g_lhs, weights)):
                part = None
                for value in split2(jnp.concatenate(values, axis=0)):
                    product = lax.dot_general(left, value, along, preferred_element_type=f32)
                    part = product if part is None else part + product
                for group in range(2 if base == 0 else 1):
                    row = (base + group) * SLOTS * SUBL + start // BLOCK * SUBL
                    rows = pl.ds(pl.multiple_of(row, SUBL), SUBL)
                    sums_ref[rows, :] = (
                        sums_ref[rows, :] + part[group * SUBL : (group + 1) * SUBL]
                    )

    pipelined(items_ref[3 * (pieces + SUBL) + 1], front, back)

    def rows_of(row):
        group, place = divmod(row, SUBL)
        return sums_ref[pl.ds(group * SLOTS * SUBL + place, SLOTS, stride=SUBL), :]

    moments = [rows_of(0), rows_of(1), rows_of(2)]
    moments += [rows_of(3 + 2 * i) + rows_of(4 + 2 * i) for i in range(3)]
    terms = [value * ln_2 for value in moments]
    terms += [rows_of(TOP + i) + rows_of(TOP + 4 + i) for i in range(3)]
    order = lane_order((SLOTS, LANES), True)
    even = lax.axis_index("region") % 2 == 0
    inner_ref[...] = jnp.zeros_like(inner_ref)
    outer_ref[...] = jnp.zeros_like(outer_ref)
    for term_no, value in enumerate(terms):
        value = jnp.take_along_axis(value, order, axis=1)
        own_ref[term_no] = value[:own_blocks]
        high = value[own_blocks : own_blocks + 1]
        low = value[own_blocks + 1 : own_blocks + 2]
        inner_ref[term_no : term_no + 1, :] = jnp.where(even, high, low)
        outer_ref[term_no : term_no + 1, :] = jnp.where(even, low, high)


def update_kernel(
    params_ref,
    first_ref,
    second_ref,
    own_ref,
    inner_ref,
    outer_ref,
    gradient_ref,
    new_params_ref,
    new_first_ref,
    new_second_ref,
    rows_ref,
    grads_ref,
):
    own_blocks = own_ref.shape[1]
    for block in range(own_blocks):
        rows_ref[pl.ds(block, PARAMS, stride=own_blocks), :] = params_ref[
            :, block * BLOCK : (block + 1) * BLOCK
        ]
    rows = [rows_ref[i * own_blocks : (i + 1) * own_blocks, :] for i in range(PARAMS)]
    slot = lax.broadcasted_iota(jnp.int32, (own_blocks, LANES), 0)
    even = lax.axis_index("region") % 2 == 0
    from_low = jnp.where(even, outer_ref[...], inner_ref[...])
    from_high = jnp.where(even, inner_ref[...], outer_ref[...])
    cots = []
    for term_no in range(9):
        low = jnp.where(slot == 0, from_low[term_no : term_no + 1, :], 0.0)
        high = jnp.where(slot == own_blocks - 1, from_high[term_no : term_no + 1, :], 0.0)
        cots.append(own_ref[term_no] + low + high)
    _, pull_back = jax.vjp(splat_rows, rows)
    pulled = pull_back((cots[:6], cots[6:]))[0]
    for i in range(PARAMS):
        grads_ref[i * own_blocks : (i + 1) * own_blocks, :] = pulled[i]
    for block in range(own_blocks):
        span = slice(block * BLOCK, (block + 1) * BLOCK)
        gradient = grads_ref[pl.ds(block, PARAMS, stride=own_blocks), :]
        new_first = beta_one * first_ref[:, span] + (1 - beta_one) * gradient
        new_second = beta_two * second_ref[:, span] + (1 - beta_two) * gradient * gradient
        update = (
            new_first
            / (1 - beta_one**adam_step)
            / (jnp.sqrt(new_second / (1 - beta_two**adam_step)) + tiny)
        )
        gradient_ref[:, span] = gradient
        new_params_ref[:, span] = params_ref[:, span] - rate * update
        new_first_ref[:, span] = new_first
        new_second_ref[:, span] = new_second


def exchange(to_inner, to_outer):
    count = lax.axis_size("region")
    inner = [(i, i ^ 1) for i in range(count) if (i ^ 1) < count]
    outer = [(i, i + 1) for i in range(1, count - 1, 2)]
    outer += [(target, source) for source, target in outer]
    return lax.ppermute(to_inner, "region", inner), lax.ppermute(to_outer, "region", outer)


def on_device(
    params,
    first_moment,
    second_moment,
    piece_blocks,
    piece_live,
    piece_owner,
    piece_cell,
    target,
    background,
):
    own_blocks = params.shape[1] // BLOCK
    doms = lax.axis_size("dom")
    pieces = piece_live.shape[1]
    tiles = target.shape[1]
    even = lax.axis_index("region") % 2 == 0
    low, high = params[:, :BLOCK], params[:, -BLOCK:]
    inner, outer = exchange(jnp.where(even, high, low), jnp.where(even, low, high))
    basis = jnp.asarray(pixel_basis(pieces))
    smem = pl.BlockSpec(memory_space=pltpu.SMEM)
    vmem = pl.BlockSpec(memory_space=pltpu.VMEM)
    plane = pltpu.VMEM((2 * BLOCK, PIX), f32)
    strip = pltpu.VMEM((2 * SUBL, PIX), f32)
    piece_rows = pltpu.VMEM((PIX // LANES * (pieces + 1) * SUBL, LANES), f32)
    payload, table, items = pl.pallas_call(
        forward_kernel,
        out_shape=(
            jax.ShapeDtypeStruct((doms, pieces + tiles, LANES), f32),
            jax.ShapeDtypeStruct(((own_blocks + 3) * BLOCK, KT), bf16),
            jax.ShapeDtypeStruct((3 * (pieces + SUBL) + 2,), jnp.int32),
        ),
        in_specs=[smem] * 2 + [vmem] * 7,
        out_specs=(vmem, vmem, smem),
        scratch_shapes=[
            pltpu.VMEM((64 * SUBL, LANES), f32),
            pltpu.VMEM((64 * SUBL, LANES), f32),
            pltpu.VMEM(((KT // SUBL + 1) * SLOTS * SUBL, LANES), f32),
            pltpu.VMEM((own_blocks + 3, TOP, LANES), bf16),
            piece_rows,
            [plane] * 2,
            [strip] * 2,
            [strip] * 2,
        ],
        name="forward",
    )(
        piece_blocks[0].T,
        piece_live,
        piece_owner,
        piece_cell,
        params,
        inner,
        outer,
        jnp.transpose(target[0], (1, 0, 2)),
        basis,
    )
    arrived = lax.all_to_all(payload, "dom", split_axis=0, concat_axis=0, tiled=True)
    back = pl.pallas_call(
        composite_kernel,
        out_shape=jax.ShapeDtypeStruct((doms, pieces, LANES), f32),
        in_specs=[smem, vmem],
        out_specs=vmem,
        name="composite",
    )(background, arrived)
    returned = lax.all_to_all(back, "dom", split_axis=0, concat_axis=0, tiled=True)
    own, to_inner, to_outer = pl.pallas_call(
        backward_kernel,
        out_shape=(
            jax.ShapeDtypeStruct((9, own_blocks, LANES), f32),
            jax.ShapeDtypeStruct((SLOTS, LANES), f32),
            jax.ShapeDtypeStruct((SLOTS, LANES), f32),
        ),
        in_specs=[smem] + [vmem] * 3,
        out_specs=(vmem, vmem, vmem),
        scratch_shapes=[
            piece_rows,
            pltpu.VMEM((3 * SLOTS * SUBL, LANES), f32),
            [plane] * 2,
            [plane] * 2,
            [plane] * 2,
            [strip] * 2,
            [strip] * 2,
        ],
        name="backward",
    )(items, returned, table, basis)
    inner, outer = exchange(to_inner, to_outer)
    shape = jax.ShapeDtypeStruct(params.shape, f32)
    return pl.pallas_call(
        update_kernel,
        out_shape=(shape, shape, shape, shape),
        in_specs=[vmem] * 6,
        out_specs=(vmem,) * 4,
        scratch_shapes=[
            pltpu.VMEM((64 * own_blocks, LANES), f32),
            pltpu.VMEM((64 * own_blocks, LANES), f32),
        ],
        name="update",
    )(params, first_moment, second_moment, own, inner, outer)


def solution(mesh):
    in_specs = (
        P(None, ("region", "dom")),
        P(None, ("region", "dom")),
        P(None, ("region", "dom")),
        P(("region", "dom"), None, None),
        P(("region", "dom"), None),
        P(("region", "dom"), None),
        P(("region", "dom"), None),
        P(("region", "dom"), None, None, None),
        P(),
    )
    out_specs = (P(None, ("region", "dom")),) * 4
    return jax.shard_map(
        on_device, mesh=mesh, in_specs=in_specs, out_specs=out_specs, check_vma=False
    )
```

```python
import math

import numpy as np
import jax
import jax.numpy as jnp
from jax import lax
from jax.experimental import pallas as pl
from jax.experimental.pallas import tpu as pltpu
from jax.sharding import PartitionSpec as P

PARAMS = 59
TSIDE = 16
WIN = 8
BLOCK = 128
MAXD = 8
PIX = 256

harmonic_zero = 0.28209479177387814
harmonic_one = 0.4886025119029199
harmonic_two = (
    1.0925484305920792,
    -1.0925484305920792,
    0.31539156525252005,
    -1.0925484305920792,
    0.5462742152960396,
)
harmonic_three = (
    -0.5900435899266435,
    2.890611442640554,
    -0.4570457994644658,
    0.3731763325901154,
    -0.4570457994644658,
    1.445305721320277,
    -0.5900435899266435,
)
beta_one = 0.9
beta_two = 0.999
rate = 0.001
adam_step = 100
tiny = 1e-08
log2_e = math.log2(math.e)
ln_2 = math.log(2.0)

LANES = 128
SUBL = 8
ROWS = BLOCK // SUBL
GROUP = LANES // 4
BASIS = 9
KE = 32
KC = 2 * SUBL
KT = KE + KC
TOP = 16
SLOTS = 16
vmem_limit = 12 * 2**20
f32 = jnp.float32
bf16 = jnp.bfloat16


def splat_rows(rows):
    mean_x, mean_y, mean_z = rows[0], rows[1], rows[2]
    scales = [jnp.exp(rows[3]), jnp.exp(rows[4]), jnp.exp(rows[5])]
    norm_sq = rows[6] * rows[6] + rows[7] * rows[7] + rows[8] * rows[8] + rows[9] * rows[9]
    inv_norm = 1.0 / jnp.sqrt(norm_sq)
    quat_w, quat_x, quat_y, quat_z = [rows[6 + i] * inv_norm for i in range(4)]
    rotation = [
        [
            1 - 2 * (quat_y * quat_y + quat_z * quat_z),
            2 * (quat_x * quat_y - quat_w * quat_z),
            2 * (quat_x * quat_z + quat_w * quat_y),
        ],
        [
            2 * (quat_x * quat_y + quat_w * quat_z),
            1 - 2 * (quat_x * quat_x + quat_z * quat_z),
            2 * (quat_y * quat_z - quat_w * quat_x),
        ],
        [
            2 * (quat_x * quat_z - quat_w * quat_y),
            2 * (quat_y * quat_z + quat_w * quat_x),
            1 - 2 * (quat_x * quat_x + quat_y * quat_y),
        ],
    ]
    focal_px = 0.3125 * float(WIN * TSIDE)
    inv_z = 1.0 / mean_z
    scale_z = focal_px * inv_z
    off_u = scale_z * mean_x
    off_v = scale_z * mean_y
    slope_u = off_u * inv_z
    slope_v = off_v * inv_z
    proj_u = [(scale_z * rotation[0][i] - slope_u * rotation[2][i]) * scales[i] for i in range(3)]
    proj_v = [(scale_z * rotation[1][i] - slope_v * rotation[2][i]) * scales[i] for i in range(3)]
    sigma_xx = proj_u[0] * proj_u[0] + proj_u[1] * proj_u[1] + proj_u[2] * proj_u[2] + 0.3
    sigma_xy = proj_u[0] * proj_v[0] + proj_u[1] * proj_v[1] + proj_u[2] * proj_v[2]
    sigma_yy = proj_v[0] * proj_v[0] + proj_v[1] * proj_v[1] + proj_v[2] * proj_v[2] + 0.3
    determinant = sigma_xx * sigma_yy - sigma_xy * sigma_xy
    inv_det = log2_e / determinant
    con_xx = sigma_yy * inv_det
    con_xy = -sigma_xy * inv_det
    con_yy = sigma_xx * inv_det
    lin_x = con_xx * off_u + con_xy * off_v
    lin_y = con_xy * off_u + con_yy * off_v
    logit = rows[10]
    log_opacity = (logit - jnp.log(1.0 + jnp.exp(logit))) * log2_e
    const = log_opacity - 0.5 * (lin_x * off_u + lin_y * off_v)
    coefs = [const, lin_x, lin_y, -0.5 * con_xx, -con_xy, -0.5 * con_yy]
    inv_len = 1.0 / jnp.sqrt(mean_x * mean_x + mean_y * mean_y + mean_z * mean_z)
    dir_x, dir_y, dir_z = mean_x * inv_len, mean_y * inv_len, mean_z * inv_len
    sq_x, sq_y, sq_z = dir_x * dir_x, dir_y * dir_y, dir_z * dir_z
    harmonics = [
        None,
        -harmonic_one * dir_y,
        harmonic_one * dir_z,
        -harmonic_one * dir_x,
        harmonic_two[0] * dir_x * dir_y,
        harmonic_two[1] * dir_y * dir_z,
        harmonic_two[2] * (2 * sq_z - sq_x - sq_y),
        harmonic_two[3] * dir_x * dir_z,
        harmonic_two[4] * (sq_x - sq_y),
        harmonic_three[0] * dir_y * (3 * sq_x - sq_y),
        harmonic_three[1] * dir_x * dir_y * dir_z,
        harmonic_three[2] * dir_y * (4 * sq_z - sq_x - sq_y),
        harmonic_three[3] * dir_z * (2 * sq_z - 3 * sq_x - 3 * sq_y),
        harmonic_three[4] * dir_x * (4 * sq_z - sq_x - sq_y),
        harmonic_three[5] * dir_z * (sq_x - sq_y),
        harmonic_three[6] * dir_x * (sq_x - 3 * sq_y),
    ]
    colours = []
    for colour_no in range(3):
        base = 11 + 16 * colour_no
        total = rows[base] * harmonic_zero
        for k in range(1, 16):
            total = total + rows[base + k] * harmonics[k]
        colours.append(jnp.maximum(total + 0.5, 0.0))
    return coefs, colours


def split3(value):
    high = value.astype(bf16).astype(f32)
    rest = value - high
    middle = rest.astype(bf16).astype(f32)
    return high, middle, rest - middle


def split2(value):
    high = value.astype(bf16)
    return high, (value - high.astype(f32)).astype(bf16)


def pixel_basis(pieces):
    tiles = np.arange(pieces)[:, None]
    pixels = np.arange(PIX)[None, :]
    half = WIN * TSIDE / 2
    pos_x = TSIDE * (tiles % WIN) + pixels % TSIDE + 0.5 - half
    pos_y = TSIDE * (tiles // WIN) + pixels // TSIDE + 0.5 - half
    rows = [np.ones_like(pos_x), pos_x, pos_y]
    for product in (pos_x * pos_x, pos_x * pos_y, pos_y * pos_y):
        high = product.astype(bf16).astype(np.float64)
        rows += [high, product - high]
    table = np.zeros((pieces, KE, PIX))
    for row_no, row in enumerate(rows * 3):
        table[:, row_no] = row
    return table.astype(bf16)


def basis_coefs(coefs):
    return [coefs[i] for i in (0, 1, 2, 3, 3, 4, 4, 5, 5)]


def lane_order(shape, inverse):
    lane = lax.broadcasted_iota(jnp.int32, shape, 1)
    if inverse:
        return (lane % ROWS) * SUBL + lane // ROWS
    return (lane % SUBL) * ROWS + lane // SUBL


def prefix_product(total):
    sub = lax.broadcasted_iota(jnp.int32, total.shape, 0)
    run = total
    for step in (1, 2, 4):
        run = jnp.where(sub >= step, run * pltpu.roll(run, step, 0), run)
    before = jnp.where(sub >= 1, pltpu.roll(run, 1, 0), 1.0)
    return before, run[SUBL - 1 :]


def suffix_affine(total, keep, behind):
    sub = lax.broadcasted_iota(jnp.int32, total.shape, 0)
    value, gain = total, keep
    for step in (1, 2, 4):
        inside = sub < SUBL - step
        next_value = jnp.where(inside, pltpu.roll(value, SUBL - step, 0), 0.0)
        next_gain = jnp.where(inside, pltpu.roll(gain, SUBL - step, 0), 1.0)
        value = value + gain * next_value
        gain = gain * next_gain
    whole = value + gain * behind
    after = jnp.where(sub < SUBL - 1, pltpu.roll(whole, SUBL - 1, 0), behind)
    return after, whole[:1]


def list_items(blocks_ref, live_ref, items_ref, pieces, own_blocks):
    room = pieces + SUBL
    doubles, singles = jnp.int32(0), jnp.int32(0)
    for piece in range(pieces):
        entries = []
        for slot in range(2):
            block = blocks_ref[slot, piece]
            place = jnp.where(block == 0, own_blocks + 1, block - 1)
            entries.append(place * 64 + piece)
        items_ref[doubles] = entries[0]
        items_ref[room + doubles] = entries[1]
        items_ref[2 * room + singles] = entries[0]
        second = live_ref[0, piece] - 1
        doubles = doubles + second
        singles = singles + 1 - second
    for spare in range(6):
        items_ref[2 * room + singles + spare] = (own_blocks + 2) * 64 + pieces
    items_ref[3 * room] = doubles
    items_ref[3 * room + 1] = (doubles + (singles + 1) // 2 + 1) // 2


def item_slots(items_ref, item, pieces):
    room = pieces + SUBL
    doubles = items_ref[3 * room]
    chained = item < doubles
    single = 2 * (room + item - doubles)
    first = items_ref[jnp.where(chained, item, single)]
    second = items_ref[jnp.where(chained, room + item, single + 1)]
    slots = []
    for entry in (first, second):
        slots.append((entry % 64, pl.multiple_of(entry // 64 * BLOCK, BLOCK)))
    return chained, slots


def pipelined(pairs, front, back):
    front(0, 0)

    def step(pair, carry):
        for side in range(2):
            front(2 * pair + side + 1, 1 - side)
            back(2 * pair + side, side)
        return carry

    lax.fori_loop(0, pairs, step, 0)


def exponents(table_ref, basis_ref, piece, start, pieces):
    unit = basis_ref[jnp.minimum(piece, pieces - 1)]
    rhs = jnp.concatenate([unit, jnp.zeros((KC, PIX), bf16)], axis=0)
    return jnp.dot(table_ref[pl.ds(start, BLOCK), :], rhs, preferred_element_type=f32)


def forward_kernel(
    blocks_ref,
    live_ref,
    owner_ref,
    cell_ref,
    params_ref,
    inner_ref,
    outer_ref,
    target_ref,
    basis_ref,
    out_ref,
    table_ref,
    items_ref,
    own_rows_ref,
    copy_rows_ref,
    stage_ref,
    colour_ref,
    result_ref,
    local_refs,
    before_refs,
    left_refs,
):
    doms, pieces = out_ref.shape[0], basis_ref.shape[0]
    own_blocks = params_ref.shape[1] // BLOCK
    region_idx, regions = lax.axis_index("region"), lax.axis_size("region")
    even = region_idx % 2 == 0
    list_items(blocks_ref, live_ref, items_ref, pieces, own_blocks)
    for block in range(own_blocks):
        own_rows_ref[pl.ds(block, PARAMS, stride=SUBL), :] = params_ref[
            :, block * BLOCK : (block + 1) * BLOCK
        ]
    inner, outer = inner_ref[...], outer_ref[...]
    copy_rows_ref[pl.ds(0, PARAMS, stride=SUBL), :] = jnp.where(even, inner, outer)
    copy_rows_ref[pl.ds(1, PARAMS, stride=SUBL), :] = jnp.where(even, outer, inner)
    rows = []
    for i in range(PARAMS):
        span = slice(i * SUBL, (i + 1) * SUBL)
        rows.append(jnp.concatenate([own_rows_ref[span, :], copy_rows_ref[span, :]], axis=0))
    coefs, colours = splat_rows(rows)
    shape = (SLOTS, LANES)
    slot_no = lax.broadcasted_iota(jnp.int32, shape, 0)
    present = (
        (slot_no < own_blocks)
        | ((slot_no == own_blocks) & (region_idx < regions - 1))
        | ((slot_no == own_blocks + 1) & (region_idx > 0))
    )
    order = lane_order(shape, False)

    def settled(value, absent):
        return jnp.take_along_axis(jnp.where(present, value, absent), order, axis=1)

    coefs = [settled(value, -1e9 if i == 0 else 0.0) for i, value in enumerate(coefs)]
    colours = [settled(value, 0.0) for value in colours]
    nothing = jnp.zeros(shape, f32)
    parts = basis_coefs([split3(value) for value in coefs])
    lines = [parts[row % BASIS][row // BASIS] for row in range(3 * BASIS)]
    lines += [nothing] * (KE - 3 * BASIS)
    triples = [split3(value) for value in colours]
    for level in (0, 0, 1, 0, 0, 1):
        lines += [triple[level] for triple in triples] + [nothing]
    for row, value in enumerate(lines):
        group, place = divmod(row, SUBL)
        base = group * SLOTS * SUBL + place
        stage_ref[pl.ds(base, SUBL, stride=SUBL), :] = value[:SUBL]
        stage_ref[pl.ds(base + SUBL * SUBL, 4, stride=SUBL), :] = value[SUBL : SUBL + 4]
    for block in range(own_blocks + 3):
        tiles = [
            stage_ref[(group * SLOTS + block) * SUBL : (group * SLOTS + block + 1) * SUBL, :]
            for group in range(len(lines) // SUBL)
        ]
        span = slice(block * BLOCK, (block + 1) * BLOCK)
        table_ref[span, :] = jnp.concatenate(tiles[: KT // SUBL], axis=0).T.astype(bf16)
        colour_ref[block] = jnp.concatenate(tiles[KT // SUBL :] * 2, axis=0).astype(bf16)

    def front(item, side):
        chained, slots = item_slots(items_ref, item, pieces)
        carry = None
        for slot, (piece, start) in enumerate(slots):
            alphas = jnp.exp2(exponents(table_ref, basis_ref, piece, start, pieces))
            keep = None
            for row in range(ROWS):
                alpha = alphas[row * SUBL : (row + 1) * SUBL]
                weight = alpha if keep is None else alpha * keep
                keep = 1.0 - alpha if keep is None else keep - weight
                first = slot * BLOCK + row * SUBL
                local_refs[side][first : first + SUBL, :] = weight
            before, total = prefix_product(keep)
            if slot == 1:
                carry = jnp.where(chained, carry, 1.0)
                before, total = before * carry, total * carry
            carry = total
            before_refs[side][slot * SUBL : (slot + 1) * SUBL, :] = before
            left_refs[side][slot : slot + 1, :] = total

    def back(item, side):
        chained, slots = item_slots(items_ref, item, pieces)
        sums = None
        for slot, (piece, start) in enumerate(slots):
            before = before_refs[side][slot * SUBL : (slot + 1) * SUBL, :]
            weights = []
            for row in range(ROWS):
                first = slot * BLOCK + row * SUBL
                weights.append(local_refs[side][first : first + SUBL, :] * before)
            high, low = split2(jnp.concatenate(weights, axis=0))
            left = colour_ref[start // BLOCK]
            wide = jnp.dot(left, high, preferred_element_type=f32)
            wide = (wide + jnp.dot(left, low, preferred_element_type=f32))[:SUBL]
            wide = wide + pltpu.roll(wide, 4, 0)
            sums = wide + jnp.where(chained, sums, 0.0) if slot else wide
            row_no = lax.broadcasted_iota(jnp.int32, sums.shape, 0)
            value = jnp.where(row_no == 3, 1.0 - left_refs[side][slot : slot + 1, :], sums)
            for half in range(PIX // LANES):
                first = pl.multiple_of((half * (pieces + 1) + piece) * SUBL, SUBL)
                result_ref[pl.ds(first, SUBL), :] = value[:, half * LANES : (half + 1) * LANES]

    pipelined(items_ref[3 * (pieces + SUBL) + 1], front, back)
    width = PIX // doms
    lane = lax.broadcasted_iota(jnp.int32, (pieces, LANES), 1)
    tile_lane = lax.broadcasted_iota(jnp.int32, (SUBL, LANES), 1)
    tiles = target_ref.shape[1]
    cell = cell_ref[...]
    labels = (cell % MAXD) * (doms * tiles) + owner_ref[...] * tiles + cell // MAXD
    labels = jnp.concatenate(
        [jnp.zeros((1, LANES - pieces), f32), labels.astype(f32)], axis=1
    )
    labels = jnp.broadcast_to(labels, (SUBL, LANES))
    for dom in range(doms):
        half, offset = divmod(dom * width, LANES)
        span = slice(half * LANES, (half + 1) * LANES)
        packed, aimed = None, None
        for channel in range(4):
            shift = (channel * GROUP - offset) % LANES
            first = half * (pieces + 1) * SUBL + channel
            value = result_ref[pl.ds(first, pieces, stride=SUBL), :]
            value = pltpu.roll(value, shift, 1) if shift else value
            packed = value if packed is None else jnp.where(lane >= channel * GROUP, value, packed)
            if channel < 3:
                value = target_ref[channel, :, span]
                value = pltpu.roll(value, shift, 1) if shift else value
            else:
                value = labels
            aimed = value if aimed is None else jnp.where(tile_lane >= channel * GROUP, value, aimed)
        out_ref[dom, :pieces, :] = packed
        out_ref[dom, pieces : pieces + tiles, :] = aimed


def composite_kernel(background_ref, arrived_ref, out_ref):
    doms, pieces = out_ref.shape[0], out_ref.shape[1]
    tiles = arrived_ref.shape[1] - pieces
    all_pieces, all_tiles = doms * pieces, doms * tiles
    per_row = LANES // GROUP
    lane = lax.broadcasted_iota(jnp.int32, (1, LANES), 1)
    label_rows = []
    for dom in range(doms):
        place = dom % per_row
        value = arrived_ref[dom, pieces : pieces + 1, :]
        shift = ((place - 3) * GROUP) % LANES
        value = pltpu.roll(value, shift, 1) if shift else value
        if place == 0:
            label_rows.append(value)
        else:
            label_rows[-1] = jnp.where(lane >= place * GROUP, value, label_rows[-1])
    cells_all = MAXD * all_tiles
    cell_no = lax.broadcasted_iota(jnp.int32, (cells_all, LANES), 0).astype(f32)
    to_cells = jnp.concatenate(
        [jnp.where(cell_no == row, 1.0, 0.0).astype(bf16) for row in label_rows], axis=1
    )
    upright = jnp.concatenate([jnp.broadcast_to(row, (SUBL, LANES)).T for row in label_rows], axis=0)
    cell_no = lax.broadcasted_iota(jnp.int32, (all_pieces, cells_all), 1).astype(f32)
    to_pieces = jnp.where(cell_no == upright[:, :1], 1.0, 0.0).astype(bf16)

    def moved(matrix, values):
        triple = jnp.concatenate([part.astype(bf16) for part in split3(values)], axis=1)
        wide = jnp.dot(matrix, triple, preferred_element_type=f32)
        return wide[:, :LANES] + wide[:, LANES : 2 * LANES] + wide[:, 2 * LANES :]

    data = arrived_ref[:, :pieces, :].reshape(all_pieces, LANES)
    cells = moved(to_cells, data)
    goal = arrived_ref[:, pieces:, :].reshape(all_tiles, LANES)
    lane = lax.broadcasted_iota(jnp.int32, (all_tiles, LANES), 1)
    last = lane >= 3 * GROUP
    backdrop = jnp.where(
        lane < GROUP,
        background_ref[0],
        jnp.where(lane < 2 * GROUP, background_ref[1], background_ref[2]),
    )

    def spread(value):
        return pltpu.roll(value, GROUP, 1) + pltpu.roll(value, 2 * GROUP, 1) + pltpu.roll(
            value, 3 * GROUP, 1
        )

    fronts, through, layers = [], [], []
    front = jnp.ones((all_tiles, LANES), f32)
    composite = jnp.zeros((all_tiles, LANES), f32)
    for depth in range(MAXD):
        layer = cells[depth * all_tiles : (depth + 1) * all_tiles]
        passed = jnp.where(last, 1.0 - layer, 0.0)
        passed = passed + spread(passed)
        fronts.append(front)
        through.append(passed)
        layers.append(layer)
        composite = composite + front * layer
        front = front * passed
    residual = jnp.where(last, 0.0, composite + front * backdrop - goal)
    behind = backdrop
    grads = [None] * MAXD
    for depth in reversed(range(MAXD)):
        grads[depth] = fronts[depth] * jnp.where(last, spread(residual * behind), residual)
        behind = layers[depth] + through[depth] * behind
    back = moved(to_pieces, jnp.concatenate(grads, axis=0))
    out_ref[...] = back.reshape(out_ref.shape)


def backward_kernel(
    items_ref,
    back_ref,
    table_ref,
    basis_ref,
    own_ref,
    inner_ref,
    outer_ref,
    grad_ref,
    sums_ref,
    alpha_refs,
    shade_refs,
    local_refs,
    before_refs,
    hidden_refs,
):
    doms, pieces = back_ref.shape[0], back_ref.shape[1]
    own_blocks = own_ref.shape[1]
    width = PIX // doms
    lane = lax.broadcasted_iota(jnp.int32, (pieces, LANES), 1)
    grad_ref[...] = jnp.zeros_like(grad_ref)
    sums_ref[...] = jnp.zeros_like(sums_ref)
    for half in range(PIX // LANES):
        for channel in range(4):
            gathered = None
            for dom in range(half * LANES // width, (half + 1) * LANES // width):
                offset = dom * width - half * LANES
                shift = (offset - channel * GROUP) % LANES
                value = back_ref[dom]
                value = pltpu.roll(value, shift, 1) if shift else value
                gathered = value if gathered is None else jnp.where(lane >= offset, value, gathered)
            first = half * (pieces + 1) * SUBL + channel
            grad_ref[pl.ds(first, pieces, stride=SUBL), :] = gathered

    def grads_of(piece):
        halves = []
        for half in range(PIX // LANES):
            first = pl.multiple_of((half * (pieces + 1) + piece) * SUBL, SUBL)
            halves.append(grad_ref[pl.ds(first, SUBL), :])
        grads = jnp.concatenate(halves, axis=1)
        upper = lax.broadcasted_iota(jnp.int32, grads.shape, 0) < 4
        high, middle, low = split3(grads)
        first = jnp.where(upper, high, pltpu.roll(middle, 4, 0))
        return grads, first, jnp.where(upper, high, pltpu.roll(low, 4, 0))

    def front(item, side):
        chained, slots = item_slots(items_ref, item, pieces)
        carry, ends = None, []
        for slot, (piece, start) in enumerate(slots):
            alphas = jnp.exp2(exponents(table_ref, basis_ref, piece, start, pieces))
            grads, first, second = grads_of(piece)
            rhs = jnp.concatenate([first, second], axis=0).astype(bf16)
            rhs = jnp.concatenate([jnp.zeros((KE, PIX), bf16), rhs], axis=0)
            shades = jnp.dot(table_ref[pl.ds(start, BLOCK), :], rhs, preferred_element_type=f32)
            span = slice(slot * BLOCK, (slot + 1) * BLOCK)
            alpha_refs[side][span, :] = alphas
            shade_refs[side][span, :] = shades
            keep, total = None, None
            for row in range(ROWS):
                alpha = alphas[row * SUBL : (row + 1) * SUBL]
                weight = alpha if keep is None else alpha * keep
                keep = 1.0 - alpha if keep is None else keep - weight
                value = weight * shades[row * SUBL : (row + 1) * SUBL]
                total = value if total is None else total + value
                first = slot * BLOCK + row * SUBL
                local_refs[side][first : first + SUBL, :] = weight
            before, whole = prefix_product(keep)
            if slot == 1:
                before = before * jnp.where(chained, carry, 1.0)
            carry = whole
            before_refs[side][slot * SUBL : (slot + 1) * SUBL, :] = before
            ends.append((total, keep, grads[3:4]))
        behind = None
        for slot in (1, 0):
            total, keep, final = ends[slot]
            behind = jnp.where(chained, behind, final) if slot == 0 else final
            hidden, behind = suffix_affine(total, keep, behind)
            hidden_refs[side][slot * SUBL : (slot + 1) * SUBL, :] = hidden

    def back(item, side):
        along = (((1,), (1,)), ((), ()))
        _, slots = item_slots(items_ref, item, pieces)
        for slot, (piece, start) in enumerate(slots):
            before = before_refs[side][slot * SUBL : (slot + 1) * SUBL, :]
            hidden = hidden_refs[side][slot * SUBL : (slot + 1) * SUBL, :]
            pulls, weights = [None] * ROWS, [None] * ROWS
            for row in reversed(range(ROWS)):
                first = slot * BLOCK + row * SUBL
                span = slice(first, first + SUBL)
                weight = local_refs[side][span, :] * before
                gap = shade_refs[side][span, :] - hidden
                weights[row] = weight
                pulls[row] = weight * gap
                hidden = hidden + alpha_refs[side][span, :] * gap
            unit = basis_ref[jnp.minimum(piece, pieces - 1)][:TOP]
            _, first, second = grads_of(piece)
            g_lhs = jnp.concatenate([first, second], axis=0).astype(bf16)
            for base, left, values in ((0, unit, pulls), (2, g_lhs, weights)):
                part = None
                for value in split2(jnp.concatenate(values, axis=0)):
                    product = lax.dot_general(left, value, along, preferred_element_type=f32)
                    part = product if part is None else part + product
                for group in range(2 if base == 0 else 1):
                    row = (base + group) * SLOTS * SUBL + start // BLOCK * SUBL
                    rows = pl.ds(pl.multiple_of(row, SUBL), SUBL)
                    sums_ref[rows, :] = (
                        sums_ref[rows, :] + part[group * SUBL : (group + 1) * SUBL]
                    )

    pipelined(items_ref[3 * (pieces + SUBL) + 1], front, back)

    def rows_of(row):
        group, place = divmod(row, SUBL)
        return sums_ref[pl.ds(group * SLOTS * SUBL + place, SLOTS, stride=SUBL), :]

    moments = [rows_of(0), rows_of(1), rows_of(2)]
    moments += [rows_of(3 + 2 * i) + rows_of(4 + 2 * i) for i in range(3)]
    terms = [value * ln_2 for value in moments]
    terms += [rows_of(TOP + i) + rows_of(TOP + 4 + i) for i in range(3)]
    order = lane_order((SLOTS, LANES), True)
    even = lax.axis_index("region") % 2 == 0
    inner_ref[...] = jnp.zeros_like(inner_ref)
    outer_ref[...] = jnp.zeros_like(outer_ref)
    for term_no, value in enumerate(terms):
        value = jnp.take_along_axis(value, order, axis=1)
        own_ref[term_no] = value[:own_blocks]
        high = value[own_blocks : own_blocks + 1]
        low = value[own_blocks + 1 : own_blocks + 2]
        inner_ref[term_no : term_no + 1, :] = jnp.where(even, high, low)
        outer_ref[term_no : term_no + 1, :] = jnp.where(even, low, high)


def update_kernel(
    params_ref,
    first_ref,
    second_ref,
    own_ref,
    inner_ref,
    outer_ref,
    gradient_ref,
    new_params_ref,
    new_first_ref,
    new_second_ref,
    rows_ref,
    grads_ref,
):
    own_blocks = own_ref.shape[1]
    for block in range(own_blocks):
        rows_ref[pl.ds(block, PARAMS, stride=own_blocks), :] = params_ref[
            :, block * BLOCK : (block + 1) * BLOCK
        ]
    rows = [rows_ref[i * own_blocks : (i + 1) * own_blocks, :] for i in range(PARAMS)]
    slot = lax.broadcasted_iota(jnp.int32, (own_blocks, LANES), 0)
    even = lax.axis_index("region") % 2 == 0
    from_low = jnp.where(even, outer_ref[...], inner_ref[...])
    from_high = jnp.where(even, inner_ref[...], outer_ref[...])
    cots = []
    for term_no in range(9):
        low = jnp.where(slot == 0, from_low[term_no : term_no + 1, :], 0.0)
        high = jnp.where(slot == own_blocks - 1, from_high[term_no : term_no + 1, :], 0.0)
        cots.append(own_ref[term_no] + low + high)
    _, pull_back = jax.vjp(splat_rows, rows)
    pulled = pull_back((cots[:6], cots[6:]))[0]
    for i in range(PARAMS):
        grads_ref[i * own_blocks : (i + 1) * own_blocks, :] = pulled[i]
    for block in range(own_blocks):
        span = slice(block * BLOCK, (block + 1) * BLOCK)
        gradient = grads_ref[pl.ds(block, PARAMS, stride=own_blocks), :]
        new_first = beta_one * first_ref[:, span] + (1 - beta_one) * gradient
        new_second = beta_two * second_ref[:, span] + (1 - beta_two) * gradient * gradient
        update = (
            new_first
            / (1 - beta_one**adam_step)
            / (jnp.sqrt(new_second / (1 - beta_two**adam_step)) + tiny)
        )
        gradient_ref[:, span] = gradient
        new_params_ref[:, span] = params_ref[:, span] - rate * update
        new_first_ref[:, span] = new_first
        new_second_ref[:, span] = new_second


def exchange(to_inner, to_outer):
    count = lax.axis_size("region")
    inner = [(i, i ^ 1) for i in range(count) if (i ^ 1) < count]
    outer = [(i, i + 1) for i in range(1, count - 1, 2)]
    outer += [(target, source) for source, target in outer]
    return lax.ppermute(to_inner, "region", inner), lax.ppermute(to_outer, "region", outer)


def on_device(
    params,
    first_moment,
    second_moment,
    piece_blocks,
    piece_live,
    piece_owner,
    piece_cell,
    target,
    background,
):
    own_blocks = params.shape[1] // BLOCK
    doms = lax.axis_size("dom")
    pieces = piece_live.shape[1]
    tiles = target.shape[1]
    even = lax.axis_index("region") % 2 == 0
    low, high = params[:, :BLOCK], params[:, -BLOCK:]
    inner, outer = exchange(jnp.where(even, high, low), jnp.where(even, low, high))
    basis = jnp.asarray(pixel_basis(pieces))
    smem = pl.BlockSpec(memory_space=pltpu.SMEM)
    vmem = pl.BlockSpec(memory_space=pltpu.VMEM)
    plane = pltpu.VMEM((2 * BLOCK, PIX), f32)
    strip = pltpu.VMEM((2 * SUBL, PIX), f32)
    piece_rows = pltpu.VMEM((PIX // LANES * (pieces + 1) * SUBL, LANES), f32)
    payload, table, items = pl.pallas_call(
        forward_kernel,
        out_shape=(
            jax.ShapeDtypeStruct((doms, pieces + tiles, LANES), f32),
            jax.ShapeDtypeStruct(((own_blocks + 3) * BLOCK, KT), bf16),
            jax.ShapeDtypeStruct((3 * (pieces + SUBL) + 2,), jnp.int32),
        ),
        in_specs=[smem] * 2 + [vmem] * 7,
        out_specs=(vmem, vmem, smem),
        scratch_shapes=[
            pltpu.VMEM((64 * SUBL, LANES), f32),
            pltpu.VMEM((64 * SUBL, LANES), f32),
            pltpu.VMEM(((KT // SUBL + 1) * SLOTS * SUBL, LANES), f32),
            pltpu.VMEM((own_blocks + 3, TOP, LANES), bf16),
            piece_rows,
            [plane] * 2,
            [strip] * 2,
            [strip] * 2,
        ],
        name="forward",
        compiler_params=pltpu.CompilerParams(vmem_limit_bytes=vmem_limit),
    )(
        piece_blocks[0].T,
        piece_live,
        piece_owner,
        piece_cell,
        params,
        inner,
        outer,
        jnp.transpose(target[0], (1, 0, 2)),
        basis,
    )
    arrived = lax.all_to_all(payload, "dom", split_axis=0, concat_axis=0, tiled=True)
    back = pl.pallas_call(
        composite_kernel,
        out_shape=jax.ShapeDtypeStruct((doms, pieces, LANES), f32),
        in_specs=[smem, vmem],
        out_specs=vmem,
        name="composite",
        compiler_params=pltpu.CompilerParams(vmem_limit_bytes=vmem_limit),
    )(background, arrived)
    returned = lax.all_to_all(back, "dom", split_axis=0, concat_axis=0, tiled=True)
    own, to_inner, to_outer = pl.pallas_call(
        backward_kernel,
        out_shape=(
            jax.ShapeDtypeStruct((9, own_blocks, LANES), f32),
            jax.ShapeDtypeStruct((SLOTS, LANES), f32),
            jax.ShapeDtypeStruct((SLOTS, LANES), f32),
        ),
        in_specs=[smem] + [vmem] * 3,
        out_specs=(vmem, vmem, vmem),
        scratch_shapes=[
            piece_rows,
            pltpu.VMEM((3 * SLOTS * SUBL, LANES), f32),
            [plane] * 2,
            [plane] * 2,
            [plane] * 2,
            [strip] * 2,
            [strip] * 2,
        ],
        name="backward",
        compiler_params=pltpu.CompilerParams(vmem_limit_bytes=vmem_limit),
    )(items, returned, table, basis)
    inner, outer = exchange(to_inner, to_outer)
    shape = jax.ShapeDtypeStruct(params.shape, f32)
    return pl.pallas_call(
        update_kernel,
        out_shape=(shape, shape, shape, shape),
        in_specs=[vmem] * 6,
        out_specs=(vmem,) * 4,
        scratch_shapes=[
            pltpu.VMEM((64 * own_blocks, LANES), f32),
            pltpu.VMEM((64 * own_blocks, LANES), f32),
        ],
        name="update",
        compiler_params=pltpu.CompilerParams(vmem_limit_bytes=vmem_limit),
    )(params, first_moment, second_moment, own, inner, outer)


def solution(mesh):
    in_specs = (
        P(None, ("region", "dom")),
        P(None, ("region", "dom")),
        P(None, ("region", "dom")),
        P(("region", "dom"), None, None),
        P(("region", "dom"), None),
        P(("region", "dom"), None),
        P(("region", "dom"), None),
        P(("region", "dom"), None, None, None),
        P(),
    )
    out_specs = (P(None, ("region", "dom")),) * 4
    return jax.shard_map(
        on_device, mesh=mesh, in_specs=in_specs, out_specs=out_specs, check_vma=False
    )
```

```python
import math

import numpy as np
import jax
import jax.numpy as jnp
from jax import lax
from jax.experimental import pallas as pl
from jax.experimental.pallas import tpu as pltpu
from jax.sharding import PartitionSpec as P

PARAMS = 59
TSIDE = 16
WIN = 8
BLOCK = 128
MAXD = 8
PIX = 256

harmonic_zero = 0.28209479177387814
harmonic_one = 0.4886025119029199
harmonic_two = (
    1.0925484305920792,
    -1.0925484305920792,
    0.31539156525252005,
    -1.0925484305920792,
    0.5462742152960396,
)
harmonic_three = (
    -0.5900435899266435,
    2.890611442640554,
    -0.4570457994644658,
    0.3731763325901154,
    -0.4570457994644658,
    1.445305721320277,
    -0.5900435899266435,
)
beta_one = 0.9
beta_two = 0.999
rate = 0.001
adam_step = 100
tiny = 1e-08
log2_e = math.log2(math.e)
ln_2 = math.log(2.0)

LANES = 128
SUBL = 8
ROWS = BLOCK // SUBL
GROUP = LANES // 4
BASIS = 9
KE = 32
KC = 2 * SUBL
KT = KE + KC
TOP = 16
SLOTS = 16
vmem_limit = 12 * 2**20
f32 = jnp.float32
bf16 = jnp.bfloat16


def splat_rows(rows):
    mean_x, mean_y, mean_z = rows[0], rows[1], rows[2]
    scales = [jnp.exp(rows[3]), jnp.exp(rows[4]), jnp.exp(rows[5])]
    norm_sq = rows[6] * rows[6] + rows[7] * rows[7] + rows[8] * rows[8] + rows[9] * rows[9]
    inv_norm = 1.0 / jnp.sqrt(norm_sq)
    quat_w, quat_x, quat_y, quat_z = [rows[6 + i] * inv_norm for i in range(4)]
    rotation = [
        [
            1 - 2 * (quat_y * quat_y + quat_z * quat_z),
            2 * (quat_x * quat_y - quat_w * quat_z),
            2 * (quat_x * quat_z + quat_w * quat_y),
        ],
        [
            2 * (quat_x * quat_y + quat_w * quat_z),
            1 - 2 * (quat_x * quat_x + quat_z * quat_z),
            2 * (quat_y * quat_z - quat_w * quat_x),
        ],
        [
            2 * (quat_x * quat_z - quat_w * quat_y),
            2 * (quat_y * quat_z + quat_w * quat_x),
            1 - 2 * (quat_x * quat_x + quat_y * quat_y),
        ],
    ]
    focal_px = 0.3125 * float(WIN * TSIDE)
    inv_z = 1.0 / mean_z
    scale_z = focal_px * inv_z
    off_u = scale_z * mean_x
    off_v = scale_z * mean_y
    slope_u = off_u * inv_z
    slope_v = off_v * inv_z
    proj_u = [(scale_z * rotation[0][i] - slope_u * rotation[2][i]) * scales[i] for i in range(3)]
    proj_v = [(scale_z * rotation[1][i] - slope_v * rotation[2][i]) * scales[i] for i in range(3)]
    sigma_xx = proj_u[0] * proj_u[0] + proj_u[1] * proj_u[1] + proj_u[2] * proj_u[2] + 0.3
    sigma_xy = proj_u[0] * proj_v[0] + proj_u[1] * proj_v[1] + proj_u[2] * proj_v[2]
    sigma_yy = proj_v[0] * proj_v[0] + proj_v[1] * proj_v[1] + proj_v[2] * proj_v[2] + 0.3
    determinant = sigma_xx * sigma_yy - sigma_xy * sigma_xy
    inv_det = log2_e / determinant
    con_xx = sigma_yy * inv_det
    con_xy = -sigma_xy * inv_det
    con_yy = sigma_xx * inv_det
    lin_x = con_xx * off_u + con_xy * off_v
    lin_y = con_xy * off_u + con_yy * off_v
    logit = rows[10]
    log_opacity = (logit - jnp.log(1.0 + jnp.exp(logit))) * log2_e
    const = log_opacity - 0.5 * (lin_x * off_u + lin_y * off_v)
    coefs = [const, lin_x, lin_y, -0.5 * con_xx, -con_xy, -0.5 * con_yy]
    inv_len = 1.0 / jnp.sqrt(mean_x * mean_x + mean_y * mean_y + mean_z * mean_z)
    dir_x, dir_y, dir_z = mean_x * inv_len, mean_y * inv_len, mean_z * inv_len
    sq_x, sq_y, sq_z = dir_x * dir_x, dir_y * dir_y, dir_z * dir_z
    harmonics = [
        None,
        -harmonic_one * dir_y,
        harmonic_one * dir_z,
        -harmonic_one * dir_x,
        harmonic_two[0] * dir_x * dir_y,
        harmonic_two[1] * dir_y * dir_z,
        harmonic_two[2] * (2 * sq_z - sq_x - sq_y),
        harmonic_two[3] * dir_x * dir_z,
        harmonic_two[4] * (sq_x - sq_y),
        harmonic_three[0] * dir_y * (3 * sq_x - sq_y),
        harmonic_three[1] * dir_x * dir_y * dir_z,
        harmonic_three[2] * dir_y * (4 * sq_z - sq_x - sq_y),
        harmonic_three[3] * dir_z * (2 * sq_z - 3 * sq_x - 3 * sq_y),
        harmonic_three[4] * dir_x * (4 * sq_z - sq_x - sq_y),
        harmonic_three[5] * dir_z * (sq_x - sq_y),
        harmonic_three[6] * dir_x * (sq_x - 3 * sq_y),
    ]
    colours = []
    for colour_no in range(3):
        base = 11 + 16 * colour_no
        total = rows[base] * harmonic_zero
        for k in range(1, 16):
            total = total + rows[base + k] * harmonics[k]
        colours.append(jnp.maximum(total + 0.5, 0.0))
    return coefs, colours


def split3(value):
    high = value.astype(bf16).astype(f32)
    rest = value - high
    middle = rest.astype(bf16).astype(f32)
    return high, middle, rest - middle


def split2(value):
    high = value.astype(bf16)
    return high, (value - high.astype(f32)).astype(bf16)


def pixel_basis(pieces):
    tiles = np.arange(pieces)[:, None]
    pixels = np.arange(PIX)[None, :]
    half = WIN * TSIDE / 2
    pos_x = TSIDE * (tiles % WIN) + pixels % TSIDE + 0.5 - half
    pos_y = TSIDE * (tiles // WIN) + pixels // TSIDE + 0.5 - half
    rows = [np.ones_like(pos_x), pos_x, pos_y]
    for product in (pos_x * pos_x, pos_x * pos_y, pos_y * pos_y):
        high = product.astype(bf16).astype(np.float64)
        rows += [high, product - high]
    table = np.zeros((pieces, KE, PIX))
    for row_no, row in enumerate(rows * 3):
        table[:, row_no] = row
    return table.astype(bf16)


def basis_coefs(coefs):
    return [coefs[i] for i in (0, 1, 2, 3, 3, 4, 4, 5, 5)]


def lane_order(shape, inverse):
    lane = lax.broadcasted_iota(jnp.int32, shape, 1)
    if inverse:
        return (lane % ROWS) * SUBL + lane // ROWS
    return (lane % SUBL) * ROWS + lane // SUBL


def prefix_product(total):
    sub = lax.broadcasted_iota(jnp.int32, total.shape, 0)
    run = total
    for step in (1, 2, 4):
        run = jnp.where(sub >= step, run * pltpu.roll(run, step, 0), run)
    before = jnp.where(sub >= 1, pltpu.roll(run, 1, 0), 1.0)
    return before, run[SUBL - 1 :]


def suffix_affine(total, keep, behind):
    sub = lax.broadcasted_iota(jnp.int32, total.shape, 0)
    value, gain = total, keep
    for step in (1, 2, 4):
        inside = sub < SUBL - step
        next_value = jnp.where(inside, pltpu.roll(value, SUBL - step, 0), 0.0)
        next_gain = jnp.where(inside, pltpu.roll(gain, SUBL - step, 0), 1.0)
        value = value + gain * next_value
        gain = gain * next_gain
    whole = value + gain * behind
    after = jnp.where(sub < SUBL - 1, pltpu.roll(whole, SUBL - 1, 0), behind)
    return after, whole[:1]


def list_items(blocks_ref, live_ref, items_ref, pieces, own_blocks):
    room = pieces + SUBL
    size = 3 * room + 2
    doubles = [jnp.int32(0), jnp.int32(size)]
    singles = [jnp.int32(2 * room), jnp.int32(size + 2 * room)]
    for piece in range(pieces):
        places = []
        for slot in range(2):
            block = blocks_ref[slot, piece]
            places.append(jnp.where(block == 0, own_blocks + 1, block - 1))
        second = live_ref[0, piece] - 1
        edge = jnp.where(second > 0, jnp.maximum(places[0], places[1]), places[0]) >= own_blocks
        double = jnp.where(edge, doubles[1], doubles[0])
        single = jnp.where(edge, singles[1], singles[0])
        entry = places[0] * 64 + piece
        items_ref[double] = entry
        items_ref[room + double] = places[1] * 64 + piece
        items_ref[single] = entry
        edge_second = jnp.where(edge, second, 0)
        edge_first = jnp.where(edge, 1 - second, 0)
        doubles = [doubles[0] + second - edge_second, doubles[1] + edge_second]
        singles = [singles[0] + 1 - second - edge_first, singles[1] + edge_first]
    counts, sizes = [], []
    for which in range(2):
        for spare in range(6):
            items_ref[singles[which] + spare] = (own_blocks + 2) * 64 + pieces
        counts.append(doubles[which] - which * size)
        sizes.append(counts[which] + (singles[which] - which * size - 2 * room + 1) // 2)
    items_ref[size - 2] = counts[0]
    items_ref[size - 1] = counts[1]
    items_ref[2 * size - 2] = sizes[1]
    items_ref[2 * size - 1] = sizes[0] + sizes[1]


def item_ranges(items_ref, pieces):
    size = 3 * (pieces + SUBL) + 2
    return (items_ref[2 * size - 2] + 1) // 2, (items_ref[2 * size - 1] + 1) // 2


def item_slots(items_ref, item, pieces):
    room = pieces + SUBL
    size = 3 * room + 2
    edges = items_ref[2 * size - 2]
    edge = item < edges
    doubles = jnp.where(edge, items_ref[size - 1], items_ref[size - 2])
    base = jnp.where(edge, size, 0)
    item = jnp.where(edge, item, item - edges)
    chained = item < doubles
    single = base + 2 * (room + item - doubles)
    first = items_ref[jnp.where(chained, base + item, single)]
    second = items_ref[jnp.where(chained, base + room + item, single + 1)]
    found = [chained.astype(jnp.int32)]
    for entry in (first, second):
        found += [entry & 63, lax.shift_right_logical(entry, 6)]
    return tuple(found)


def pipelined(items_ref, pieces, begin, end, multiply, front, back):
    def slots_of(item):
        return item_slots(items_ref, item, pieces)

    first = slots_of(2 * begin)
    front(first, multiply(first), 0)

    def step(pair, carry):
        this, middle, last = carry
        ahead = multiply(middle)
        further = multiply(last)
        back(this, 0)
        front(middle, ahead, 1)
        back(middle, 1)
        front(last, further, 0)
        return last, slots_of(2 * pair + 3), slots_of(2 * pair + 4)

    lax.fori_loop(begin, end, step, (first, slots_of(2 * begin + 1), slots_of(2 * begin + 2)))


def block_rows(block):
    return pl.ds(pl.multiple_of(block * BLOCK, BLOCK), BLOCK)


def exponents(table_ref, basis_ref, piece, block, pieces):
    unit = basis_ref[jnp.minimum(piece, pieces - 1)]
    rhs = jnp.concatenate([unit, jnp.zeros((KC, PIX), bf16)], axis=0)
    return jnp.dot(table_ref[block_rows(block), :], rhs, preferred_element_type=f32)


def fill_tables(rows, present, places, stage_ref, table_ref, colour_ref):
    coefs, colours = splat_rows(rows)
    shape = (SUBL, LANES)
    order = lane_order(shape, False)

    def settled(value, absent):
        if present is not None:
            value = jnp.where(present, value, absent)
        return jnp.take_along_axis(value, order, axis=1)

    coefs = [settled(value, -1e9 if i == 0 else 0.0) for i, value in enumerate(coefs)]
    colours = [settled(value, 0.0) for value in colours]
    nothing = jnp.zeros(shape, f32)
    parts = basis_coefs([split3(value) for value in coefs])
    lines = [parts[row % BASIS][row // BASIS] for row in range(3 * BASIS)]
    lines += [nothing] * (KE - 3 * BASIS)
    triples = [split3(value) for value in colours]
    for level in (0, 0, 1, 0, 0, 1):
        lines += [triple[level] for triple in triples] + [nothing]
    for row, value in enumerate(lines):
        group, place = divmod(row, SUBL)
        stage_ref[pl.ds(group * SUBL * SUBL + place, SUBL, stride=SUBL), :] = value
    for sublane, block in enumerate(places):
        tiles = [
            stage_ref[(group * SUBL + sublane) * SUBL : (group * SUBL + sublane + 1) * SUBL, :]
            for group in range(len(lines) // SUBL)
        ]
        span = slice(block * BLOCK, (block + 1) * BLOCK)
        table_ref[span, :] = jnp.concatenate(tiles[: KT // SUBL], axis=0).T.astype(bf16)
        colour_ref[block] = jnp.concatenate(tiles[KT // SUBL :] * 2, axis=0).astype(bf16)


def render_items(begin, end, items_ref, table_ref, colour_ref, basis_ref, result_ref, scratch):
    local_refs, before_refs, left_refs = scratch
    pieces = basis_ref.shape[0]

    def multiply(found):
        return [
            exponents(table_ref, basis_ref, found[1 + 2 * slot], found[2 + 2 * slot], pieces)
            for slot in range(2)
        ]

    def front(found, powers, side):
        chained = found[0] > 0
        carry = None
        for slot in range(2):
            alphas = jnp.exp2(powers[slot])
            keep = None
            for row in range(ROWS):
                alpha = alphas[row * SUBL : (row + 1) * SUBL]
                weight = alpha if keep is None else alpha * keep
                keep = 1.0 - alpha if keep is None else keep - weight
                first = slot * BLOCK + row * SUBL
                local_refs[side][first : first + SUBL, :] = weight
            before, total = prefix_product(keep)
            if slot == 1:
                carry = jnp.where(chained, carry, 1.0)
                before, total = before * carry, total * carry
            carry = total
            before_refs[side][slot * SUBL : (slot + 1) * SUBL, :] = before
            left_refs[side][slot : slot + 1, :] = total

    def back(found, side):
        chained = found[0] > 0
        sums = None
        for slot in range(2):
            piece, block = found[1 + 2 * slot], found[2 + 2 * slot]
            before = before_refs[side][slot * SUBL : (slot + 1) * SUBL, :]
            weights = []
            for row in range(ROWS):
                first = slot * BLOCK + row * SUBL
                weights.append(local_refs[side][first : first + SUBL, :] * before)
            high, low = split2(jnp.concatenate(weights, axis=0))
            left = colour_ref[block]
            wide = jnp.dot(left, high, preferred_element_type=f32)
            wide = (wide + jnp.dot(left, low, preferred_element_type=f32))[:SUBL]
            wide = wide + pltpu.roll(wide, 4, 0)
            sums = wide + jnp.where(chained, sums, 0.0) if slot else wide
            row_no = lax.broadcasted_iota(jnp.int32, sums.shape, 0)
            value = jnp.where(row_no == 3, 1.0 - left_refs[side][slot : slot + 1, :], sums)
            for half in range(PIX // LANES):
                first = pl.multiple_of((half * (pieces + 1) + piece) * SUBL, SUBL)
                result_ref[pl.ds(first, SUBL), :] = value[:, half * LANES : (half + 1) * LANES]

    pipelined(items_ref, pieces, begin, end, multiply, front, back)


def forward_kernel(
    far_blocks_ref,
    far_live_ref,
    far_params_ref,
    far_basis_ref,
    far_owner_ref,
    far_cell_ref,
    far_target_ref,
    table_ref,
    colour_ref,
    result_ref,
    basis_ref,
    aimed_ref,
    items_ref,
    blocks_ref,
    live_ref,
    params_ref,
    owner_ref,
    cell_ref,
    target_ref,
    arrivals,
    rows_ref,
    stage_ref,
    *scratch,
):
    pieces = basis_ref.shape[0]
    own_blocks = params_ref.shape[1] // BLOCK
    moves = (
        (far_blocks_ref, blocks_ref),
        (far_live_ref, live_ref),
        (far_params_ref, params_ref),
        (far_owner_ref, owner_ref),
        (far_cell_ref, cell_ref),
        (far_target_ref, target_ref),
        (far_basis_ref, basis_ref),
    )
    fetches = [
        pltpu.make_async_copy(far, near, arrivals.at[i]) for i, (far, near) in enumerate(moves)
    ]
    for fetch in fetches:
        fetch.start()
    fetches[0].wait()
    fetches[1].wait()
    list_items(blocks_ref, live_ref, items_ref, pieces, own_blocks)
    fetches[2].wait()
    for block in range(own_blocks):
        rows_ref[pl.ds(block, PARAMS, stride=SUBL), :] = params_ref[
            :, block * BLOCK : (block + 1) * BLOCK
        ]
    rows = [rows_ref[i * SUBL : (i + 1) * SUBL, :] for i in range(PARAMS)]
    fill_tables(rows, None, range(own_blocks), stage_ref, table_ref, colour_ref)
    empty = own_blocks + 2
    column = lax.broadcasted_iota(jnp.int32, (BLOCK, KT), 1)
    table_ref[empty * BLOCK : (empty + 1) * BLOCK, :] = jnp.where(column == 0, -1e9, 0.0).astype(
        bf16
    )
    colour_ref[empty] = jnp.zeros((TOP, LANES), bf16)
    for fetch in fetches[3:]:
        fetch.wait()
    doms = aimed_ref.shape[0]
    width, tiles = PIX // doms, target_ref.shape[1]
    tile_lane = lax.broadcasted_iota(jnp.int32, (SUBL, LANES), 1)
    cell = cell_ref[...]
    labels = (cell % MAXD) * (doms * tiles) + owner_ref[...] * tiles + cell // MAXD
    labels = jnp.concatenate(
        [jnp.zeros((1, LANES - pieces), f32), labels.astype(f32)], axis=1
    )
    labels = jnp.broadcast_to(labels, (SUBL, LANES))
    for dom in range(doms):
        half, offset = divmod(dom * width, LANES)
        span = slice(half * LANES, (half + 1) * LANES)
        aimed = labels
        for channel in (2, 1, 0):
            shift = (channel * GROUP - offset) % LANES
            value = target_ref[channel, :, span]
            value = pltpu.roll(value, shift, 1) if shift else value
            aimed = jnp.where(tile_lane < (channel + 1) * GROUP, value, aimed)
        aimed_ref[dom] = aimed
    edge_pairs, pairs = item_ranges(items_ref, pieces)
    render_items(edge_pairs, pairs, items_ref, table_ref, colour_ref, basis_ref, result_ref, scratch)


def forward_edge_kernel(
    items_ref,
    inner_ref,
    outer_ref,
    aimed_ref,
    basis_ref,
    table_in_ref,
    colour_in_ref,
    result_in_ref,
    table_ref,
    colour_ref,
    result_ref,
    out_ref,
    rows_ref,
    stage_ref,
    *scratch,
):
    del table_in_ref, colour_in_ref, result_in_ref
    doms, pieces = out_ref.shape[0], basis_ref.shape[0]
    own_blocks = table_ref.shape[0] // BLOCK - 3
    region_idx, regions = lax.axis_index("region"), lax.axis_size("region")
    even = region_idx % 2 == 0
    inner, outer = inner_ref[...], outer_ref[...]
    rows_ref[pl.ds(0, PARAMS, stride=SUBL), :] = jnp.where(even, inner, outer)
    rows_ref[pl.ds(1, PARAMS, stride=SUBL), :] = jnp.where(even, outer, inner)
    rows = [rows_ref[i * SUBL : (i + 1) * SUBL, :] for i in range(PARAMS)]
    sublane = lax.broadcasted_iota(jnp.int32, (SUBL, LANES), 0)
    present = ((sublane == 0) & (region_idx < regions - 1)) | ((sublane == 1) & (region_idx > 0))
    places = (own_blocks, own_blocks + 1)
    fill_tables(rows, present, places, stage_ref, table_ref, colour_ref)
    render_items(0, item_ranges(items_ref, pieces)[0], items_ref, table_ref, colour_ref, basis_ref, result_ref, scratch)
    width = PIX // doms
    lane = lax.broadcasted_iota(jnp.int32, (pieces, LANES), 1)
    tiles = aimed_ref.shape[1]
    for dom in range(doms):
        half, offset = divmod(dom * width, LANES)
        packed = None
        for channel in range(4):
            shift = (channel * GROUP - offset) % LANES
            first = half * (pieces + 1) * SUBL + channel
            value = result_ref[pl.ds(first, pieces, stride=SUBL), :]
            value = pltpu.roll(value, shift, 1) if shift else value
            packed = value if packed is None else jnp.where(lane >= channel * GROUP, value, packed)
        out_ref[dom, :pieces, :] = packed
        out_ref[dom, pieces : pieces + tiles, :] = aimed_ref[dom]


def composite_kernel(background_ref, arrived_ref, out_ref):
    doms, pieces = out_ref.shape[0], out_ref.shape[1]
    tiles = arrived_ref.shape[1] - pieces
    all_pieces, all_tiles = doms * pieces, doms * tiles
    per_row = LANES // GROUP
    lane = lax.broadcasted_iota(jnp.int32, (1, LANES), 1)
    label_rows = []
    for dom in range(doms):
        place = dom % per_row
        value = arrived_ref[dom, pieces : pieces + 1, :]
        shift = ((place - 3) * GROUP) % LANES
        value = pltpu.roll(value, shift, 1) if shift else value
        if place == 0:
            label_rows.append(value)
        else:
            label_rows[-1] = jnp.where(lane >= place * GROUP, value, label_rows[-1])
    cells_all = MAXD * all_tiles
    cell_no = lax.broadcasted_iota(jnp.int32, (cells_all, LANES), 0).astype(f32)
    to_cells = jnp.concatenate(
        [jnp.where(cell_no == row, 1.0, 0.0).astype(bf16) for row in label_rows], axis=1
    )
    upright = jnp.concatenate([jnp.broadcast_to(row, (SUBL, LANES)).T for row in label_rows], axis=0)
    cell_no = lax.broadcasted_iota(jnp.int32, (all_pieces, cells_all), 1).astype(f32)
    to_pieces = jnp.where(cell_no == upright[:, :1], 1.0, 0.0).astype(bf16)

    def moved(matrix, values):
        triple = jnp.concatenate([part.astype(bf16) for part in split3(values)], axis=1)
        wide = jnp.dot(matrix, triple, preferred_element_type=f32)
        return wide[:, :LANES] + wide[:, LANES : 2 * LANES] + wide[:, 2 * LANES :]

    data = arrived_ref[:, :pieces, :].reshape(all_pieces, LANES)
    cells = moved(to_cells, data)
    goal = arrived_ref[:, pieces:, :].reshape(all_tiles, LANES)
    lane = lax.broadcasted_iota(jnp.int32, (all_tiles, LANES), 1)
    last = lane >= 3 * GROUP
    backdrop = jnp.where(
        lane < GROUP,
        background_ref[0],
        jnp.where(lane < 2 * GROUP, background_ref[1], background_ref[2]),
    )

    def spread(value):
        return pltpu.roll(value, GROUP, 1) + pltpu.roll(value, 2 * GROUP, 1) + pltpu.roll(
            value, 3 * GROUP, 1
        )

    fronts, through, layers = [], [], []
    front = jnp.ones((all_tiles, LANES), f32)
    composite = jnp.zeros((all_tiles, LANES), f32)
    for depth in range(MAXD):
        layer = cells[depth * all_tiles : (depth + 1) * all_tiles]
        passed = jnp.where(last, 1.0 - layer, 0.0)
        passed = passed + spread(passed)
        fronts.append(front)
        through.append(passed)
        layers.append(layer)
        composite = composite + front * layer
        front = front * passed
    residual = jnp.where(last, 0.0, composite + front * backdrop - goal)
    behind = backdrop
    grads = [None] * MAXD
    for depth in reversed(range(MAXD)):
        grads[depth] = fronts[depth] * jnp.where(last, spread(residual * behind), residual)
        behind = layers[depth] + through[depth] * behind
    back = moved(to_pieces, jnp.concatenate(grads, axis=0))
    out_ref[...] = back.reshape(out_ref.shape)


def pull_items(begin, end, items_ref, table_ref, basis_ref, grad_ref, sums_ref, scratch):
    alpha_refs, shade_refs, local_refs, before_refs, hidden_refs = scratch
    pieces = basis_ref.shape[0]

    def grads_of(piece):
        halves = []
        for half in range(PIX // LANES):
            first = pl.multiple_of((half * (pieces + 1) + piece) * SUBL, SUBL)
            halves.append(grad_ref[pl.ds(first, SUBL), :])
        grads = jnp.concatenate(halves, axis=1)
        upper = lax.broadcasted_iota(jnp.int32, grads.shape, 0) < 4
        high, middle, low = split3(grads)
        first = jnp.where(upper, high, pltpu.roll(middle, 4, 0))
        return grads, first, jnp.where(upper, high, pltpu.roll(low, 4, 0))

    def multiply(found):
        products = []
        for slot in range(2):
            piece, block = found[1 + 2 * slot], found[2 + 2 * slot]
            grads, first, second = grads_of(piece)
            rhs = jnp.concatenate([first, second], axis=0).astype(bf16)
            rhs = jnp.concatenate([jnp.zeros((KE, PIX), bf16), rhs], axis=0)
            shades = jnp.dot(table_ref[block_rows(block), :], rhs, preferred_element_type=f32)
            powers = exponents(table_ref, basis_ref, piece, block, pieces)
            products.append((powers, shades, grads[3:4]))
        return products

    def front(found, products, side):
        chained = found[0] > 0
        carry, ends = None, []
        for slot, (powers, shades, final) in enumerate(products):
            alphas = jnp.exp2(powers)
            span = slice(slot * BLOCK, (slot + 1) * BLOCK)
            alpha_refs[side][span, :] = alphas
            shade_refs[side][span, :] = shades
            keep, total = None, None
            for row in range(ROWS):
                alpha = alphas[row * SUBL : (row + 1) * SUBL]
                weight = alpha if keep is None else alpha * keep
                keep = 1.0 - alpha if keep is None else keep - weight
                value = weight * shades[row * SUBL : (row + 1) * SUBL]
                total = value if total is None else total + value
                first = slot * BLOCK + row * SUBL
                local_refs[side][first : first + SUBL, :] = weight
            before, whole = prefix_product(keep)
            if slot == 1:
                before = before * jnp.where(chained, carry, 1.0)
            carry = whole
            before_refs[side][slot * SUBL : (slot + 1) * SUBL, :] = before
            ends.append((total, keep, final))
        behind = None
        for slot in (1, 0):
            total, keep, final = ends[slot]
            behind = jnp.where(chained, behind, final) if slot == 0 else final
            hidden, behind = suffix_affine(total, keep, behind)
            hidden_refs[side][slot * SUBL : (slot + 1) * SUBL, :] = hidden

    def back(found, side):
        along = (((1,), (1,)), ((), ()))
        for slot in range(2):
            piece, block = found[1 + 2 * slot], found[2 + 2 * slot]
            before = before_refs[side][slot * SUBL : (slot + 1) * SUBL, :]
            hidden = hidden_refs[side][slot * SUBL : (slot + 1) * SUBL, :]
            pulls, weights = [None] * ROWS, [None] * ROWS
            for row in reversed(range(ROWS)):
                first = slot * BLOCK + row * SUBL
                span = slice(first, first + SUBL)
                weight = local_refs[side][span, :] * before
                gap = shade_refs[side][span, :] - hidden
                weights[row] = weight
                pulls[row] = weight * gap
                hidden = hidden + alpha_refs[side][span, :] * gap
            unit = basis_ref[jnp.minimum(piece, pieces - 1)][:TOP]
            _, first, second = grads_of(piece)
            g_lhs = jnp.concatenate([first, second], axis=0).astype(bf16)
            for base, left, values in ((0, unit, pulls), (2, g_lhs, weights)):
                part = None
                for value in split2(jnp.concatenate(values, axis=0)):
                    product = lax.dot_general(left, value, along, preferred_element_type=f32)
                    part = product if part is None else part + product
                for group in range(2 if base == 0 else 1):
                    row = (base + group) * SLOTS * SUBL + block * SUBL
                    rows = pl.ds(pl.multiple_of(row, SUBL), SUBL)
                    sums_ref[rows, :] = (
                        sums_ref[rows, :] + part[group * SUBL : (group + 1) * SUBL]
                    )

    pipelined(items_ref, pieces, begin, end, multiply, front, back)


def early_pairs(items_ref, pieces):
    edge_pairs, pairs = item_ranges(items_ref, pieces)
    return jnp.minimum(jnp.maximum(edge_pairs, pieces * 3 // 16), pairs), pairs


def summed_terms(sums_ref):
    def rows_of(row):
        group, place = divmod(row, SUBL)
        return sums_ref[pl.ds(group * SLOTS * SUBL + place, SLOTS, stride=SUBL), :]

    moments = [rows_of(0), rows_of(1), rows_of(2)]
    moments += [rows_of(3 + 2 * i) + rows_of(4 + 2 * i) for i in range(3)]
    terms = [value * ln_2 for value in moments]
    terms += [rows_of(TOP + i) + rows_of(TOP + 4 + i) for i in range(3)]
    order = lane_order((SLOTS, LANES), True)
    return [jnp.take_along_axis(value, order, axis=1) for value in terms]


def backward_edge_kernel(
    items_ref,
    back_ref,
    table_ref,
    basis_ref,
    grad_ref,
    sums_ref,
    inner_ref,
    outer_ref,
    *scratch,
):
    doms, pieces = back_ref.shape[0], back_ref.shape[1]
    own_blocks = table_ref.shape[0] // BLOCK - 3
    width = PIX // doms
    lane = lax.broadcasted_iota(jnp.int32, (pieces, LANES), 1)
    grad_ref[...] = jnp.zeros_like(grad_ref)
    sums_ref[...] = jnp.zeros_like(sums_ref)
    for half in range(PIX // LANES):
        for channel in range(4):
            gathered = None
            for dom in range(half * LANES // width, (half + 1) * LANES // width):
                offset = dom * width - half * LANES
                shift = (offset - channel * GROUP) % LANES
                value = back_ref[dom]
                value = pltpu.roll(value, shift, 1) if shift else value
                gathered = value if gathered is None else jnp.where(lane >= offset, value, gathered)
            first = half * (pieces + 1) * SUBL + channel
            grad_ref[pl.ds(first, pieces, stride=SUBL), :] = gathered

    early, _ = early_pairs(items_ref, pieces)
    pull_items(0, early, items_ref, table_ref, basis_ref, grad_ref, sums_ref, scratch)
    even = lax.axis_index("region") % 2 == 0
    inner_ref[...] = jnp.zeros_like(inner_ref)
    outer_ref[...] = jnp.zeros_like(outer_ref)
    for term_no, value in enumerate(summed_terms(sums_ref)):
        high = value[own_blocks : own_blocks + 1]
        low = value[own_blocks + 1 : own_blocks + 2]
        inner_ref[term_no : term_no + 1, :] = jnp.where(even, high, low)
        outer_ref[term_no : term_no + 1, :] = jnp.where(even, low, high)


def backward_kernel(
    items_ref, table_ref, basis_ref, grad_ref, edge_sums_ref, own_ref, sums_ref, *scratch
):
    sums_ref[...] = edge_sums_ref[...]
    early, pairs = early_pairs(items_ref, basis_ref.shape[0])
    pull_items(early, pairs, items_ref, table_ref, basis_ref, grad_ref, sums_ref, scratch)
    for term_no, value in enumerate(summed_terms(sums_ref)):
        own_ref[term_no] = value[: own_ref.shape[1]]


def update_kernel(
    params_ref,
    first_ref,
    second_ref,
    own_ref,
    inner_ref,
    outer_ref,
    gradient_ref,
    new_params_ref,
    new_first_ref,
    new_second_ref,
    rows_ref,
    grads_ref,
):
    own_blocks = own_ref.shape[1]
    for block in range(own_blocks):
        rows_ref[pl.ds(block, PARAMS, stride=own_blocks), :] = params_ref[
            :, block * BLOCK : (block + 1) * BLOCK
        ]
    rows = [rows_ref[i * own_blocks : (i + 1) * own_blocks, :] for i in range(PARAMS)]
    slot = lax.broadcasted_iota(jnp.int32, (own_blocks, LANES), 0)
    even = lax.axis_index("region") % 2 == 0
    from_low = jnp.where(even, outer_ref[...], inner_ref[...])
    from_high = jnp.where(even, inner_ref[...], outer_ref[...])
    cots = []
    for term_no in range(9):
        low = jnp.where(slot == 0, from_low[term_no : term_no + 1, :], 0.0)
        high = jnp.where(slot == own_blocks - 1, from_high[term_no : term_no + 1, :], 0.0)
        cots.append(own_ref[term_no] + low + high)
    _, pull_back = jax.vjp(splat_rows, rows)
    pulled = pull_back((cots[:6], cots[6:]))[0]
    for i in range(PARAMS):
        grads_ref[i * own_blocks : (i + 1) * own_blocks, :] = pulled[i]
    for block in range(own_blocks):
        span = slice(block * BLOCK, (block + 1) * BLOCK)
        gradient = grads_ref[pl.ds(block, PARAMS, stride=own_blocks), :]
        new_first = beta_one * first_ref[:, span] + (1 - beta_one) * gradient
        new_second = beta_two * second_ref[:, span] + (1 - beta_two) * gradient * gradient
        update = (
            new_first
            / (1 - beta_one**adam_step)
            / (jnp.sqrt(new_second / (1 - beta_two**adam_step)) + tiny)
        )
        gradient_ref[:, span] = gradient
        new_params_ref[:, span] = params_ref[:, span] - rate * update
        new_first_ref[:, span] = new_first
        new_second_ref[:, span] = new_second


def exchange(to_inner, to_outer):
    count = lax.axis_size("region")
    inner = [(i, i ^ 1) for i in range(count) if (i ^ 1) < count]
    outer = [(i, i + 1) for i in range(1, count - 1, 2)]
    outer += [(target, source) for source, target in outer]
    far = lax.ppermute(to_outer, "region", outer)
    return lax.ppermute(to_inner, "region", inner), far


def on_device(
    params,
    first_moment,
    second_moment,
    piece_blocks,
    piece_live,
    piece_owner,
    piece_cell,
    target,
    background,
):
    own_blocks = params.shape[1] // BLOCK
    doms = lax.axis_size("dom")
    pieces = piece_live.shape[1]
    tiles = target.shape[1]
    even = lax.axis_index("region") % 2 == 0
    low, high = params[:, :BLOCK], params[:, -BLOCK:]
    inner, outer = exchange(jnp.where(even, high, low), jnp.where(even, low, high))
    basis = jnp.asarray(pixel_basis(pieces))
    smem = pl.BlockSpec(memory_space=pltpu.SMEM)
    vmem = pl.BlockSpec(memory_space=pltpu.VMEM)
    plane = pltpu.VMEM((2 * BLOCK, PIX), f32)
    strip = pltpu.VMEM((2 * SUBL, PIX), f32)
    piece_rows = (PIX // LANES * (pieces + 1) * SUBL, LANES)
    sums_shape = (3 * SLOTS * SUBL, LANES)
    table_shape = jax.ShapeDtypeStruct(((own_blocks + 3) * BLOCK, KT), bf16)
    colour_shape = jax.ShapeDtypeStruct((own_blocks + 3, TOP, LANES), bf16)
    result_shape = jax.ShapeDtypeStruct(piece_rows, f32)
    forward_scratch = [
        pltpu.VMEM((64 * SUBL, LANES), f32),
        pltpu.VMEM(((KT // SUBL + 1) * SUBL * SUBL, LANES), f32),
        [plane] * 2,
        [strip] * 2,
        [strip] * 2,
    ]
    backward_scratch = [[plane] * 2, [plane] * 2, [plane] * 2, [strip] * 2, [strip] * 2]
    params_limit = pltpu.CompilerParams(vmem_limit_bytes=vmem_limit)
    table, colour, result, basis, aimed, items = pl.pallas_call(
        forward_kernel,
        out_shape=(
            table_shape,
            colour_shape,
            result_shape,
            jax.ShapeDtypeStruct(basis.shape, bf16),
            jax.ShapeDtypeStruct((doms, tiles, LANES), f32),
            jax.ShapeDtypeStruct((2 * (3 * (pieces + SUBL) + 2),), jnp.int32),
        ),
        in_specs=[pl.BlockSpec(memory_space=pltpu.HBM)] * 7,
        out_specs=(vmem,) * 5 + (smem,),
        scratch_shapes=[
            pltpu.SMEM((2, pieces), jnp.int32),
            pltpu.SMEM((1, pieces), jnp.int32),
            pltpu.VMEM(params.shape, f32),
            pltpu.VMEM((1, pieces), jnp.int32),
            pltpu.VMEM((1, pieces), jnp.int32),
            pltpu.VMEM((3, tiles, PIX), f32),
            pltpu.SemaphoreType.DMA((7,)),
        ]
        + forward_scratch,
        compiler_params=params_limit,
        name="forward",
    )(
        *[
            pltpu.with_memory_space_constraint(value, pltpu.HBM)
            for value in (
                piece_blocks[0].T,
                piece_live,
                params,
                basis,
                piece_owner,
                piece_cell,
                jnp.transpose(target[0], (1, 0, 2)),
            )
        ]
    )
    table, _, _, payload = pl.pallas_call(
        forward_edge_kernel,
        out_shape=(
            table_shape,
            colour_shape,
            result_shape,
            jax.ShapeDtypeStruct((doms, pieces + tiles, LANES), f32),
        ),
        in_specs=[smem] + [vmem] * 7,
        out_specs=(vmem,) * 4,
        scratch_shapes=forward_scratch,
        input_output_aliases={5: 0, 6: 1, 7: 2},
        compiler_params=params_limit,
        name="forward_edge",
    )(
        items,
        inner,
        outer,
        aimed,
        basis,
        table,
        colour,
        result,
    )
    arrived = lax.all_to_all(payload, "dom", split_axis=0, concat_axis=0, tiled=True)
    back = pl.pallas_call(
        composite_kernel,
        out_shape=jax.ShapeDtypeStruct((doms, pieces, LANES), f32),
        in_specs=[smem, vmem],
        out_specs=vmem,
        compiler_params=params_limit,
        name="composite",
    )(background, arrived)
    returned = lax.all_to_all(back, "dom", split_axis=0, concat_axis=0, tiled=True)
    grads, edge_sums, to_inner, to_outer = pl.pallas_call(
        backward_edge_kernel,
        out_shape=(
            result_shape,
            jax.ShapeDtypeStruct(sums_shape, f32),
            jax.ShapeDtypeStruct((SLOTS, LANES), f32),
            jax.ShapeDtypeStruct((SLOTS, LANES), f32),
        ),
        in_specs=[smem] + [vmem] * 3,
        out_specs=(vmem,) * 4,
        scratch_shapes=backward_scratch,
        compiler_params=params_limit,
        name="backward_edge",
    )(items, returned, table, basis)
    inner, outer = exchange(to_inner, to_outer)
    own = pl.pallas_call(
        backward_kernel,
        out_shape=jax.ShapeDtypeStruct((9, own_blocks, LANES), f32),
        in_specs=[smem] + [vmem] * 4,
        out_specs=vmem,
        scratch_shapes=[pltpu.VMEM(sums_shape, f32)] + backward_scratch,
        compiler_params=params_limit,
        name="backward",
    )(items, table, basis, grads, edge_sums)
    shape = jax.ShapeDtypeStruct(params.shape, f32)
    return pl.pallas_call(
        update_kernel,
        out_shape=(shape, shape, shape, shape),
        in_specs=[vmem] * 6,
        out_specs=(vmem,) * 4,
        scratch_shapes=[
            pltpu.VMEM((64 * own_blocks, LANES), f32),
            pltpu.VMEM((64 * own_blocks, LANES), f32),
        ],
        name="update",
        compiler_params=pltpu.CompilerParams(vmem_limit_bytes=vmem_limit),
    )(params, first_moment, second_moment, own, inner, outer)


def solution(mesh):
    in_specs = (
        P(None, ("region", "dom")),
        P(None, ("region", "dom")),
        P(None, ("region", "dom")),
        P(("region", "dom"), None, None),
        P(("region", "dom"), None),
        P(("region", "dom"), None),
        P(("region", "dom"), None),
        P(("region", "dom"), None, None, None),
        P(),
    )
    out_specs = (P(None, ("region", "dom")),) * 4
    return jax.shard_map(
        on_device, mesh=mesh, in_specs=in_specs, out_specs=out_specs, check_vma=False
    )
```

```python
import math

import numpy as np
import jax
import jax.numpy as jnp
from jax import lax
from jax.experimental import pallas as pl
from jax.experimental.pallas import tpu as pltpu
from jax.sharding import PartitionSpec as P

PARAMS = 59
TSIDE = 16
WIN = 8
BLOCK = 128
MAXD = 8
PIX = 256

harmonic_zero = 0.28209479177387814
harmonic_one = 0.4886025119029199
harmonic_two = (
    1.0925484305920792,
    -1.0925484305920792,
    0.31539156525252005,
    -1.0925484305920792,
    0.5462742152960396,
)
harmonic_three = (
    -0.5900435899266435,
    2.890611442640554,
    -0.4570457994644658,
    0.3731763325901154,
    -0.4570457994644658,
    1.445305721320277,
    -0.5900435899266435,
)
beta_one = 0.9
beta_two = 0.999
rate = 0.001
adam_step = 100
tiny = 1e-08
log2_e = math.log2(math.e)
ln_2 = math.log(2.0)

LANES = 128
SUBL = 8
ROWS = BLOCK // SUBL
GROUP = LANES // 4
BASIS = 9
KE = 32
KC = 2 * SUBL
KT = KE + KC
TOP = 16
SLOTS = 16
vmem_limit = 12 * 2**20
f32 = jnp.float32
bf16 = jnp.bfloat16


def splat_rows(rows):
    mean_x, mean_y, mean_z = rows[0], rows[1], rows[2]
    scales = [jnp.exp(rows[3]), jnp.exp(rows[4]), jnp.exp(rows[5])]
    norm_sq = rows[6] * rows[6] + rows[7] * rows[7] + rows[8] * rows[8] + rows[9] * rows[9]
    inv_norm = 1.0 / jnp.sqrt(norm_sq)
    quat_w, quat_x, quat_y, quat_z = [rows[6 + i] * inv_norm for i in range(4)]
    rotation = [
        [
            1 - 2 * (quat_y * quat_y + quat_z * quat_z),
            2 * (quat_x * quat_y - quat_w * quat_z),
            2 * (quat_x * quat_z + quat_w * quat_y),
        ],
        [
            2 * (quat_x * quat_y + quat_w * quat_z),
            1 - 2 * (quat_x * quat_x + quat_z * quat_z),
            2 * (quat_y * quat_z - quat_w * quat_x),
        ],
        [
            2 * (quat_x * quat_z - quat_w * quat_y),
            2 * (quat_y * quat_z + quat_w * quat_x),
            1 - 2 * (quat_x * quat_x + quat_y * quat_y),
        ],
    ]
    focal_px = 0.3125 * float(WIN * TSIDE)
    inv_z = 1.0 / mean_z
    scale_z = focal_px * inv_z
    off_u = scale_z * mean_x
    off_v = scale_z * mean_y
    slope_u = off_u * inv_z
    slope_v = off_v * inv_z
    proj_u = [(scale_z * rotation[0][i] - slope_u * rotation[2][i]) * scales[i] for i in range(3)]
    proj_v = [(scale_z * rotation[1][i] - slope_v * rotation[2][i]) * scales[i] for i in range(3)]
    sigma_xx = proj_u[0] * proj_u[0] + proj_u[1] * proj_u[1] + proj_u[2] * proj_u[2] + 0.3
    sigma_xy = proj_u[0] * proj_v[0] + proj_u[1] * proj_v[1] + proj_u[2] * proj_v[2]
    sigma_yy = proj_v[0] * proj_v[0] + proj_v[1] * proj_v[1] + proj_v[2] * proj_v[2] + 0.3
    determinant = sigma_xx * sigma_yy - sigma_xy * sigma_xy
    inv_det = log2_e / determinant
    con_xx = sigma_yy * inv_det
    con_xy = -sigma_xy * inv_det
    con_yy = sigma_xx * inv_det
    lin_x = con_xx * off_u + con_xy * off_v
    lin_y = con_xy * off_u + con_yy * off_v
    logit = rows[10]
    log_opacity = (logit - jnp.log(1.0 + jnp.exp(logit))) * log2_e
    const = log_opacity - 0.5 * (lin_x * off_u + lin_y * off_v)
    coefs = [const, lin_x, lin_y, -0.5 * con_xx, -con_xy, -0.5 * con_yy]
    inv_len = 1.0 / jnp.sqrt(mean_x * mean_x + mean_y * mean_y + mean_z * mean_z)
    dir_x, dir_y, dir_z = mean_x * inv_len, mean_y * inv_len, mean_z * inv_len
    sq_x, sq_y, sq_z = dir_x * dir_x, dir_y * dir_y, dir_z * dir_z
    harmonics = [
        None,
        -harmonic_one * dir_y,
        harmonic_one * dir_z,
        -harmonic_one * dir_x,
        harmonic_two[0] * dir_x * dir_y,
        harmonic_two[1] * dir_y * dir_z,
        harmonic_two[2] * (2 * sq_z - sq_x - sq_y),
        harmonic_two[3] * dir_x * dir_z,
        harmonic_two[4] * (sq_x - sq_y),
        harmonic_three[0] * dir_y * (3 * sq_x - sq_y),
        harmonic_three[1] * dir_x * dir_y * dir_z,
        harmonic_three[2] * dir_y * (4 * sq_z - sq_x - sq_y),
        harmonic_three[3] * dir_z * (2 * sq_z - 3 * sq_x - 3 * sq_y),
        harmonic_three[4] * dir_x * (4 * sq_z - sq_x - sq_y),
        harmonic_three[5] * dir_z * (sq_x - sq_y),
        harmonic_three[6] * dir_x * (sq_x - 3 * sq_y),
    ]
    colours = []
    for colour_no in range(3):
        base = 11 + 16 * colour_no
        total = rows[base] * harmonic_zero
        for k in range(1, 16):
            total = total + rows[base + k] * harmonics[k]
        colours.append(jnp.maximum(total + 0.5, 0.0))
    return coefs, colours


def split3(value):
    high = value.astype(bf16).astype(f32)
    rest = value - high
    middle = rest.astype(bf16).astype(f32)
    return high, middle, rest - middle


def split2(value):
    high = value.astype(bf16)
    return high, (value - high.astype(f32)).astype(bf16)


def pixel_basis(pieces):
    tiles = np.arange(pieces)[:, None]
    pixels = np.arange(PIX)[None, :]
    half = WIN * TSIDE / 2
    pos_x = TSIDE * (tiles % WIN) + pixels % TSIDE + 0.5 - half
    pos_y = TSIDE * (tiles // WIN) + pixels // TSIDE + 0.5 - half
    rows = [np.ones_like(pos_x), pos_x, pos_y]
    for product in (pos_x * pos_x, pos_x * pos_y, pos_y * pos_y):
        high = product.astype(bf16).astype(np.float64)
        rows += [high, product - high]
    table = np.zeros((pieces, KE, PIX))
    for row_no, row in enumerate(rows * 3):
        table[:, row_no] = row
    return table.astype(bf16)


def basis_coefs(coefs):
    return [coefs[i] for i in (0, 1, 2, 3, 3, 4, 4, 5, 5)]


def lane_order(shape, inverse):
    lane = lax.broadcasted_iota(jnp.int32, shape, 1)
    if inverse:
        return (lane % ROWS) * SUBL + lane // ROWS
    return (lane % SUBL) * ROWS + lane // SUBL


def prefix_product(total):
    sub = lax.broadcasted_iota(jnp.int32, total.shape, 0)
    run = total
    for step in (1, 2, 4):
        run = jnp.where(sub >= step, run * pltpu.roll(run, step, 0), run)
    before = jnp.where(sub >= 1, pltpu.roll(run, 1, 0), 1.0)
    return before, run[SUBL - 1 :]


def suffix_affine(total, keep, behind):
    sub = lax.broadcasted_iota(jnp.int32, total.shape, 0)
    value, gain = total, keep
    for step in (1, 2, 4):
        inside = sub < SUBL - step
        next_value = jnp.where(inside, pltpu.roll(value, SUBL - step, 0), 0.0)
        next_gain = jnp.where(inside, pltpu.roll(gain, SUBL - step, 0), 1.0)
        value = value + gain * next_value
        gain = gain * next_gain
    whole = value + gain * behind
    after = jnp.where(sub < SUBL - 1, pltpu.roll(whole, SUBL - 1, 0), behind)
    return after, whole[:1]


def list_items(blocks_ref, live_ref, items_ref, pieces, own_blocks):
    room = pieces + SUBL
    size = 3 * room + 2
    doubles = [jnp.int32(0), jnp.int32(size)]
    singles = [jnp.int32(2 * room), jnp.int32(size + 2 * room)]
    for piece in range(pieces):
        places = []
        for slot in range(2):
            block = blocks_ref[slot, piece]
            places.append(jnp.where(block == 0, own_blocks + 1, block - 1))
        second = live_ref[0, piece] - 1
        edge = jnp.where(second > 0, jnp.maximum(places[0], places[1]), places[0]) >= own_blocks
        double = jnp.where(edge, doubles[1], doubles[0])
        single = jnp.where(edge, singles[1], singles[0])
        entry = places[0] * 64 + piece
        items_ref[double] = entry
        items_ref[room + double] = places[1] * 64 + piece
        items_ref[single] = entry
        edge_second = jnp.where(edge, second, 0)
        edge_first = jnp.where(edge, 1 - second, 0)
        doubles = [doubles[0] + second - edge_second, doubles[1] + edge_second]
        singles = [singles[0] + 1 - second - edge_first, singles[1] + edge_first]
    counts, sizes = [], []
    for which in range(2):
        for spare in range(6):
            items_ref[singles[which] + spare] = (own_blocks + 2) * 64 + pieces
        counts.append(doubles[which] - which * size)
        sizes.append(counts[which] + (singles[which] - which * size - 2 * room + 1) // 2)
    items_ref[size - 2] = counts[0]
    items_ref[size - 1] = counts[1]
    items_ref[2 * size - 2] = sizes[1]
    items_ref[2 * size - 1] = sizes[0] + sizes[1]


def item_ranges(items_ref, pieces):
    size = 3 * (pieces + SUBL) + 2
    return (items_ref[2 * size - 2] + 1) // 2, (items_ref[2 * size - 1] + 1) // 2


def item_slots(items_ref, item, pieces):
    room = pieces + SUBL
    size = 3 * room + 2
    edges = items_ref[2 * size - 2]
    edge = item < edges
    doubles = jnp.where(edge, items_ref[size - 1], items_ref[size - 2])
    base = jnp.where(edge, size, 0)
    item = jnp.where(edge, item, item - edges)
    chained = item < doubles
    single = base + 2 * (room + item - doubles)
    first = items_ref[jnp.where(chained, base + item, single)]
    second = items_ref[jnp.where(chained, base + room + item, single + 1)]
    found = [chained.astype(jnp.int32)]
    for entry in (first, second):
        found += [entry & 63, lax.shift_right_logical(entry, 6)]
    return tuple(found)


def pipelined(items_ref, pieces, begin, end, multiply, front, back):
    def slots_of(item):
        return item_slots(items_ref, item, pieces)

    first = slots_of(2 * begin)
    front(first, multiply(first), 0)

    def step(pair, carry):
        this, middle, last = carry
        ahead = multiply(middle)
        further = multiply(last)
        back(this, 0)
        front(middle, ahead, 1)
        back(middle, 1)
        front(last, further, 0)
        return last, slots_of(2 * pair + 3), slots_of(2 * pair + 4)

    def two_steps(double, carry):
        pair = begin + 2 * double
        return step(pair + 1, step(pair, carry))

    doubles = (end - begin) // 2
    carry = (first, slots_of(2 * begin + 1), slots_of(2 * begin + 2))
    carry = lax.fori_loop(0, doubles, two_steps, carry)
    lax.fori_loop(begin + 2 * doubles, end, step, carry)


def block_rows(block):
    return pl.ds(pl.multiple_of(block * BLOCK, BLOCK), BLOCK)


def exponents(table_ref, basis_ref, piece, block, pieces):
    unit = basis_ref[jnp.minimum(piece, pieces - 1)]
    rhs = jnp.concatenate([unit, jnp.zeros((KC, PIX), bf16)], axis=0)
    return jnp.dot(table_ref[block_rows(block), :], rhs, preferred_element_type=f32)


def fill_tables(rows, present, places, stage_ref, table_ref, colour_ref):
    coefs, colours = splat_rows(rows)
    shape = (SUBL, LANES)
    order = lane_order(shape, False)

    def settled(value, absent):
        if present is not None:
            value = jnp.where(present, value, absent)
        return jnp.take_along_axis(value, order, axis=1)

    coefs = [settled(value, -1e9 if i == 0 else 0.0) for i, value in enumerate(coefs)]
    colours = [settled(value, 0.0) for value in colours]
    nothing = jnp.zeros(shape, f32)
    parts = basis_coefs([split3(value) for value in coefs])
    lines = [parts[row % BASIS][row // BASIS] for row in range(3 * BASIS)]
    lines += [nothing] * (KE - 3 * BASIS)
    triples = [split3(value) for value in colours]
    for level in (0, 0, 1, 0, 0, 1):
        lines += [triple[level] for triple in triples] + [nothing]
    for row, value in enumerate(lines):
        group, place = divmod(row, SUBL)
        stage_ref[pl.ds(group * SUBL * SUBL + place, SUBL, stride=SUBL), :] = value
    for sublane, block in enumerate(places):
        tiles = [
            stage_ref[(group * SUBL + sublane) * SUBL : (group * SUBL + sublane + 1) * SUBL, :]
            for group in range(len(lines) // SUBL)
        ]
        span = slice(block * BLOCK, (block + 1) * BLOCK)
        table_ref[span, :] = jnp.concatenate(tiles[: KT // SUBL], axis=0).T.astype(bf16)
        colour_ref[block] = jnp.concatenate(tiles[KT // SUBL :] * 2, axis=0).astype(bf16)


def render_items(begin, end, items_ref, table_ref, colour_ref, basis_ref, result_ref, scratch):
    local_refs, before_refs, left_refs = scratch
    pieces = basis_ref.shape[0]

    def multiply(found):
        return [
            exponents(table_ref, basis_ref, found[1 + 2 * slot], found[2 + 2 * slot], pieces)
            for slot in range(2)
        ]

    def front(found, powers, side):
        chained = found[0] > 0
        carry = None
        for slot in range(2):
            alphas = jnp.exp2(powers[slot])
            keep = None
            for row in range(ROWS):
                alpha = alphas[row * SUBL : (row + 1) * SUBL]
                weight = alpha if keep is None else alpha * keep
                keep = 1.0 - alpha if keep is None else keep - weight
                first = slot * BLOCK + row * SUBL
                local_refs[side][first : first + SUBL, :] = weight
            before, total = prefix_product(keep)
            if slot == 1:
                carry = jnp.where(chained, carry, 1.0)
                before, total = before * carry, total * carry
            carry = total
            before_refs[side][slot * SUBL : (slot + 1) * SUBL, :] = before
            left_refs[side][slot : slot + 1, :] = total

    def back(found, side):
        chained = found[0] > 0
        sums = None
        for slot in range(2):
            piece, block = found[1 + 2 * slot], found[2 + 2 * slot]
            before = before_refs[side][slot * SUBL : (slot + 1) * SUBL, :]
            weights = []
            for row in range(ROWS):
                first = slot * BLOCK + row * SUBL
                weights.append(local_refs[side][first : first + SUBL, :] * before)
            high, low = split2(jnp.concatenate(weights, axis=0))
            left = colour_ref[block]
            wide = jnp.dot(left, high, preferred_element_type=f32)
            wide = (wide + jnp.dot(left, low, preferred_element_type=f32))[:SUBL]
            wide = wide + pltpu.roll(wide, 4, 0)
            sums = wide + jnp.where(chained, sums, 0.0) if slot else wide
            row_no = lax.broadcasted_iota(jnp.int32, sums.shape, 0)
            value = jnp.where(row_no == 3, 1.0 - left_refs[side][slot : slot + 1, :], sums)
            for half in range(PIX // LANES):
                first = pl.multiple_of((half * (pieces + 1) + piece) * SUBL, SUBL)
                result_ref[pl.ds(first, SUBL), :] = value[:, half * LANES : (half + 1) * LANES]

    pipelined(items_ref, pieces, begin, end, multiply, front, back)


def forward_kernel(
    far_blocks_ref,
    far_live_ref,
    far_params_ref,
    far_basis_ref,
    far_owner_ref,
    far_cell_ref,
    far_target_ref,
    table_ref,
    colour_ref,
    result_ref,
    basis_ref,
    aimed_ref,
    items_ref,
    blocks_ref,
    live_ref,
    params_ref,
    owner_ref,
    cell_ref,
    target_ref,
    arrivals,
    rows_ref,
    stage_ref,
    *scratch,
):
    pieces = basis_ref.shape[0]
    own_blocks = params_ref.shape[1] // BLOCK
    moves = (
        (far_blocks_ref, blocks_ref),
        (far_live_ref, live_ref),
        (far_params_ref, params_ref),
        (far_owner_ref, owner_ref),
        (far_cell_ref, cell_ref),
        (far_target_ref, target_ref),
        (far_basis_ref, basis_ref),
    )
    fetches = [
        pltpu.make_async_copy(far, near, arrivals.at[i]) for i, (far, near) in enumerate(moves)
    ]
    for fetch in fetches:
        fetch.start()
    for fetch in fetches[:3]:
        fetch.wait()
    list_items(blocks_ref, live_ref, items_ref, pieces, own_blocks)
    for block in range(own_blocks):
        rows_ref[pl.ds(block, PARAMS, stride=SUBL), :] = params_ref[
            :, block * BLOCK : (block + 1) * BLOCK
        ]
    rows = [rows_ref[i * SUBL : (i + 1) * SUBL, :] for i in range(PARAMS)]
    fill_tables(rows, None, range(own_blocks), stage_ref, table_ref, colour_ref)
    empty = own_blocks + 2
    column = lax.broadcasted_iota(jnp.int32, (BLOCK, KT), 1)
    table_ref[empty * BLOCK : (empty + 1) * BLOCK, :] = jnp.where(column == 0, -1e9, 0.0).astype(
        bf16
    )
    colour_ref[empty] = jnp.zeros((TOP, LANES), bf16)
    for fetch in fetches[3:]:
        fetch.wait()
    doms = aimed_ref.shape[0]
    width, tiles = PIX // doms, target_ref.shape[1]
    tile_lane = lax.broadcasted_iota(jnp.int32, (SUBL, LANES), 1)
    cell = cell_ref[...]
    labels = (cell % MAXD) * (doms * tiles) + owner_ref[...] * tiles + cell // MAXD
    labels = jnp.concatenate(
        [jnp.zeros((1, LANES - pieces), f32), labels.astype(f32)], axis=1
    )
    labels = jnp.broadcast_to(labels, (SUBL, LANES))
    for dom in range(doms):
        half, offset = divmod(dom * width, LANES)
        span = slice(half * LANES, (half + 1) * LANES)
        aimed = labels
        for channel in (2, 1, 0):
            shift = (channel * GROUP - offset) % LANES
            value = target_ref[channel, :, span]
            value = pltpu.roll(value, shift, 1) if shift else value
            aimed = jnp.where(tile_lane < (channel + 1) * GROUP, value, aimed)
        aimed_ref[dom] = aimed
    edge_pairs, pairs = item_ranges(items_ref, pieces)
    render_items(edge_pairs, pairs, items_ref, table_ref, colour_ref, basis_ref, result_ref, scratch)


def forward_edge_kernel(
    items_ref,
    inner_ref,
    outer_ref,
    aimed_ref,
    basis_ref,
    table_in_ref,
    colour_in_ref,
    result_in_ref,
    table_ref,
    colour_ref,
    result_ref,
    out_ref,
    rows_ref,
    stage_ref,
    *scratch,
):
    del table_in_ref, colour_in_ref, result_in_ref
    doms, pieces = out_ref.shape[0], basis_ref.shape[0]
    own_blocks = table_ref.shape[0] // BLOCK - 3
    region_idx, regions = lax.axis_index("region"), lax.axis_size("region")
    even = region_idx % 2 == 0
    inner, outer = inner_ref[...], outer_ref[...]
    rows_ref[pl.ds(0, PARAMS, stride=SUBL), :] = jnp.where(even, inner, outer)
    rows_ref[pl.ds(1, PARAMS, stride=SUBL), :] = jnp.where(even, outer, inner)
    rows = [rows_ref[i * SUBL : (i + 1) * SUBL, :] for i in range(PARAMS)]
    sublane = lax.broadcasted_iota(jnp.int32, (SUBL, LANES), 0)
    present = ((sublane == 0) & (region_idx < regions - 1)) | ((sublane == 1) & (region_idx > 0))
    places = (own_blocks, own_blocks + 1)
    fill_tables(rows, present, places, stage_ref, table_ref, colour_ref)
    render_items(0, item_ranges(items_ref, pieces)[0], items_ref, table_ref, colour_ref, basis_ref, result_ref, scratch)
    width = PIX // doms
    lane = lax.broadcasted_iota(jnp.int32, (pieces, LANES), 1)
    tiles = aimed_ref.shape[1]
    for dom in range(doms):
        half, offset = divmod(dom * width, LANES)
        packed = None
        for channel in range(4):
            shift = (channel * GROUP - offset) % LANES
            first = half * (pieces + 1) * SUBL + channel
            value = result_ref[pl.ds(first, pieces, stride=SUBL), :]
            value = pltpu.roll(value, shift, 1) if shift else value
            packed = value if packed is None else jnp.where(lane >= channel * GROUP, value, packed)
        out_ref[dom, :pieces, :] = packed
        out_ref[dom, pieces : pieces + tiles, :] = aimed_ref[dom]


def composite_kernel(background_ref, arrived_ref, out_ref):
    doms, pieces = out_ref.shape[0], out_ref.shape[1]
    tiles = arrived_ref.shape[1] - pieces
    all_pieces, all_tiles = doms * pieces, doms * tiles
    per_row = LANES // GROUP
    lane = lax.broadcasted_iota(jnp.int32, (1, LANES), 1)
    label_rows = []
    for dom in range(doms):
        place = dom % per_row
        value = arrived_ref[dom, pieces : pieces + 1, :]
        shift = ((place - 3) * GROUP) % LANES
        value = pltpu.roll(value, shift, 1) if shift else value
        if place == 0:
            label_rows.append(value)
        else:
            label_rows[-1] = jnp.where(lane >= place * GROUP, value, label_rows[-1])
    cells_all = MAXD * all_tiles
    cell_no = lax.broadcasted_iota(jnp.int32, (cells_all, LANES), 0).astype(f32)
    to_cells = jnp.concatenate(
        [jnp.where(cell_no == row, 1.0, 0.0).astype(bf16) for row in label_rows], axis=1
    )
    upright = jnp.concatenate([jnp.broadcast_to(row, (SUBL, LANES)).T for row in label_rows], axis=0)
    cell_no = lax.broadcasted_iota(jnp.int32, (all_pieces, cells_all), 1).astype(f32)
    to_pieces = jnp.where(cell_no == upright[:, :1], 1.0, 0.0).astype(bf16)

    def moved(matrix, values):
        triple = jnp.concatenate([part.astype(bf16) for part in split3(values)], axis=1)
        wide = jnp.dot(matrix, triple, preferred_element_type=f32)
        return wide[:, :LANES] + wide[:, LANES : 2 * LANES] + wide[:, 2 * LANES :]

    data = arrived_ref[:, :pieces, :].reshape(all_pieces, LANES)
    cells = moved(to_cells, data)
    goal = arrived_ref[:, pieces:, :].reshape(all_tiles, LANES)
    lane = lax.broadcasted_iota(jnp.int32, (all_tiles, LANES), 1)
    last = lane >= 3 * GROUP
    backdrop = jnp.where(
        lane < GROUP,
        background_ref[0],
        jnp.where(lane < 2 * GROUP, background_ref[1], background_ref[2]),
    )

    def spread(value):
        return pltpu.roll(value, GROUP, 1) + pltpu.roll(value, 2 * GROUP, 1) + pltpu.roll(
            value, 3 * GROUP, 1
        )

    fronts, through, layers = [], [], []
    front = jnp.ones((all_tiles, LANES), f32)
    composite = jnp.zeros((all_tiles, LANES), f32)
    for depth in range(MAXD):
        layer = cells[depth * all_tiles : (depth + 1) * all_tiles]
        passed = jnp.where(last, 1.0 - layer, 0.0)
        passed = passed + spread(passed)
        fronts.append(front)
        through.append(passed)
        layers.append(layer)
        composite = composite + front * layer
        front = front * passed
    residual = jnp.where(last, 0.0, composite + front * backdrop - goal)
    behind = backdrop
    grads = [None] * MAXD
    for depth in reversed(range(MAXD)):
        grads[depth] = fronts[depth] * jnp.where(last, spread(residual * behind), residual)
        behind = layers[depth] + through[depth] * behind
    back = moved(to_pieces, jnp.concatenate(grads, axis=0))
    out_ref[...] = back.reshape(out_ref.shape)


def pull_items(begin, end, items_ref, table_ref, basis_ref, grad_ref, sums_ref, scratch):
    alpha_refs, shade_refs, local_refs, before_refs, hidden_refs = scratch
    pieces = basis_ref.shape[0]

    def grads_of(piece):
        halves = []
        for half in range(PIX // LANES):
            first = pl.multiple_of((half * (pieces + 1) + piece) * SUBL, SUBL)
            halves.append(grad_ref[pl.ds(first, SUBL), :])
        grads = jnp.concatenate(halves, axis=1)
        upper = lax.broadcasted_iota(jnp.int32, grads.shape, 0) < 4
        high, middle, low = split3(grads)
        first = jnp.where(upper, high, pltpu.roll(middle, 4, 0))
        return grads, first, jnp.where(upper, high, pltpu.roll(low, 4, 0))

    def multiply(found):
        products = []
        for slot in range(2):
            piece, block = found[1 + 2 * slot], found[2 + 2 * slot]
            grads, first, second = grads_of(piece)
            rhs = jnp.concatenate([first, second], axis=0).astype(bf16)
            rhs = jnp.concatenate([jnp.zeros((KE, PIX), bf16), rhs], axis=0)
            shades = jnp.dot(table_ref[block_rows(block), :], rhs, preferred_element_type=f32)
            powers = exponents(table_ref, basis_ref, piece, block, pieces)
            products.append((powers, shades, grads[3:4]))
        return products

    def front(found, products, side):
        chained = found[0] > 0
        carry, ends = None, []
        for slot, (powers, shades, final) in enumerate(products):
            alphas = jnp.exp2(powers)
            span = slice(slot * BLOCK, (slot + 1) * BLOCK)
            alpha_refs[side][span, :] = alphas
            shade_refs[side][span, :] = shades
            keep, total = None, None
            for row in range(ROWS):
                alpha = alphas[row * SUBL : (row + 1) * SUBL]
                weight = alpha if keep is None else alpha * keep
                keep = 1.0 - alpha if keep is None else keep - weight
                value = weight * shades[row * SUBL : (row + 1) * SUBL]
                total = value if total is None else total + value
                first = slot * BLOCK + row * SUBL
                local_refs[side][first : first + SUBL, :] = weight
            before, whole = prefix_product(keep)
            if slot == 1:
                before = before * jnp.where(chained, carry, 1.0)
            carry = whole
            before_refs[side][slot * SUBL : (slot + 1) * SUBL, :] = before
            ends.append((total, keep, final))
        behind = None
        for slot in (1, 0):
            total, keep, final = ends[slot]
            behind = jnp.where(chained, behind, final) if slot == 0 else final
            hidden, behind = suffix_affine(total, keep, behind)
            hidden_refs[side][slot * SUBL : (slot + 1) * SUBL, :] = hidden

    def back(found, side):
        along = (((1,), (1,)), ((), ()))
        for slot in range(2):
            piece, block = found[1 + 2 * slot], found[2 + 2 * slot]
            before = before_refs[side][slot * SUBL : (slot + 1) * SUBL, :]
            hidden = hidden_refs[side][slot * SUBL : (slot + 1) * SUBL, :]
            pulls, weights = [None] * ROWS, [None] * ROWS
            for row in reversed(range(ROWS)):
                first = slot * BLOCK + row * SUBL
                span = slice(first, first + SUBL)
                weight = local_refs[side][span, :] * before
                gap = shade_refs[side][span, :] - hidden
                weights[row] = weight
                pulls[row] = weight * gap
                hidden = hidden + alpha_refs[side][span, :] * gap
            unit = basis_ref[jnp.minimum(piece, pieces - 1)][:TOP]
            _, first, second = grads_of(piece)
            g_lhs = jnp.concatenate([first, second], axis=0).astype(bf16)
            for base, left, values in ((0, unit, pulls), (2, g_lhs, weights)):
                part = None
                for value in split2(jnp.concatenate(values, axis=0)):
                    product = lax.dot_general(left, value, along, preferred_element_type=f32)
                    part = product if part is None else part + product
                for group in range(2 if base == 0 else 1):
                    row = (base + group) * SLOTS * SUBL + block * SUBL
                    rows = pl.ds(pl.multiple_of(row, SUBL), SUBL)
                    sums_ref[rows, :] = (
                        sums_ref[rows, :] + part[group * SUBL : (group + 1) * SUBL]
                    )

    pipelined(items_ref, pieces, begin, end, multiply, front, back)


def early_pairs(items_ref, pieces):
    edge_pairs, pairs = item_ranges(items_ref, pieces)
    return jnp.minimum(jnp.maximum(edge_pairs, pieces * 3 // 16), pairs), pairs


def summed_terms(sums_ref):
    def rows_of(row):
        group, place = divmod(row, SUBL)
        return sums_ref[pl.ds(group * SLOTS * SUBL + place, SLOTS, stride=SUBL), :]

    moments = [rows_of(0), rows_of(1), rows_of(2)]
    moments += [rows_of(3 + 2 * i) + rows_of(4 + 2 * i) for i in range(3)]
    terms = [value * ln_2 for value in moments]
    terms += [rows_of(TOP + i) + rows_of(TOP + 4 + i) for i in range(3)]
    order = lane_order((SLOTS, LANES), True)
    return [jnp.take_along_axis(value, order, axis=1) for value in terms]


def backward_edge_kernel(
    items_ref,
    back_ref,
    table_ref,
    basis_ref,
    grad_ref,
    sums_ref,
    inner_ref,
    outer_ref,
    *scratch,
):
    doms, pieces = back_ref.shape[0], back_ref.shape[1]
    own_blocks = table_ref.shape[0] // BLOCK - 3
    width = PIX // doms
    lane = lax.broadcasted_iota(jnp.int32, (pieces, LANES), 1)
    grad_ref[...] = jnp.zeros_like(grad_ref)
    sums_ref[...] = jnp.zeros_like(sums_ref)
    for half in range(PIX // LANES):
        for channel in range(4):
            gathered = None
            for dom in range(half * LANES // width, (half + 1) * LANES // width):
                offset = dom * width - half * LANES
                shift = (offset - channel * GROUP) % LANES
                value = back_ref[dom]
                value = pltpu.roll(value, shift, 1) if shift else value
                gathered = value if gathered is None else jnp.where(lane >= offset, value, gathered)
            first = half * (pieces + 1) * SUBL + channel
            grad_ref[pl.ds(first, pieces, stride=SUBL), :] = gathered

    early, _ = early_pairs(items_ref, pieces)
    pull_items(0, early, items_ref, table_ref, basis_ref, grad_ref, sums_ref, scratch)
    even = lax.axis_index("region") % 2 == 0
    inner_ref[...] = jnp.zeros_like(inner_ref)
    outer_ref[...] = jnp.zeros_like(outer_ref)
    for term_no, value in enumerate(summed_terms(sums_ref)):
        high = value[own_blocks : own_blocks + 1]
        low = value[own_blocks + 1 : own_blocks + 2]
        inner_ref[term_no : term_no + 1, :] = jnp.where(even, high, low)
        outer_ref[term_no : term_no + 1, :] = jnp.where(even, low, high)


def backward_kernel(
    items_ref, table_ref, basis_ref, grad_ref, edge_sums_ref, own_ref, sums_ref, *scratch
):
    sums_ref[...] = edge_sums_ref[...]
    early, pairs = early_pairs(items_ref, basis_ref.shape[0])
    pull_items(early, pairs, items_ref, table_ref, basis_ref, grad_ref, sums_ref, scratch)
    for term_no, value in enumerate(summed_terms(sums_ref)):
        own_ref[term_no] = value[: own_ref.shape[1]]


def update_kernel(
    params_ref,
    first_ref,
    second_ref,
    own_ref,
    inner_ref,
    outer_ref,
    gradient_ref,
    new_params_ref,
    new_first_ref,
    new_second_ref,
    rows_ref,
    grads_ref,
):
    own_blocks = own_ref.shape[1]
    for block in range(own_blocks):
        rows_ref[pl.ds(block, PARAMS, stride=own_blocks), :] = params_ref[
            :, block * BLOCK : (block + 1) * BLOCK
        ]
    rows = [rows_ref[i * own_blocks : (i + 1) * own_blocks, :] for i in range(PARAMS)]
    slot = lax.broadcasted_iota(jnp.int32, (own_blocks, LANES), 0)
    even = lax.axis_index("region") % 2 == 0
    from_low = jnp.where(even, outer_ref[...], inner_ref[...])
    from_high = jnp.where(even, inner_ref[...], outer_ref[...])
    cots = []
    for term_no in range(9):
        low = jnp.where(slot == 0, from_low[term_no : term_no + 1, :], 0.0)
        high = jnp.where(slot == own_blocks - 1, from_high[term_no : term_no + 1, :], 0.0)
        cots.append(own_ref[term_no] + low + high)
    _, pull_back = jax.vjp(splat_rows, rows)
    pulled = pull_back((cots[:6], cots[6:]))[0]
    for i in range(PARAMS):
        grads_ref[i * own_blocks : (i + 1) * own_blocks, :] = pulled[i]
    for block in range(own_blocks):
        span = slice(block * BLOCK, (block + 1) * BLOCK)
        gradient = grads_ref[pl.ds(block, PARAMS, stride=own_blocks), :]
        new_first = beta_one * first_ref[:, span] + (1 - beta_one) * gradient
        new_second = beta_two * second_ref[:, span] + (1 - beta_two) * gradient * gradient
        update = (
            new_first
            / (1 - beta_one**adam_step)
            / (jnp.sqrt(new_second / (1 - beta_two**adam_step)) + tiny)
        )
        gradient_ref[:, span] = gradient
        new_params_ref[:, span] = params_ref[:, span] - rate * update
        new_first_ref[:, span] = new_first
        new_second_ref[:, span] = new_second


def exchange(to_inner, to_outer):
    count = lax.axis_size("region")
    inner = [(i, i ^ 1) for i in range(count) if (i ^ 1) < count]
    outer = [(i, i + 1) for i in range(1, count - 1, 2)]
    outer += [(target, source) for source, target in outer]
    near = lax.ppermute(to_inner, "region", inner)
    far = lax.ppermute(to_outer, "region", outer)
    return near, far


def on_device(
    params,
    first_moment,
    second_moment,
    piece_blocks,
    piece_live,
    piece_owner,
    piece_cell,
    target,
    background,
):
    own_blocks = params.shape[1] // BLOCK
    doms = lax.axis_size("dom")
    pieces = piece_live.shape[1]
    tiles = target.shape[1]
    even = lax.axis_index("region") % 2 == 0
    low, high = params[:, :BLOCK], params[:, -BLOCK:]
    inner, outer = exchange(jnp.where(even, high, low), jnp.where(even, low, high))
    basis = jnp.asarray(pixel_basis(pieces))
    smem = pl.BlockSpec(memory_space=pltpu.SMEM)
    vmem = pl.BlockSpec(memory_space=pltpu.VMEM)
    plane = pltpu.VMEM((2 * BLOCK, PIX), f32)
    strip = pltpu.VMEM((2 * SUBL, PIX), f32)
    piece_rows = (PIX // LANES * (pieces + 1) * SUBL, LANES)
    sums_shape = (3 * SLOTS * SUBL, LANES)
    table_shape = jax.ShapeDtypeStruct(((own_blocks + 3) * BLOCK, KT), bf16)
    colour_shape = jax.ShapeDtypeStruct((own_blocks + 3, TOP, LANES), bf16)
    result_shape = jax.ShapeDtypeStruct(piece_rows, f32)
    forward_scratch = [
        pltpu.VMEM((64 * SUBL, LANES), f32),
        pltpu.VMEM(((KT // SUBL + 1) * SUBL * SUBL, LANES), f32),
        [plane] * 2,
        [strip] * 2,
        [strip] * 2,
    ]
    backward_scratch = [[plane] * 2, [plane] * 2, [plane] * 2, [strip] * 2, [strip] * 2]
    params_limit = pltpu.CompilerParams(vmem_limit_bytes=vmem_limit)
    table, colour, result, basis, aimed, items = pl.pallas_call(
        forward_kernel,
        out_shape=(
            table_shape,
            colour_shape,
            result_shape,
            jax.ShapeDtypeStruct(basis.shape, bf16),
            jax.ShapeDtypeStruct((doms, tiles, LANES), f32),
            jax.ShapeDtypeStruct((2 * (3 * (pieces + SUBL) + 2),), jnp.int32),
        ),
        in_specs=[pl.BlockSpec(memory_space=pltpu.HBM)] * 7,
        out_specs=(vmem,) * 5 + (smem,),
        scratch_shapes=[
            pltpu.SMEM((2, pieces), jnp.int32),
            pltpu.SMEM((1, pieces), jnp.int32),
            pltpu.VMEM(params.shape, f32),
            pltpu.VMEM((1, pieces), jnp.int32),
            pltpu.VMEM((1, pieces), jnp.int32),
            pltpu.VMEM((3, tiles, PIX), f32),
            pltpu.SemaphoreType.DMA((7,)),
        ]
        + forward_scratch,
        compiler_params=params_limit,
        name="forward",
    )(
        *[
            pltpu.with_memory_space_constraint(value, pltpu.HBM)
            for value in (
                piece_blocks[0].T,
                piece_live,
                params,
                basis,
                piece_owner,
                piece_cell,
                jnp.transpose(target[0], (1, 0, 2)),
            )
        ]
    )
    table, _, _, payload = pl.pallas_call(
        forward_edge_kernel,
        out_shape=(
            table_shape,
            colour_shape,
            result_shape,
            jax.ShapeDtypeStruct((doms, pieces + tiles, LANES), f32),
        ),
        in_specs=[smem] + [vmem] * 7,
        out_specs=(vmem,) * 4,
        scratch_shapes=forward_scratch,
        input_output_aliases={5: 0, 6: 1, 7: 2},
        compiler_params=params_limit,
        name="forward_edge",
    )(
        items,
        inner,
        outer,
        aimed,
        basis,
        table,
        colour,
        result,
    )
    arrived = lax.all_to_all(payload, "dom", split_axis=0, concat_axis=0, tiled=True)
    back = pl.pallas_call(
        composite_kernel,
        out_shape=jax.ShapeDtypeStruct((doms, pieces, LANES), f32),
        in_specs=[smem, vmem],
        out_specs=vmem,
        compiler_params=params_limit,
        name="composite",
    )(background, arrived)
    returned = lax.all_to_all(back, "dom", split_axis=0, concat_axis=0, tiled=True)
    grads, edge_sums, to_inner, to_outer = pl.pallas_call(
        backward_edge_kernel,
        out_shape=(
            result_shape,
            jax.ShapeDtypeStruct(sums_shape, f32),
            jax.ShapeDtypeStruct((SLOTS, LANES), f32),
            jax.ShapeDtypeStruct((SLOTS, LANES), f32),
        ),
        in_specs=[smem] + [vmem] * 3,
        out_specs=(vmem,) * 4,
        scratch_shapes=backward_scratch,
        compiler_params=params_limit,
        name="backward_edge",
    )(items, returned, table, basis)
    inner, outer = exchange(to_inner, to_outer)
    own = pl.pallas_call(
        backward_kernel,
        out_shape=jax.ShapeDtypeStruct((9, own_blocks, LANES), f32),
        in_specs=[smem] + [vmem] * 4,
        out_specs=vmem,
        scratch_shapes=[pltpu.VMEM(sums_shape, f32)] + backward_scratch,
        compiler_params=params_limit,
        name="backward",
    )(items, table, basis, grads, edge_sums)
    shape = jax.ShapeDtypeStruct(params.shape, f32)
    return pl.pallas_call(
        update_kernel,
        out_shape=(shape, shape, shape, shape),
        in_specs=[vmem] * 6,
        out_specs=(vmem,) * 4,
        scratch_shapes=[
            pltpu.VMEM((64 * own_blocks, LANES), f32),
            pltpu.VMEM((64 * own_blocks, LANES), f32),
        ],
        name="update",
        compiler_params=pltpu.CompilerParams(vmem_limit_bytes=vmem_limit),
    )(params, first_moment, second_moment, own, inner, outer)


def solution(mesh):
    in_specs = (
        P(None, ("region", "dom")),
        P(None, ("region", "dom")),
        P(None, ("region", "dom")),
        P(("region", "dom"), None, None),
        P(("region", "dom"), None),
        P(("region", "dom"), None),
        P(("region", "dom"), None),
        P(("region", "dom"), None, None, None),
        P(),
    )
    out_specs = (P(None, ("region", "dom")),) * 4
    return jax.shard_map(
        on_device, mesh=mesh, in_specs=in_specs, out_specs=out_specs, check_vma=False
    )
```

```python
import math

import numpy as np
import jax
import jax.numpy as jnp
from jax import lax
from jax.experimental import pallas as pl
from jax.experimental.pallas import tpu as pltpu
from jax.sharding import PartitionSpec as P

PARAMS = 59
TSIDE = 16
WIN = 8
BLOCK = 128
MAXD = 8
PIX = 256

harmonic_zero = 0.28209479177387814
harmonic_one = 0.4886025119029199
harmonic_two = (
    1.0925484305920792,
    -1.0925484305920792,
    0.31539156525252005,
    -1.0925484305920792,
    0.5462742152960396,
)
harmonic_three = (
    -0.5900435899266435,
    2.890611442640554,
    -0.4570457994644658,
    0.3731763325901154,
    -0.4570457994644658,
    1.445305721320277,
    -0.5900435899266435,
)
beta_one = 0.9
beta_two = 0.999
rate = 0.001
adam_step = 100
tiny = 1e-08
log2_e = math.log2(math.e)
ln_2 = math.log(2.0)

LANES = 128
SUBL = 8
ROWS = BLOCK // SUBL
GROUP = LANES // 4
BASIS = 9
KE = 32
KC = 2 * SUBL
KT = KE + KC
TOP = 16
SLOTS = 16
vmem_limit = 12 * 2**20
f32 = jnp.float32
bf16 = jnp.bfloat16


def splat_rows(rows):
    mean_x, mean_y, mean_z = rows[0], rows[1], rows[2]
    scales = [jnp.exp(rows[3]), jnp.exp(rows[4]), jnp.exp(rows[5])]
    norm_sq = rows[6] * rows[6] + rows[7] * rows[7] + rows[8] * rows[8] + rows[9] * rows[9]
    inv_norm = 1.0 / jnp.sqrt(norm_sq)
    quat_w, quat_x, quat_y, quat_z = [rows[6 + i] * inv_norm for i in range(4)]
    rotation = [
        [
            1 - 2 * (quat_y * quat_y + quat_z * quat_z),
            2 * (quat_x * quat_y - quat_w * quat_z),
            2 * (quat_x * quat_z + quat_w * quat_y),
        ],
        [
            2 * (quat_x * quat_y + quat_w * quat_z),
            1 - 2 * (quat_x * quat_x + quat_z * quat_z),
            2 * (quat_y * quat_z - quat_w * quat_x),
        ],
        [
            2 * (quat_x * quat_z - quat_w * quat_y),
            2 * (quat_y * quat_z + quat_w * quat_x),
            1 - 2 * (quat_x * quat_x + quat_y * quat_y),
        ],
    ]
    focal_px = 0.3125 * float(WIN * TSIDE)
    inv_z = 1.0 / mean_z
    scale_z = focal_px * inv_z
    off_u = scale_z * mean_x
    off_v = scale_z * mean_y
    slope_u = off_u * inv_z
    slope_v = off_v * inv_z
    proj_u = [(scale_z * rotation[0][i] - slope_u * rotation[2][i]) * scales[i] for i in range(3)]
    proj_v = [(scale_z * rotation[1][i] - slope_v * rotation[2][i]) * scales[i] for i in range(3)]
    sigma_xx = proj_u[0] * proj_u[0] + proj_u[1] * proj_u[1] + proj_u[2] * proj_u[2] + 0.3
    sigma_xy = proj_u[0] * proj_v[0] + proj_u[1] * proj_v[1] + proj_u[2] * proj_v[2]
    sigma_yy = proj_v[0] * proj_v[0] + proj_v[1] * proj_v[1] + proj_v[2] * proj_v[2] + 0.3
    determinant = sigma_xx * sigma_yy - sigma_xy * sigma_xy
    inv_det = log2_e / determinant
    con_xx = sigma_yy * inv_det
    con_xy = -sigma_xy * inv_det
    con_yy = sigma_xx * inv_det
    lin_x = con_xx * off_u + con_xy * off_v
    lin_y = con_xy * off_u + con_yy * off_v
    logit = rows[10]
    log_opacity = (logit - jnp.log(1.0 + jnp.exp(logit))) * log2_e
    const = log_opacity - 0.5 * (lin_x * off_u + lin_y * off_v)
    coefs = [const, lin_x, lin_y, -0.5 * con_xx, -con_xy, -0.5 * con_yy]
    inv_len = 1.0 / jnp.sqrt(mean_x * mean_x + mean_y * mean_y + mean_z * mean_z)
    dir_x, dir_y, dir_z = mean_x * inv_len, mean_y * inv_len, mean_z * inv_len
    sq_x, sq_y, sq_z = dir_x * dir_x, dir_y * dir_y, dir_z * dir_z
    harmonics = [
        None,
        -harmonic_one * dir_y,
        harmonic_one * dir_z,
        -harmonic_one * dir_x,
        harmonic_two[0] * dir_x * dir_y,
        harmonic_two[1] * dir_y * dir_z,
        harmonic_two[2] * (2 * sq_z - sq_x - sq_y),
        harmonic_two[3] * dir_x * dir_z,
        harmonic_two[4] * (sq_x - sq_y),
        harmonic_three[0] * dir_y * (3 * sq_x - sq_y),
        harmonic_three[1] * dir_x * dir_y * dir_z,
        harmonic_three[2] * dir_y * (4 * sq_z - sq_x - sq_y),
        harmonic_three[3] * dir_z * (2 * sq_z - 3 * sq_x - 3 * sq_y),
        harmonic_three[4] * dir_x * (4 * sq_z - sq_x - sq_y),
        harmonic_three[5] * dir_z * (sq_x - sq_y),
        harmonic_three[6] * dir_x * (sq_x - 3 * sq_y),
    ]
    colours = []
    for colour_no in range(3):
        base = 11 + 16 * colour_no
        total = rows[base] * harmonic_zero
        for k in range(1, 16):
            total = total + rows[base + k] * harmonics[k]
        colours.append(jnp.maximum(total + 0.5, 0.0))
    return coefs, colours


def split3(value):
    high = value.astype(bf16).astype(f32)
    rest = value - high
    middle = rest.astype(bf16).astype(f32)
    return high, middle, rest - middle


def split2(value):
    high = value.astype(bf16)
    return high, (value - high.astype(f32)).astype(bf16)


def pixel_basis(pieces):
    tiles = np.arange(pieces)[:, None]
    pixels = np.arange(PIX)[None, :]
    half = WIN * TSIDE / 2
    pos_x = TSIDE * (tiles % WIN) + pixels % TSIDE + 0.5 - half
    pos_y = TSIDE * (tiles // WIN) + pixels // TSIDE + 0.5 - half
    rows = [np.ones_like(pos_x), pos_x, pos_y]
    for product in (pos_x * pos_x, pos_x * pos_y, pos_y * pos_y):
        high = product.astype(bf16).astype(np.float64)
        rows += [high, product - high]
    table = np.zeros((pieces, KE, PIX))
    for row_no, row in enumerate(rows * 3):
        table[:, row_no] = row
    return table.astype(bf16)


def basis_coefs(coefs):
    return [coefs[i] for i in (0, 1, 2, 3, 3, 4, 4, 5, 5)]


def lane_order(shape, inverse):
    lane = lax.broadcasted_iota(jnp.int32, shape, 1)
    if inverse:
        return (lane % ROWS) * SUBL + lane // ROWS
    return (lane % SUBL) * ROWS + lane // SUBL


def prefix_product(total):
    sub = lax.broadcasted_iota(jnp.int32, total.shape, 0)
    run = total
    for step in (1, 2, 4):
        run = jnp.where(sub >= step, run * pltpu.roll(run, step, 0), run)
    before = jnp.where(sub >= 1, pltpu.roll(run, 1, 0), 1.0)
    return before, run[SUBL - 1 :]


def suffix_affine(total, keep, behind):
    sub = lax.broadcasted_iota(jnp.int32, total.shape, 0)
    value, gain = total, keep
    for step in (1, 2, 4):
        inside = sub < SUBL - step
        next_value = jnp.where(inside, pltpu.roll(value, SUBL - step, 0), 0.0)
        next_gain = jnp.where(inside, pltpu.roll(gain, SUBL - step, 0), 1.0)
        value = value + gain * next_value
        gain = gain * next_gain
    whole = value + gain * behind
    after = jnp.where(sub < SUBL - 1, pltpu.roll(whole, SUBL - 1, 0), behind)
    return after, whole[:1]


def list_items(blocks_ref, live_ref, items_ref, pieces, own_blocks):
    room = pieces + SUBL
    size = 3 * room + 2
    doubles = [jnp.int32(0), jnp.int32(size)]
    singles = [jnp.int32(2 * room), jnp.int32(size + 2 * room)]
    for piece in range(pieces):
        places = []
        for slot in range(2):
            block = blocks_ref[slot, piece]
            places.append(jnp.where(block == 0, own_blocks + 1, block - 1))
        second = live_ref[0, piece] - 1
        edge = jnp.where(second > 0, jnp.maximum(places[0], places[1]), places[0]) >= own_blocks
        double = jnp.where(edge, doubles[1], doubles[0])
        single = jnp.where(edge, singles[1], singles[0])
        entry = places[0] * 64 + piece
        items_ref[double] = entry
        items_ref[room + double] = places[1] * 64 + piece
        items_ref[single] = entry
        edge_second = jnp.where(edge, second, 0)
        edge_first = jnp.where(edge, 1 - second, 0)
        doubles = [doubles[0] + second - edge_second, doubles[1] + edge_second]
        singles = [singles[0] + 1 - second - edge_first, singles[1] + edge_first]
    counts, sizes = [], []
    for which in range(2):
        for spare in range(6):
            items_ref[singles[which] + spare] = (own_blocks + 2) * 64 + pieces
        counts.append(doubles[which] - which * size)
        sizes.append(counts[which] + (singles[which] - which * size - 2 * room + 1) // 2)
    items_ref[size - 2] = counts[0]
    items_ref[size - 1] = counts[1]
    items_ref[2 * size - 2] = sizes[1]
    items_ref[2 * size - 1] = sizes[0] + sizes[1]


def item_ranges(items_ref, pieces):
    size = 3 * (pieces + SUBL) + 2
    return (items_ref[2 * size - 2] + 1) // 2, (items_ref[2 * size - 1] + 1) // 2


def item_slots(items_ref, item, pieces):
    room = pieces + SUBL
    size = 3 * room + 2
    edges = items_ref[2 * size - 2]
    raw = item
    edge = item < edges
    doubles = jnp.where(edge, items_ref[size - 1], items_ref[size - 2])
    base = jnp.where(edge, size, 0)
    item = jnp.where(edge, item, item - edges)
    chained = item < doubles
    single = base + 2 * (room + item - doubles)
    first = items_ref[jnp.where(chained, base + item, single)]
    second = items_ref[jnp.where(chained, base + room + item, single + 1)]
    found = [chained.astype(jnp.int32)]
    for entry in (first, second):
        found += [entry & 63, lax.shift_right_logical(entry, 6)]
    return (*found, raw)


def pipelined(items_ref, pieces, begin, end, multiply, front, back):
    def slots_of(item):
        return item_slots(items_ref, item, pieces)

    first = slots_of(2 * begin)
    front(first, multiply(first), 0)

    def step(pair, carry):
        this, middle, last = carry
        ahead = multiply(middle)
        further = multiply(last)
        back(this, 0)
        front(middle, ahead, 1)
        back(middle, 1)
        front(last, further, 0)
        return last, slots_of(2 * pair + 3), slots_of(2 * pair + 4)

    def two_steps(double, carry):
        pair = begin + 2 * double
        return step(pair + 1, step(pair, carry))

    doubles = (end - begin) // 2
    carry = (first, slots_of(2 * begin + 1), slots_of(2 * begin + 2))
    carry = lax.fori_loop(0, doubles, two_steps, carry)
    lax.fori_loop(begin + 2 * doubles, end, step, carry)


def block_rows(block):
    return pl.ds(pl.multiple_of(block * BLOCK, BLOCK), BLOCK)


def exponents(table_ref, basis_ref, piece, block, pieces):
    unit = basis_ref[jnp.minimum(piece, pieces - 1)]
    rhs = jnp.concatenate([unit, jnp.zeros((KC, PIX), bf16)], axis=0)
    return jnp.dot(table_ref[block_rows(block), :], rhs, preferred_element_type=f32)


def fill_tables(rows, present, places, stage_ref, table_ref, colour_ref):
    coefs, colours = splat_rows(rows)
    shape = (SUBL, LANES)
    order = lane_order(shape, False)

    def settled(value, absent):
        if present is not None:
            value = jnp.where(present, value, absent)
        return jnp.take_along_axis(value, order, axis=1)

    coefs = [settled(value, -1e9 if i == 0 else 0.0) for i, value in enumerate(coefs)]
    colours = [settled(value, 0.0) for value in colours]
    nothing = jnp.zeros(shape, f32)
    parts = basis_coefs([split3(value) for value in coefs])
    lines = [parts[row % BASIS][row // BASIS] for row in range(3 * BASIS)]
    lines += [nothing] * (KE - 3 * BASIS)
    triples = [split3(value) for value in colours]
    for level in (0, 0, 1, 0, 0, 1):
        lines += [triple[level] for triple in triples] + [nothing]
    for row, value in enumerate(lines):
        group, place = divmod(row, SUBL)
        stage_ref[pl.ds(group * SUBL * SUBL + place, SUBL, stride=SUBL), :] = value
    for sublane, block in enumerate(places):
        tiles = [
            stage_ref[(group * SUBL + sublane) * SUBL : (group * SUBL + sublane + 1) * SUBL, :]
            for group in range(len(lines) // SUBL)
        ]
        span = slice(block * BLOCK, (block + 1) * BLOCK)
        table_ref[span, :] = jnp.concatenate(tiles[: KT // SUBL], axis=0).T.astype(bf16)
        colour_ref[block] = jnp.concatenate(tiles[KT // SUBL :] * 2, axis=0).astype(bf16)


def render_items(
    begin, end, items_ref, table_ref, colour_ref, basis_ref, result_ref, saved_refs, scratch
):
    local_refs, before_refs, left_refs = scratch
    alpha_all_ref, local_all_ref, ends_all_ref = saved_refs
    pieces = basis_ref.shape[0]

    def multiply(found):
        return [
            exponents(table_ref, basis_ref, found[1 + 2 * slot], found[2 + 2 * slot], pieces)
            for slot in range(2)
        ]

    def front(found, powers, side):
        chained = found[0] > 0
        carry = None
        for slot in range(2):
            alphas = jnp.exp2(powers[slot])
            keep = None
            alpha_all_ref[found[5], slot * BLOCK : (slot + 1) * BLOCK, :] = alphas
            for row in range(ROWS):
                alpha = alphas[row * SUBL : (row + 1) * SUBL]
                weight = alpha if keep is None else alpha * keep
                keep = 1.0 - alpha if keep is None else keep - weight
                first = slot * BLOCK + row * SUBL
                local_refs[side][first : first + SUBL, :] = weight
                local_all_ref[found[5], first : first + SUBL, :] = weight
            before, total = prefix_product(keep)
            if slot == 1:
                carry = jnp.where(chained, carry, 1.0)
                before, total = before * carry, total * carry
            carry = total
            before_refs[side][slot * SUBL : (slot + 1) * SUBL, :] = before
            left_refs[side][slot : slot + 1, :] = total
            ends_all_ref[found[5], 2 * slot * SUBL : (2 * slot + 1) * SUBL, :] = before
            ends_all_ref[found[5], (2 * slot + 1) * SUBL : (2 * slot + 2) * SUBL, :] = keep

    def back(found, side):
        chained = found[0] > 0
        sums = None
        for slot in range(2):
            piece, block = found[1 + 2 * slot], found[2 + 2 * slot]
            before = before_refs[side][slot * SUBL : (slot + 1) * SUBL, :]
            weights = []
            for row in range(ROWS):
                first = slot * BLOCK + row * SUBL
                weights.append(local_refs[side][first : first + SUBL, :] * before)
            high, low = split2(jnp.concatenate(weights, axis=0))
            left = colour_ref[block]
            wide = jnp.dot(left, high, preferred_element_type=f32)
            wide = (wide + jnp.dot(left, low, preferred_element_type=f32))[:SUBL]
            wide = wide + pltpu.roll(wide, 4, 0)
            sums = wide + jnp.where(chained, sums, 0.0) if slot else wide
            row_no = lax.broadcasted_iota(jnp.int32, sums.shape, 0)
            value = jnp.where(row_no == 3, 1.0 - left_refs[side][slot : slot + 1, :], sums)
            for half in range(PIX // LANES):
                first = pl.multiple_of((half * (pieces + 1) + piece) * SUBL, SUBL)
                result_ref[pl.ds(first, SUBL), :] = value[:, half * LANES : (half + 1) * LANES]

    pipelined(items_ref, pieces, begin, end, multiply, front, back)


def forward_kernel(
    far_blocks_ref,
    far_live_ref,
    far_params_ref,
    far_basis_ref,
    far_owner_ref,
    far_cell_ref,
    far_target_ref,
    table_ref,
    colour_ref,
    result_ref,
    basis_ref,
    aimed_ref,
    alpha_all_ref,
    local_all_ref,
    ends_all_ref,
    items_ref,
    blocks_ref,
    live_ref,
    params_ref,
    owner_ref,
    cell_ref,
    target_ref,
    arrivals,
    rows_ref,
    stage_ref,
    *scratch,
):
    pieces = basis_ref.shape[0]
    own_blocks = params_ref.shape[1] // BLOCK
    moves = (
        (far_blocks_ref, blocks_ref),
        (far_live_ref, live_ref),
        (far_params_ref, params_ref),
        (far_owner_ref, owner_ref),
        (far_cell_ref, cell_ref),
        (far_target_ref, target_ref),
        (far_basis_ref, basis_ref),
    )
    fetches = [
        pltpu.make_async_copy(far, near, arrivals.at[i]) for i, (far, near) in enumerate(moves)
    ]
    for fetch in fetches:
        fetch.start()
    for fetch in fetches[:3]:
        fetch.wait()
    list_items(blocks_ref, live_ref, items_ref, pieces, own_blocks)
    for block in range(own_blocks):
        rows_ref[pl.ds(block, PARAMS, stride=SUBL), :] = params_ref[
            :, block * BLOCK : (block + 1) * BLOCK
        ]
    rows = [rows_ref[i * SUBL : (i + 1) * SUBL, :] for i in range(PARAMS)]
    fill_tables(rows, None, range(own_blocks), stage_ref, table_ref, colour_ref)
    empty = own_blocks + 2
    column = lax.broadcasted_iota(jnp.int32, (BLOCK, KT), 1)
    table_ref[empty * BLOCK : (empty + 1) * BLOCK, :] = jnp.where(column == 0, -1e9, 0.0).astype(
        bf16
    )
    colour_ref[empty] = jnp.zeros((TOP, LANES), bf16)
    for fetch in fetches[3:]:
        fetch.wait()
    doms = aimed_ref.shape[0]
    width, tiles = PIX // doms, target_ref.shape[1]
    tile_lane = lax.broadcasted_iota(jnp.int32, (SUBL, LANES), 1)
    cell = cell_ref[...]
    labels = (cell % MAXD) * (doms * tiles) + owner_ref[...] * tiles + cell // MAXD
    labels = jnp.concatenate(
        [jnp.zeros((1, LANES - pieces), f32), labels.astype(f32)], axis=1
    )
    labels = jnp.broadcast_to(labels, (SUBL, LANES))
    for dom in range(doms):
        half, offset = divmod(dom * width, LANES)
        span = slice(half * LANES, (half + 1) * LANES)
        aimed = labels
        for channel in (2, 1, 0):
            shift = (channel * GROUP - offset) % LANES
            value = target_ref[channel, :, span]
            value = pltpu.roll(value, shift, 1) if shift else value
            aimed = jnp.where(tile_lane < (channel + 1) * GROUP, value, aimed)
        aimed_ref[dom] = aimed
    edge_pairs, pairs = item_ranges(items_ref, pieces)
    saved = (alpha_all_ref, local_all_ref, ends_all_ref)
    render_items(edge_pairs, pairs, items_ref, table_ref, colour_ref, basis_ref, result_ref, saved, scratch)


def forward_edge_kernel(
    items_ref,
    inner_ref,
    outer_ref,
    aimed_ref,
    basis_ref,
    *refs,
):
    table_ref, colour_ref, result_ref, *saved, out_ref, rows_ref, stage_ref = refs[6:15]
    scratch = refs[15:]
    doms, pieces = out_ref.shape[0], basis_ref.shape[0]
    own_blocks = table_ref.shape[0] // BLOCK - 3
    region_idx, regions = lax.axis_index("region"), lax.axis_size("region")
    even = region_idx % 2 == 0
    inner, outer = inner_ref[...], outer_ref[...]
    rows_ref[pl.ds(0, PARAMS, stride=SUBL), :] = jnp.where(even, inner, outer)
    rows_ref[pl.ds(1, PARAMS, stride=SUBL), :] = jnp.where(even, outer, inner)
    rows = [rows_ref[i * SUBL : (i + 1) * SUBL, :] for i in range(PARAMS)]
    sublane = lax.broadcasted_iota(jnp.int32, (SUBL, LANES), 0)
    present = ((sublane == 0) & (region_idx < regions - 1)) | ((sublane == 1) & (region_idx > 0))
    places = (own_blocks, own_blocks + 1)
    fill_tables(rows, present, places, stage_ref, table_ref, colour_ref)
    render_items(0, item_ranges(items_ref, pieces)[0], items_ref, table_ref, colour_ref, basis_ref, result_ref, saved, scratch)
    width = PIX // doms
    lane = lax.broadcasted_iota(jnp.int32, (pieces, LANES), 1)
    tiles = aimed_ref.shape[1]
    for dom in range(doms):
        half, offset = divmod(dom * width, LANES)
        packed = None
        for channel in range(4):
            shift = (channel * GROUP - offset) % LANES
            first = half * (pieces + 1) * SUBL + channel
            value = result_ref[pl.ds(first, pieces, stride=SUBL), :]
            value = pltpu.roll(value, shift, 1) if shift else value
            packed = value if packed is None else jnp.where(lane >= channel * GROUP, value, packed)
        out_ref[dom, :pieces, :] = packed
        out_ref[dom, pieces : pieces + tiles, :] = aimed_ref[dom]


def composite_kernel(background_ref, arrived_ref, out_ref):
    doms, pieces = out_ref.shape[0], out_ref.shape[1]
    tiles = arrived_ref.shape[1] - pieces
    all_pieces, all_tiles = doms * pieces, doms * tiles
    per_row = LANES // GROUP
    lane = lax.broadcasted_iota(jnp.int32, (1, LANES), 1)
    label_rows = []
    for dom in range(doms):
        place = dom % per_row
        value = arrived_ref[dom, pieces : pieces + 1, :]
        shift = ((place - 3) * GROUP) % LANES
        value = pltpu.roll(value, shift, 1) if shift else value
        if place == 0:
            label_rows.append(value)
        else:
            label_rows[-1] = jnp.where(lane >= place * GROUP, value, label_rows[-1])
    cells_all = MAXD * all_tiles
    cell_no = lax.broadcasted_iota(jnp.int32, (cells_all, LANES), 0).astype(f32)
    to_cells = jnp.concatenate(
        [jnp.where(cell_no == row, 1.0, 0.0).astype(bf16) for row in label_rows], axis=1
    )
    upright = jnp.concatenate([jnp.broadcast_to(row, (SUBL, LANES)).T for row in label_rows], axis=0)
    cell_no = lax.broadcasted_iota(jnp.int32, (all_pieces, cells_all), 1).astype(f32)
    to_pieces = jnp.where(cell_no == upright[:, :1], 1.0, 0.0).astype(bf16)

    def moved(matrix, values):
        wide = jnp.dot(
            matrix, jnp.concatenate(split2(values), axis=1), preferred_element_type=f32
        )
        return wide[:, :LANES] + wide[:, LANES:]

    data = arrived_ref[:, :pieces, :].reshape(all_pieces, LANES)
    cells = moved(to_cells, data)
    goal = arrived_ref[:, pieces:, :].reshape(all_tiles, LANES)
    lane = lax.broadcasted_iota(jnp.int32, (all_tiles, LANES), 1)
    last = lane >= 3 * GROUP
    backdrop = jnp.where(
        lane < GROUP,
        background_ref[0],
        jnp.where(lane < 2 * GROUP, background_ref[1], background_ref[2]),
    )

    def spread(value):
        return pltpu.roll(value, GROUP, 1) + pltpu.roll(value, 2 * GROUP, 1) + pltpu.roll(
            value, 3 * GROUP, 1
        )

    fronts, through, layers = [], [], []
    front = jnp.ones((all_tiles, LANES), f32)
    composite = jnp.zeros((all_tiles, LANES), f32)
    for depth in range(MAXD):
        layer = cells[depth * all_tiles : (depth + 1) * all_tiles]
        passed = jnp.where(last, 1.0 - layer, 0.0)
        passed = passed + spread(passed)
        fronts.append(front)
        through.append(passed)
        layers.append(layer)
        composite = composite + front * layer
        front = front * passed
    residual = jnp.where(last, 0.0, composite + front * backdrop - goal)
    behind = backdrop
    grads = [None] * MAXD
    for depth in reversed(range(MAXD)):
        grads[depth] = fronts[depth] * jnp.where(last, spread(residual * behind), residual)
        behind = layers[depth] + through[depth] * behind
    back = moved(to_pieces, jnp.concatenate(grads, axis=0))
    out_ref[...] = back.reshape(out_ref.shape)


def pull_items(
    begin, end, items_ref, table_ref, basis_ref, grad_ref, sums_ref, saved_refs, scratch
):
    shade_refs, hidden_refs = scratch
    alpha_all_ref, local_all_ref, ends_all_ref = saved_refs
    pieces = basis_ref.shape[0]

    def grads_of(piece):
        halves = []
        for half in range(PIX // LANES):
            first = pl.multiple_of((half * (pieces + 1) + piece) * SUBL, SUBL)
            halves.append(grad_ref[pl.ds(first, SUBL), :])
        grads = jnp.concatenate(halves, axis=1)
        upper = lax.broadcasted_iota(jnp.int32, grads.shape, 0) < 4
        high, middle, low = split3(grads)
        first = jnp.where(upper, high, pltpu.roll(middle, 4, 0))
        return grads, first, jnp.where(upper, high, pltpu.roll(low, 4, 0))

    def multiply(found):
        products = []
        for slot in range(2):
            piece, block = found[1 + 2 * slot], found[2 + 2 * slot]
            grads, first, second = grads_of(piece)
            rhs = jnp.concatenate([first, second], axis=0).astype(bf16)
            rhs = jnp.concatenate([jnp.zeros((KE, PIX), bf16), rhs], axis=0)
            shades = jnp.dot(table_ref[block_rows(block), :], rhs, preferred_element_type=f32)
            products.append((shades, grads[3:4]))
        return products

    def front(found, products, side):
        chained, item = found[0] > 0, found[5]
        ends = []
        for slot, (shades, final) in enumerate(products):
            span = slice(slot * BLOCK, (slot + 1) * BLOCK)
            shade_refs[side][span, :] = shades
            total = None
            for row in range(ROWS):
                first = slot * BLOCK + row * SUBL
                value = local_all_ref[item, first : first + SUBL, :] * shades[
                    row * SUBL : (row + 1) * SUBL
                ]
                total = value if total is None else total + value
            keep = ends_all_ref[item, (2 * slot + 1) * SUBL : (2 * slot + 2) * SUBL, :]
            ends.append((total, keep, final))
        behind = None
        for slot in (1, 0):
            total, keep, final = ends[slot]
            behind = jnp.where(chained, behind, final) if slot == 0 else final
            hidden, behind = suffix_affine(total, keep, behind)
            hidden_refs[side][slot * SUBL : (slot + 1) * SUBL, :] = hidden

    def back(found, side):
        along = (((1,), (1,)), ((), ()))
        for slot in range(2):
            piece, block = found[1 + 2 * slot], found[2 + 2 * slot]
            before = ends_all_ref[found[5], 2 * slot * SUBL : (2 * slot + 1) * SUBL, :]
            hidden = hidden_refs[side][slot * SUBL : (slot + 1) * SUBL, :]
            pulls, weights = [None] * ROWS, [None] * ROWS
            for row in reversed(range(ROWS)):
                first = slot * BLOCK + row * SUBL
                span = slice(first, first + SUBL)
                weight = local_all_ref[found[5], span, :] * before
                gap = shade_refs[side][span, :] - hidden
                weights[row] = weight
                pulls[row] = weight * gap
                hidden = hidden + alpha_all_ref[found[5], span, :] * gap
            unit = basis_ref[jnp.minimum(piece, pieces - 1)][:TOP]
            _, first, second = grads_of(piece)
            g_lhs = jnp.concatenate([first, second], axis=0).astype(bf16)
            for base, left, values in ((0, unit, pulls), (2, g_lhs, weights)):
                part = None
                for value in split2(jnp.concatenate(values, axis=0)):
                    product = lax.dot_general(left, value, along, preferred_element_type=f32)
                    part = product if part is None else part + product
                for group in range(2 if base == 0 else 1):
                    row = (base + group) * SLOTS * SUBL + block * SUBL
                    rows = pl.ds(pl.multiple_of(row, SUBL), SUBL)
                    sums_ref[rows, :] = (
                        sums_ref[rows, :] + part[group * SUBL : (group + 1) * SUBL]
                    )

    pipelined(items_ref, pieces, begin, end, multiply, front, back)


def early_pairs(items_ref, pieces):
    edge_pairs, pairs = item_ranges(items_ref, pieces)
    return jnp.minimum(jnp.maximum(edge_pairs, pieces * 3 // 16), pairs), pairs


def summed_terms(sums_ref):
    def rows_of(row):
        group, place = divmod(row, SUBL)
        return sums_ref[pl.ds(group * SLOTS * SUBL + place, SLOTS, stride=SUBL), :]

    moments = [rows_of(0), rows_of(1), rows_of(2)]
    moments += [rows_of(3 + 2 * i) + rows_of(4 + 2 * i) for i in range(3)]
    terms = [value * ln_2 for value in moments]
    terms += [rows_of(TOP + i) + rows_of(TOP + 4 + i) for i in range(3)]
    order = lane_order((SLOTS, LANES), True)
    return [jnp.take_along_axis(value, order, axis=1) for value in terms]


def backward_edge_kernel(
    items_ref,
    back_ref,
    table_ref,
    basis_ref,
    alpha_all_ref,
    local_all_ref,
    ends_all_ref,
    grad_ref,
    sums_ref,
    inner_ref,
    outer_ref,
    *scratch,
):
    doms, pieces = back_ref.shape[0], back_ref.shape[1]
    own_blocks = table_ref.shape[0] // BLOCK - 3
    width = PIX // doms
    lane = lax.broadcasted_iota(jnp.int32, (pieces, LANES), 1)
    grad_ref[...] = jnp.zeros_like(grad_ref)
    sums_ref[...] = jnp.zeros_like(sums_ref)
    for half in range(PIX // LANES):
        for channel in range(4):
            gathered = None
            for dom in range(half * LANES // width, (half + 1) * LANES // width):
                offset = dom * width - half * LANES
                shift = (offset - channel * GROUP) % LANES
                value = back_ref[dom]
                value = pltpu.roll(value, shift, 1) if shift else value
                gathered = value if gathered is None else jnp.where(lane >= offset, value, gathered)
            first = half * (pieces + 1) * SUBL + channel
            grad_ref[pl.ds(first, pieces, stride=SUBL), :] = gathered

    early, _ = early_pairs(items_ref, pieces)
    saved = (alpha_all_ref, local_all_ref, ends_all_ref)
    pull_items(0, early, items_ref, table_ref, basis_ref, grad_ref, sums_ref, saved, scratch)
    even = lax.axis_index("region") % 2 == 0
    inner_ref[...] = jnp.zeros_like(inner_ref)
    outer_ref[...] = jnp.zeros_like(outer_ref)
    for term_no, value in enumerate(summed_terms(sums_ref)):
        high = value[own_blocks : own_blocks + 1]
        low = value[own_blocks + 1 : own_blocks + 2]
        inner_ref[term_no : term_no + 1, :] = jnp.where(even, high, low)
        outer_ref[term_no : term_no + 1, :] = jnp.where(even, low, high)


def backward_kernel(
    items_ref, table_ref, basis_ref, grad_ref, edge_sums_ref, *refs
):
    saved, own_ref, sums_ref, scratch = refs[:3], refs[3], refs[4], refs[5:]
    sums_ref[...] = edge_sums_ref[...]
    early, pairs = early_pairs(items_ref, basis_ref.shape[0])
    pull_items(
        early, pairs, items_ref, table_ref, basis_ref, grad_ref, sums_ref, saved, scratch
    )
    for term_no, value in enumerate(summed_terms(sums_ref)):
        own_ref[term_no] = value[: own_ref.shape[1]]


def update_kernel(
    params_ref,
    first_ref,
    second_ref,
    own_ref,
    inner_ref,
    outer_ref,
    gradient_ref,
    new_params_ref,
    new_first_ref,
    new_second_ref,
    rows_ref,
    grads_ref,
):
    own_blocks = own_ref.shape[1]
    for block in range(own_blocks):
        rows_ref[pl.ds(block, PARAMS, stride=own_blocks), :] = params_ref[
            :, block * BLOCK : (block + 1) * BLOCK
        ]
    rows = [rows_ref[i * own_blocks : (i + 1) * own_blocks, :] for i in range(PARAMS)]
    slot = lax.broadcasted_iota(jnp.int32, (own_blocks, LANES), 0)
    even = lax.axis_index("region") % 2 == 0
    from_low = jnp.where(even, outer_ref[...], inner_ref[...])
    from_high = jnp.where(even, inner_ref[...], outer_ref[...])
    cots = []
    for term_no in range(9):
        low = jnp.where(slot == 0, from_low[term_no : term_no + 1, :], 0.0)
        high = jnp.where(slot == own_blocks - 1, from_high[term_no : term_no + 1, :], 0.0)
        cots.append(own_ref[term_no] + low + high)
    _, pull_back = jax.vjp(splat_rows, rows)
    pulled = pull_back((cots[:6], cots[6:]))[0]
    for i in range(PARAMS):
        grads_ref[i * own_blocks : (i + 1) * own_blocks, :] = pulled[i]
    for block in range(own_blocks):
        span = slice(block * BLOCK, (block + 1) * BLOCK)
        gradient = grads_ref[pl.ds(block, PARAMS, stride=own_blocks), :]
        new_first = beta_one * first_ref[:, span] + (1 - beta_one) * gradient
        new_second = beta_two * second_ref[:, span] + (1 - beta_two) * gradient * gradient
        update = (
            new_first
            / (1 - beta_one**adam_step)
            / (jnp.sqrt(new_second / (1 - beta_two**adam_step)) + tiny)
        )
        gradient_ref[:, span] = gradient
        new_params_ref[:, span] = params_ref[:, span] - rate * update
        new_first_ref[:, span] = new_first
        new_second_ref[:, span] = new_second


def exchange(to_inner, to_outer):
    count = lax.axis_size("region")
    inner = [(i, i ^ 1) for i in range(count) if (i ^ 1) < count]
    outer = [(i, i + 1) for i in range(1, count - 1, 2)]
    outer += [(target, source) for source, target in outer]
    near = lax.ppermute(to_inner, "region", inner)
    far = lax.ppermute(to_outer, "region", outer)
    return near, far


def on_device(
    params,
    first_moment,
    second_moment,
    piece_blocks,
    piece_live,
    piece_owner,
    piece_cell,
    target,
    background,
):
    own_blocks = params.shape[1] // BLOCK
    doms = lax.axis_size("dom")
    pieces = piece_live.shape[1]
    tiles = target.shape[1]
    even = lax.axis_index("region") % 2 == 0
    low, high = params[:, :BLOCK], params[:, -BLOCK:]
    inner, outer = exchange(jnp.where(even, high, low), jnp.where(even, low, high))
    basis = jnp.asarray(pixel_basis(pieces))
    smem = pl.BlockSpec(memory_space=pltpu.SMEM)
    vmem = pl.BlockSpec(memory_space=pltpu.VMEM)
    plane = pltpu.VMEM((2 * BLOCK, PIX), f32)
    strip = pltpu.VMEM((2 * SUBL, PIX), f32)
    piece_rows = (PIX // LANES * (pieces + 1) * SUBL, LANES)
    sums_shape = (3 * SLOTS * SUBL, LANES)
    table_shape = jax.ShapeDtypeStruct(((own_blocks + 3) * BLOCK, KT), bf16)
    colour_shape = jax.ShapeDtypeStruct((own_blocks + 3, TOP, LANES), bf16)
    result_shape = jax.ShapeDtypeStruct(piece_rows, f32)
    forward_scratch = [
        pltpu.VMEM((64 * SUBL, LANES), f32),
        pltpu.VMEM(((KT // SUBL + 1) * SUBL * SUBL, LANES), f32),
        [plane] * 2,
        [strip] * 2,
        [strip] * 2,
    ]
    backward_scratch = [[plane] * 2, [strip] * 2]
    saved_shapes = tuple(
        jax.ShapeDtypeStruct((pieces + 4, rows, PIX), f32)
        for rows in (2 * BLOCK, 2 * BLOCK, 4 * SUBL)
    )
    params_limit = pltpu.CompilerParams(vmem_limit_bytes=vmem_limit)
    table, colour, result, basis, aimed, *saved, items = pl.pallas_call(
        forward_kernel,
        out_shape=(
            table_shape,
            colour_shape,
            result_shape,
            jax.ShapeDtypeStruct(basis.shape, bf16),
            jax.ShapeDtypeStruct((doms, tiles, LANES), f32),
            *saved_shapes,
            jax.ShapeDtypeStruct((2 * (3 * (pieces + SUBL) + 2),), jnp.int32),
        ),
        in_specs=[pl.BlockSpec(memory_space=pltpu.HBM)] * 7,
        out_specs=(vmem,) * 8 + (smem,),
        scratch_shapes=[
            pltpu.SMEM((2, pieces), jnp.int32),
            pltpu.SMEM((1, pieces), jnp.int32),
            pltpu.VMEM(params.shape, f32),
            pltpu.VMEM((1, pieces), jnp.int32),
            pltpu.VMEM((1, pieces), jnp.int32),
            pltpu.VMEM((3, tiles, PIX), f32),
            pltpu.SemaphoreType.DMA((7,)),
        ]
        + forward_scratch,
        compiler_params=params_limit,
        name="forward",
    )(
        *[
            pltpu.with_memory_space_constraint(value, pltpu.HBM)
            for value in (
                piece_blocks[0].T,
                piece_live,
                params,
                basis,
                piece_owner,
                piece_cell,
                jnp.transpose(target[0], (1, 0, 2)),
            )
        ]
    )
    table, _, _, *saved, payload = pl.pallas_call(
        forward_edge_kernel,
        out_shape=(
            table_shape,
            colour_shape,
            result_shape,
            *saved_shapes,
            jax.ShapeDtypeStruct((doms, pieces + tiles, LANES), f32),
        ),
        in_specs=[smem] + [vmem] * 10,
        out_specs=(vmem,) * 7,
        scratch_shapes=forward_scratch,
        input_output_aliases={5 + i: i for i in range(6)},
        compiler_params=params_limit,
        name="forward_edge",
    )(
        items,
        inner,
        outer,
        aimed,
        basis,
        table,
        colour,
        result,
        *saved,
    )
    arrived = lax.all_to_all(payload, "dom", split_axis=0, concat_axis=0, tiled=True)
    back = pl.pallas_call(
        composite_kernel,
        out_shape=jax.ShapeDtypeStruct((doms, pieces, LANES), f32),
        in_specs=[smem, vmem],
        out_specs=vmem,
        compiler_params=params_limit,
        name="composite",
    )(background, arrived)
    returned = lax.all_to_all(back, "dom", split_axis=0, concat_axis=0, tiled=True)
    grads, edge_sums, to_inner, to_outer = pl.pallas_call(
        backward_edge_kernel,
        out_shape=(
            result_shape,
            jax.ShapeDtypeStruct(sums_shape, f32),
            jax.ShapeDtypeStruct((SLOTS, LANES), f32),
            jax.ShapeDtypeStruct((SLOTS, LANES), f32),
        ),
        in_specs=[smem] + [vmem] * 6,
        out_specs=(vmem,) * 4,
        scratch_shapes=backward_scratch,
        compiler_params=params_limit,
        name="backward_edge",
    )(items, returned, table, basis, *saved)
    inner, outer = exchange(to_inner, to_outer)
    own = pl.pallas_call(
        backward_kernel,
        out_shape=jax.ShapeDtypeStruct((9, own_blocks, LANES), f32),
        in_specs=[smem] + [vmem] * 7,
        out_specs=vmem,
        scratch_shapes=[pltpu.VMEM(sums_shape, f32)] + backward_scratch,
        compiler_params=params_limit,
        name="backward",
    )(items, table, basis, grads, edge_sums, *saved)
    shape = jax.ShapeDtypeStruct(params.shape, f32)
    return pl.pallas_call(
        update_kernel,
        out_shape=(shape, shape, shape, shape),
        in_specs=[vmem] * 6,
        out_specs=(vmem,) * 4,
        scratch_shapes=[
            pltpu.VMEM((64 * own_blocks, LANES), f32),
            pltpu.VMEM((64 * own_blocks, LANES), f32),
        ],
        name="update",
        compiler_params=pltpu.CompilerParams(vmem_limit_bytes=vmem_limit),
    )(params, first_moment, second_moment, own, inner, outer)


def solution(mesh):
    in_specs = (
        P(None, ("region", "dom")),
        P(None, ("region", "dom")),
        P(None, ("region", "dom")),
        P(("region", "dom"), None, None),
        P(("region", "dom"), None),
        P(("region", "dom"), None),
        P(("region", "dom"), None),
        P(("region", "dom"), None, None, None),
        P(),
    )
    out_specs = (P(None, ("region", "dom")),) * 4
    return jax.shard_map(
        on_device, mesh=mesh, in_specs=in_specs, out_specs=out_specs, check_vma=False
    )
```

```python
import math

import numpy as np
import jax
import jax.numpy as jnp
from jax import lax
from jax.experimental import pallas as pl
from jax.experimental.pallas import tpu as pltpu
from jax.sharding import PartitionSpec as P

PARAMS = 59
TSIDE = 16
WIN = 8
BLOCK = 128
MAXD = 8
PIX = 256

harmonic_zero = 0.28209479177387814
harmonic_one = 0.4886025119029199
harmonic_two = (
    1.0925484305920792,
    -1.0925484305920792,
    0.31539156525252005,
    -1.0925484305920792,
    0.5462742152960396,
)
harmonic_three = (
    -0.5900435899266435,
    2.890611442640554,
    -0.4570457994644658,
    0.3731763325901154,
    -0.4570457994644658,
    1.445305721320277,
    -0.5900435899266435,
)
beta_one = 0.9
beta_two = 0.999
rate = 0.001
adam_step = 100
tiny = 1e-08
log2_e = math.log2(math.e)
ln_2 = math.log(2.0)

LANES = 128
SUBL = 8
ROWS = BLOCK // SUBL
GROUP = LANES // 4
BASIS = 9
KE = 32
KC = 2 * SUBL
KT = KE + KC
TOP = 16
SLOTS = 16
vmem_limit = 12 * 2**20
f32 = jnp.float32
bf16 = jnp.bfloat16


def splat_rows(rows):
    mean_x, mean_y, mean_z = rows[0], rows[1], rows[2]
    scales = [jnp.exp(rows[3]), jnp.exp(rows[4]), jnp.exp(rows[5])]
    norm_sq = rows[6] * rows[6] + rows[7] * rows[7] + rows[8] * rows[8] + rows[9] * rows[9]
    inv_norm = 1.0 / jnp.sqrt(norm_sq)
    quat_w, quat_x, quat_y, quat_z = [rows[6 + i] * inv_norm for i in range(4)]
    rotation = [
        [
            1 - 2 * (quat_y * quat_y + quat_z * quat_z),
            2 * (quat_x * quat_y - quat_w * quat_z),
            2 * (quat_x * quat_z + quat_w * quat_y),
        ],
        [
            2 * (quat_x * quat_y + quat_w * quat_z),
            1 - 2 * (quat_x * quat_x + quat_z * quat_z),
            2 * (quat_y * quat_z - quat_w * quat_x),
        ],
        [
            2 * (quat_x * quat_z - quat_w * quat_y),
            2 * (quat_y * quat_z + quat_w * quat_x),
            1 - 2 * (quat_x * quat_x + quat_y * quat_y),
        ],
    ]
    focal_px = 0.3125 * float(WIN * TSIDE)
    inv_z = 1.0 / mean_z
    scale_z = focal_px * inv_z
    off_u = scale_z * mean_x
    off_v = scale_z * mean_y
    slope_u = off_u * inv_z
    slope_v = off_v * inv_z
    proj_u = [(scale_z * rotation[0][i] - slope_u * rotation[2][i]) * scales[i] for i in range(3)]
    proj_v = [(scale_z * rotation[1][i] - slope_v * rotation[2][i]) * scales[i] for i in range(3)]
    sigma_xx = proj_u[0] * proj_u[0] + proj_u[1] * proj_u[1] + proj_u[2] * proj_u[2] + 0.3
    sigma_xy = proj_u[0] * proj_v[0] + proj_u[1] * proj_v[1] + proj_u[2] * proj_v[2]
    sigma_yy = proj_v[0] * proj_v[0] + proj_v[1] * proj_v[1] + proj_v[2] * proj_v[2] + 0.3
    determinant = sigma_xx * sigma_yy - sigma_xy * sigma_xy
    inv_det = log2_e / determinant
    con_xx = sigma_yy * inv_det
    con_xy = -sigma_xy * inv_det
    con_yy = sigma_xx * inv_det
    lin_x = con_xx * off_u + con_xy * off_v
    lin_y = con_xy * off_u + con_yy * off_v
    logit = rows[10]
    log_opacity = (logit - jnp.log(1.0 + jnp.exp(logit))) * log2_e
    const = log_opacity - 0.5 * (lin_x * off_u + lin_y * off_v)
    coefs = [const, lin_x, lin_y, -0.5 * con_xx, -con_xy, -0.5 * con_yy]
    inv_len = 1.0 / jnp.sqrt(mean_x * mean_x + mean_y * mean_y + mean_z * mean_z)
    dir_x, dir_y, dir_z = mean_x * inv_len, mean_y * inv_len, mean_z * inv_len
    sq_x, sq_y, sq_z = dir_x * dir_x, dir_y * dir_y, dir_z * dir_z
    harmonics = [
        None,
        -harmonic_one * dir_y,
        harmonic_one * dir_z,
        -harmonic_one * dir_x,
        harmonic_two[0] * dir_x * dir_y,
        harmonic_two[1] * dir_y * dir_z,
        harmonic_two[2] * (2 * sq_z - sq_x - sq_y),
        harmonic_two[3] * dir_x * dir_z,
        harmonic_two[4] * (sq_x - sq_y),
        harmonic_three[0] * dir_y * (3 * sq_x - sq_y),
        harmonic_three[1] * dir_x * dir_y * dir_z,
        harmonic_three[2] * dir_y * (4 * sq_z - sq_x - sq_y),
        harmonic_three[3] * dir_z * (2 * sq_z - 3 * sq_x - 3 * sq_y),
        harmonic_three[4] * dir_x * (4 * sq_z - sq_x - sq_y),
        harmonic_three[5] * dir_z * (sq_x - sq_y),
        harmonic_three[6] * dir_x * (sq_x - 3 * sq_y),
    ]
    colours = []
    for colour_no in range(3):
        base = 11 + 16 * colour_no
        total = rows[base] * harmonic_zero
        for k in range(1, 16):
            total = total + rows[base + k] * harmonics[k]
        colours.append(jnp.maximum(total + 0.5, 0.0))
    return coefs, colours


def split3(value):
    high = value.astype(bf16).astype(f32)
    rest = value - high
    middle = rest.astype(bf16).astype(f32)
    return high, middle, rest - middle


def split2(value):
    high = value.astype(bf16)
    return high, (value - high.astype(f32)).astype(bf16)


def pixel_basis(pieces):
    tiles = np.arange(pieces)[:, None]
    pixels = np.arange(PIX)[None, :]
    half = WIN * TSIDE / 2
    pos_x = TSIDE * (tiles % WIN) + pixels % TSIDE + 0.5 - half
    pos_y = TSIDE * (tiles // WIN) + pixels // TSIDE + 0.5 - half
    rows = [np.ones_like(pos_x), pos_x, pos_y]
    for product in (pos_x * pos_x, pos_x * pos_y, pos_y * pos_y):
        high = product.astype(bf16).astype(np.float64)
        rows += [high, product - high]
    table = np.zeros((pieces, KE, PIX))
    for row_no, row in enumerate(rows * 3):
        table[:, row_no] = row
    return table.astype(bf16)


def basis_coefs(coefs):
    return [coefs[i] for i in (0, 1, 2, 3, 3, 4, 4, 5, 5)]


def lane_order(shape, inverse):
    lane = lax.broadcasted_iota(jnp.int32, shape, 1)
    if inverse:
        return (lane % ROWS) * SUBL + lane // ROWS
    return (lane % SUBL) * ROWS + lane // SUBL


def prefix_product(total):
    sub = lax.broadcasted_iota(jnp.int32, total.shape, 0)
    run = total
    for step in (1, 2, 4):
        run = jnp.where(sub >= step, run * pltpu.roll(run, step, 0), run)
    before = jnp.where(sub >= 1, pltpu.roll(run, 1, 0), 1.0)
    return before, run[SUBL - 1 :]


def suffix_sum(total, behind):
    sub = lax.broadcasted_iota(jnp.int32, total.shape, 0)
    value = total
    for step in (1, 2, 4):
        later = pltpu.roll(value, SUBL - step, 0)
        value = value + jnp.where(sub < SUBL - step, later, 0.0)
    whole = value + behind
    after = jnp.where(sub < SUBL - 1, pltpu.roll(whole, SUBL - 1, 0), behind)
    return after, whole[:1]


def list_items(blocks_ref, live_ref, items_ref, pieces, own_blocks):
    room = pieces + SUBL
    size = 3 * room + 2
    doubles = [jnp.int32(0), jnp.int32(size)]
    singles = [jnp.int32(2 * room), jnp.int32(size + 2 * room)]
    for piece in range(pieces):
        places = []
        for slot in range(2):
            block = blocks_ref[slot, piece]
            places.append(jnp.where(block == 0, own_blocks + 1, block - 1))
        second = live_ref[0, piece] - 1
        edge = jnp.where(second > 0, jnp.maximum(places[0], places[1]), places[0]) >= own_blocks
        double = jnp.where(edge, doubles[1], doubles[0])
        single = jnp.where(edge, singles[1], singles[0])
        entry = places[0] * 64 + piece
        items_ref[double] = entry
        items_ref[room + double] = places[1] * 64 + piece
        items_ref[single] = entry
        edge_second = jnp.where(edge, second, 0)
        edge_first = jnp.where(edge, 1 - second, 0)
        doubles = [doubles[0] + second - edge_second, doubles[1] + edge_second]
        singles = [singles[0] + 1 - second - edge_first, singles[1] + edge_first]
    counts, sizes = [], []
    for which in range(2):
        for spare in range(6):
            items_ref[singles[which] + spare] = (own_blocks + 2) * 64 + pieces
        counts.append(doubles[which] - which * size)
        sizes.append(counts[which] + (singles[which] - which * size - 2 * room + 1) // 2)
    items_ref[size - 2] = counts[0]
    items_ref[size - 1] = counts[1]
    items_ref[2 * size - 2] = sizes[1]
    items_ref[2 * size - 1] = sizes[0] + sizes[1]


def item_ranges(items_ref, pieces):
    size = 3 * (pieces + SUBL) + 2
    return (items_ref[2 * size - 2] + 1) // 2, (items_ref[2 * size - 1] + 1) // 2


def item_slots(items_ref, item, pieces):
    room = pieces + SUBL
    size = 3 * room + 2
    edges = items_ref[2 * size - 2]
    raw = item
    edge = item < edges
    doubles = jnp.where(edge, items_ref[size - 1], items_ref[size - 2])
    base = jnp.where(edge, size, 0)
    item = jnp.where(edge, item, item - edges)
    chained = item < doubles
    single = base + 2 * (room + item - doubles)
    first = items_ref[jnp.where(chained, base + item, single)]
    second = items_ref[jnp.where(chained, base + room + item, single + 1)]
    found = [chained.astype(jnp.int32)]
    for entry in (first, second):
        found += [entry & 63, lax.shift_right_logical(entry, 6)]
    return (*found, raw)


def pipelined(items_ref, pieces, begin, end, multiply, front, back):
    def slots_of(item):
        return item_slots(items_ref, item, pieces)

    first = slots_of(2 * begin)
    front(first, multiply(first), 0)

    def step(pair, carry):
        this, middle, last = carry
        ahead = multiply(middle)
        further = multiply(last)
        back(this, 0)
        front(middle, ahead, 1)
        back(middle, 1)
        front(last, further, 0)
        return last, slots_of(2 * pair + 3), slots_of(2 * pair + 4)

    def two_steps(double, carry):
        pair = begin + 2 * double
        return step(pair + 1, step(pair, carry))

    doubles = (end - begin) // 2
    carry = (first, slots_of(2 * begin + 1), slots_of(2 * begin + 2))
    carry = lax.fori_loop(0, doubles, two_steps, carry)
    lax.fori_loop(begin + 2 * doubles, end, step, carry)


def block_rows(block):
    return pl.ds(pl.multiple_of(block * BLOCK, BLOCK), BLOCK)


def exponents(table_ref, basis_ref, piece, block, pieces):
    unit = basis_ref[jnp.minimum(piece, pieces - 1)]
    rhs = jnp.concatenate([unit, jnp.zeros((KC, PIX), bf16)], axis=0)
    return jnp.dot(table_ref[block_rows(block), :], rhs, preferred_element_type=f32)


def fill_tables(rows, present, places, stage_ref, table_ref, colour_ref):
    coefs, colours = splat_rows(rows)
    shape = (SUBL, LANES)
    order = lane_order(shape, False)

    def settled(value, absent):
        if present is not None:
            value = jnp.where(present, value, absent)
        return jnp.take_along_axis(value, order, axis=1)

    coefs = [settled(value, -1e9 if i == 0 else 0.0) for i, value in enumerate(coefs)]
    colours = [settled(value, 0.0) for value in colours]
    nothing = jnp.zeros(shape, f32)
    parts = basis_coefs([split3(value) for value in coefs])
    lines = [parts[row % BASIS][row // BASIS] for row in range(3 * BASIS)]
    lines += [nothing] * (KE - 3 * BASIS)
    triples = [split3(value) for value in colours]
    for level in (0, 0, 1, 0, 0, 1):
        lines += [triple[level] for triple in triples] + [nothing]
    for row, value in enumerate(lines):
        group, place = divmod(row, SUBL)
        stage_ref[pl.ds(group * SUBL * SUBL + place, SUBL, stride=SUBL), :] = value
    for sublane, block in enumerate(places):
        tiles = [
            stage_ref[(group * SUBL + sublane) * SUBL : (group * SUBL + sublane + 1) * SUBL, :]
            for group in range(len(lines) // SUBL)
        ]
        span = slice(block * BLOCK, (block + 1) * BLOCK)
        table_ref[span, :] = jnp.concatenate(tiles[: KT // SUBL], axis=0).T.astype(bf16)
        colour_ref[block] = jnp.concatenate(tiles[KT // SUBL :] * 2, axis=0).astype(bf16)


def render_items(
    begin, end, items_ref, table_ref, colour_ref, basis_ref, result_ref, saved_refs, scratch
):
    local_refs, before_refs, left_refs = scratch
    alpha_all_ref, weight_all_ref, ends_all_ref = saved_refs
    pieces = basis_ref.shape[0]

    def multiply(found):
        return [
            exponents(table_ref, basis_ref, found[1 + 2 * slot], found[2 + 2 * slot], pieces)
            for slot in range(2)
        ]

    def front(found, powers, side):
        chained = found[0] > 0
        carry = None
        for slot in range(2):
            alphas = jnp.exp2(powers[slot])
            keep = None
            alpha_all_ref[found[5], slot * BLOCK : (slot + 1) * BLOCK, :] = alphas
            for row in range(ROWS):
                alpha = alphas[row * SUBL : (row + 1) * SUBL]
                weight = alpha if keep is None else alpha * keep
                keep = 1.0 - alpha if keep is None else keep - weight
                first = slot * BLOCK + row * SUBL
                local_refs[side][first : first + SUBL, :] = weight
            before, total = prefix_product(keep)
            if slot == 1:
                carry = jnp.where(chained, carry, 1.0)
                before, total = before * carry, total * carry
            carry = total
            before_refs[side][slot * SUBL : (slot + 1) * SUBL, :] = before
            left_refs[side][slot : slot + 1, :] = total
            ends_all_ref[found[5], slot * SUBL : (slot + 1) * SUBL, :] = before * keep

    def back(found, side):
        chained = found[0] > 0
        sums = None
        for slot in range(2):
            piece, block = found[1 + 2 * slot], found[2 + 2 * slot]
            before = before_refs[side][slot * SUBL : (slot + 1) * SUBL, :]
            weights = []
            for row in range(ROWS):
                first = slot * BLOCK + row * SUBL
                weight = local_refs[side][first : first + SUBL, :] * before
                weight_all_ref[found[5], first : first + SUBL, :] = weight
                weights.append(weight)
            high, low = split2(jnp.concatenate(weights, axis=0))
            left = colour_ref[block]
            wide = jnp.dot(left, high, preferred_element_type=f32)
            wide = (wide + jnp.dot(left, low, preferred_element_type=f32))[:SUBL]
            wide = wide + pltpu.roll(wide, 4, 0)
            sums = wide + jnp.where(chained, sums, 0.0) if slot else wide
            row_no = lax.broadcasted_iota(jnp.int32, sums.shape, 0)
            value = jnp.where(row_no == 3, 1.0 - left_refs[side][slot : slot + 1, :], sums)
            for half in range(PIX // LANES):
                first = pl.multiple_of((half * (pieces + 1) + piece) * SUBL, SUBL)
                result_ref[pl.ds(first, SUBL), :] = value[:, half * LANES : (half + 1) * LANES]

    pipelined(items_ref, pieces, begin, end, multiply, front, back)


def forward_kernel(
    far_blocks_ref,
    far_live_ref,
    far_params_ref,
    far_basis_ref,
    far_owner_ref,
    far_cell_ref,
    far_target_ref,
    table_ref,
    colour_ref,
    result_ref,
    basis_ref,
    aimed_ref,
    alpha_all_ref,
    weight_all_ref,
    ends_all_ref,
    items_ref,
    blocks_ref,
    live_ref,
    params_ref,
    owner_ref,
    cell_ref,
    target_ref,
    arrivals,
    rows_ref,
    stage_ref,
    *scratch,
):
    pieces = basis_ref.shape[0]
    own_blocks = params_ref.shape[1] // BLOCK
    moves = (
        (far_blocks_ref, blocks_ref),
        (far_live_ref, live_ref),
        (far_params_ref, params_ref),
        (far_owner_ref, owner_ref),
        (far_cell_ref, cell_ref),
        (far_target_ref, target_ref),
        (far_basis_ref, basis_ref),
    )
    fetches = [
        pltpu.make_async_copy(far, near, arrivals.at[i]) for i, (far, near) in enumerate(moves)
    ]
    for fetch in fetches:
        fetch.start()
    for fetch in fetches[:3]:
        fetch.wait()
    list_items(blocks_ref, live_ref, items_ref, pieces, own_blocks)
    for block in range(own_blocks):
        rows_ref[pl.ds(block, PARAMS, stride=SUBL), :] = params_ref[
            :, block * BLOCK : (block + 1) * BLOCK
        ]
    rows = [rows_ref[i * SUBL : (i + 1) * SUBL, :] for i in range(PARAMS)]
    fill_tables(rows, None, range(own_blocks), stage_ref, table_ref, colour_ref)
    empty = own_blocks + 2
    column = lax.broadcasted_iota(jnp.int32, (BLOCK, KT), 1)
    table_ref[empty * BLOCK : (empty + 1) * BLOCK, :] = jnp.where(column == 0, -1e9, 0.0).astype(
        bf16
    )
    colour_ref[empty] = jnp.zeros((TOP, LANES), bf16)
    for fetch in fetches[3:]:
        fetch.wait()
    doms = aimed_ref.shape[0]
    width, tiles = PIX // doms, target_ref.shape[1]
    tile_lane = lax.broadcasted_iota(jnp.int32, (SUBL, LANES), 1)
    cell = cell_ref[...]
    labels = (cell % MAXD) * (doms * tiles) + owner_ref[...] * tiles + cell // MAXD
    labels = jnp.concatenate(
        [jnp.zeros((1, LANES - pieces), f32), labels.astype(f32)], axis=1
    )
    labels = jnp.broadcast_to(labels, (SUBL, LANES))
    for dom in range(doms):
        half, offset = divmod(dom * width, LANES)
        span = slice(half * LANES, (half + 1) * LANES)
        aimed = labels
        for channel in (2, 1, 0):
            shift = (channel * GROUP - offset) % LANES
            value = target_ref[channel, :, span]
            value = pltpu.roll(value, shift, 1) if shift else value
            aimed = jnp.where(tile_lane < (channel + 1) * GROUP, value, aimed)
        aimed_ref[dom] = aimed
    edge_pairs, pairs = item_ranges(items_ref, pieces)
    saved = (alpha_all_ref, weight_all_ref, ends_all_ref)
    render_items(edge_pairs, pairs, items_ref, table_ref, colour_ref, basis_ref, result_ref, saved, scratch)


def forward_edge_kernel(
    items_ref,
    inner_ref,
    outer_ref,
    aimed_ref,
    basis_ref,
    *refs,
):
    table_ref, colour_ref, result_ref, *saved, out_ref, rows_ref, stage_ref = refs[6:15]
    scratch = refs[15:]
    doms, pieces = out_ref.shape[0], basis_ref.shape[0]
    own_blocks = table_ref.shape[0] // BLOCK - 3
    region_idx, regions = lax.axis_index("region"), lax.axis_size("region")
    even = region_idx % 2 == 0
    inner, outer = inner_ref[...], outer_ref[...]
    rows_ref[pl.ds(0, PARAMS, stride=SUBL), :] = jnp.where(even, inner, outer)
    rows_ref[pl.ds(1, PARAMS, stride=SUBL), :] = jnp.where(even, outer, inner)
    rows = [rows_ref[i * SUBL : (i + 1) * SUBL, :] for i in range(PARAMS)]
    sublane = lax.broadcasted_iota(jnp.int32, (SUBL, LANES), 0)
    present = ((sublane == 0) & (region_idx < regions - 1)) | ((sublane == 1) & (region_idx > 0))
    places = (own_blocks, own_blocks + 1)
    fill_tables(rows, present, places, stage_ref, table_ref, colour_ref)
    render_items(0, item_ranges(items_ref, pieces)[0], items_ref, table_ref, colour_ref, basis_ref, result_ref, saved, scratch)
    width = PIX // doms
    lane = lax.broadcasted_iota(jnp.int32, (pieces, LANES), 1)
    tiles = aimed_ref.shape[1]
    for dom in range(doms):
        half, offset = divmod(dom * width, LANES)
        packed = None
        for channel in range(4):
            shift = (channel * GROUP - offset) % LANES
            first = half * (pieces + 1) * SUBL + channel
            value = result_ref[pl.ds(first, pieces, stride=SUBL), :]
            value = pltpu.roll(value, shift, 1) if shift else value
            packed = value if packed is None else jnp.where(lane >= channel * GROUP, value, packed)
        out_ref[dom, :pieces, :] = packed
        out_ref[dom, pieces : pieces + tiles, :] = aimed_ref[dom]


def composite_kernel(background_ref, arrived_ref, out_ref):
    doms, pieces = out_ref.shape[0], out_ref.shape[1]
    tiles = arrived_ref.shape[1] - pieces
    all_pieces, all_tiles = doms * pieces, doms * tiles
    per_row = LANES // GROUP
    lane = lax.broadcasted_iota(jnp.int32, (1, LANES), 1)
    label_rows = []
    for dom in range(doms):
        place = dom % per_row
        value = arrived_ref[dom, pieces : pieces + 1, :]
        shift = ((place - 3) * GROUP) % LANES
        value = pltpu.roll(value, shift, 1) if shift else value
        if place == 0:
            label_rows.append(value)
        else:
            label_rows[-1] = jnp.where(lane >= place * GROUP, value, label_rows[-1])
    cells_all = MAXD * all_tiles
    cell_no = lax.broadcasted_iota(jnp.int32, (cells_all, LANES), 0).astype(f32)
    to_cells = jnp.concatenate(
        [jnp.where(cell_no == row, 1.0, 0.0).astype(bf16) for row in label_rows], axis=1
    )
    upright = jnp.concatenate([jnp.broadcast_to(row, (SUBL, LANES)).T for row in label_rows], axis=0)
    cell_no = lax.broadcasted_iota(jnp.int32, (all_pieces, cells_all), 1).astype(f32)
    to_pieces = jnp.where(cell_no == upright[:, :1], 1.0, 0.0).astype(bf16)

    def moved(matrix, values):
        wide = jnp.dot(
            matrix, jnp.concatenate(split2(values), axis=1), preferred_element_type=f32
        )
        return wide[:, :LANES] + wide[:, LANES:]

    data = arrived_ref[:, :pieces, :].reshape(all_pieces, LANES)
    cells = moved(to_cells, data)
    goal = arrived_ref[:, pieces:, :].reshape(all_tiles, LANES)
    lane = lax.broadcasted_iota(jnp.int32, (all_tiles, LANES), 1)
    last = lane >= 3 * GROUP
    backdrop = jnp.where(
        lane < GROUP,
        background_ref[0],
        jnp.where(lane < 2 * GROUP, background_ref[1], background_ref[2]),
    )

    def spread(value):
        return pltpu.roll(value, GROUP, 1) + pltpu.roll(value, 2 * GROUP, 1) + pltpu.roll(
            value, 3 * GROUP, 1
        )

    fronts, through, layers = [], [], []
    front = jnp.ones((all_tiles, LANES), f32)
    composite = jnp.zeros((all_tiles, LANES), f32)
    for depth in range(MAXD):
        layer = cells[depth * all_tiles : (depth + 1) * all_tiles]
        passed = jnp.where(last, 1.0 - layer, 0.0)
        passed = passed + spread(passed)
        fronts.append(front)
        through.append(passed)
        layers.append(layer)
        composite = composite + front * layer
        front = front * passed
    residual = jnp.where(last, 0.0, composite + front * backdrop - goal)
    behind = backdrop
    grads = [None] * MAXD
    for depth in reversed(range(MAXD)):
        grads[depth] = fronts[depth] * jnp.where(last, spread(residual * behind), residual)
        behind = layers[depth] + through[depth] * behind
    back = moved(to_pieces, jnp.concatenate(grads, axis=0))
    out_ref[...] = back.reshape(out_ref.shape)


def pull_items(
    begin, end, items_ref, table_ref, basis_ref, grad_ref, sums_ref, saved_refs, scratch
):
    shade_refs, hidden_refs = scratch
    alpha_all_ref, weight_all_ref, ends_all_ref = saved_refs
    pieces = basis_ref.shape[0]

    def grads_of(piece):
        halves = []
        for half in range(PIX // LANES):
            first = pl.multiple_of((half * (pieces + 1) + piece) * SUBL, SUBL)
            halves.append(grad_ref[pl.ds(first, SUBL), :])
        grads = jnp.concatenate(halves, axis=1)
        upper = lax.broadcasted_iota(jnp.int32, grads.shape, 0) < 4
        high, middle, low = split3(grads)
        first = jnp.where(upper, high, pltpu.roll(middle, 4, 0))
        return grads, first, jnp.where(upper, high, pltpu.roll(low, 4, 0))

    def multiply(found):
        products = []
        for slot in range(2):
            piece, block = found[1 + 2 * slot], found[2 + 2 * slot]
            grads, first, second = grads_of(piece)
            rhs = jnp.concatenate([first, second], axis=0).astype(bf16)
            rhs = jnp.concatenate([jnp.zeros((KE, PIX), bf16), rhs], axis=0)
            shades = jnp.dot(table_ref[block_rows(block), :], rhs, preferred_element_type=f32)
            products.append((shades, grads[3:4]))
        return products

    def front(found, products, side):
        chained, item = found[0] > 0, found[5]
        ends = []
        for slot, (shades, final) in enumerate(products):
            span = slice(slot * BLOCK, (slot + 1) * BLOCK)
            shade_refs[side][span, :] = shades
            total = None
            for row in range(ROWS):
                first = slot * BLOCK + row * SUBL
                value = weight_all_ref[item, first : first + SUBL, :] * shades[
                    row * SUBL : (row + 1) * SUBL
                ]
                total = value if total is None else total + value
            left = ends_all_ref[item, slot * SUBL : (slot + 1) * SUBL, :]
            ends.append((total, left, final * left[SUBL - 1 :]))
        behind = None
        for slot in (1, 0):
            total, left, final = ends[slot]
            behind = jnp.where(chained, behind, final) if slot == 0 else final
            hidden, behind = suffix_sum(total, behind)
            hidden = hidden / left
            hidden_refs[side][slot * SUBL : (slot + 1) * SUBL, :] = hidden

    def back(found, side):
        along = (((1,), (1,)), ((), ()))
        for slot in range(2):
            piece, block = found[1 + 2 * slot], found[2 + 2 * slot]
            hidden = hidden_refs[side][slot * SUBL : (slot + 1) * SUBL, :]
            pulls, weights = [None] * ROWS, [None] * ROWS
            for row in reversed(range(ROWS)):
                first = slot * BLOCK + row * SUBL
                span = slice(first, first + SUBL)
                weight = weight_all_ref[found[5], span, :]
                gap = shade_refs[side][span, :] - hidden
                weights[row] = weight
                pulls[row] = weight * gap
                hidden = hidden + alpha_all_ref[found[5], span, :] * gap
            unit = basis_ref[jnp.minimum(piece, pieces - 1)][:TOP]
            _, first, second = grads_of(piece)
            g_lhs = jnp.concatenate([first, second], axis=0).astype(bf16)
            for base, left, values in ((0, unit, pulls), (2, g_lhs, weights)):
                part = None
                for value in split2(jnp.concatenate(values, axis=0)):
                    product = lax.dot_general(left, value, along, preferred_element_type=f32)
                    part = product if part is None else part + product
                for group in range(2 if base == 0 else 1):
                    row = (base + group) * SLOTS * SUBL + block * SUBL
                    rows = pl.ds(pl.multiple_of(row, SUBL), SUBL)
                    sums_ref[rows, :] = (
                        sums_ref[rows, :] + part[group * SUBL : (group + 1) * SUBL]
                    )

    pipelined(items_ref, pieces, begin, end, multiply, front, back)


def early_pairs(items_ref, pieces):
    edge_pairs, pairs = item_ranges(items_ref, pieces)
    return jnp.minimum(jnp.maximum(edge_pairs, pieces * 3 // 16), pairs), pairs


def summed_terms(sums_ref):
    def rows_of(row):
        group, place = divmod(row, SUBL)
        return sums_ref[pl.ds(group * SLOTS * SUBL + place, SLOTS, stride=SUBL), :]

    moments = [rows_of(0), rows_of(1), rows_of(2)]
    moments += [rows_of(3 + 2 * i) + rows_of(4 + 2 * i) for i in range(3)]
    terms = [value * ln_2 for value in moments]
    terms += [rows_of(TOP + i) + rows_of(TOP + 4 + i) for i in range(3)]
    order = lane_order((SLOTS, LANES), True)
    return [jnp.take_along_axis(value, order, axis=1) for value in terms]


def backward_edge_kernel(
    items_ref,
    back_ref,
    table_ref,
    basis_ref,
    alpha_all_ref,
    weight_all_ref,
    ends_all_ref,
    grad_ref,
    sums_ref,
    inner_ref,
    outer_ref,
    *scratch,
):
    doms, pieces = back_ref.shape[0], back_ref.shape[1]
    own_blocks = table_ref.shape[0] // BLOCK - 3
    width = PIX // doms
    lane = lax.broadcasted_iota(jnp.int32, (pieces, LANES), 1)
    grad_ref[...] = jnp.zeros_like(grad_ref)
    sums_ref[...] = jnp.zeros_like(sums_ref)
    for half in range(PIX // LANES):
        for channel in range(4):
            gathered = None
            for dom in range(half * LANES // width, (half + 1) * LANES // width):
                offset = dom * width - half * LANES
                shift = (offset - channel * GROUP) % LANES
                value = back_ref[dom]
                value = pltpu.roll(value, shift, 1) if shift else value
                gathered = value if gathered is None else jnp.where(lane >= offset, value, gathered)
            first = half * (pieces + 1) * SUBL + channel
            grad_ref[pl.ds(first, pieces, stride=SUBL), :] = gathered

    early, _ = early_pairs(items_ref, pieces)
    saved = (alpha_all_ref, weight_all_ref, ends_all_ref)
    pull_items(0, early, items_ref, table_ref, basis_ref, grad_ref, sums_ref, saved, scratch)
    even = lax.axis_index("region") % 2 == 0
    inner_ref[...] = jnp.zeros_like(inner_ref)
    outer_ref[...] = jnp.zeros_like(outer_ref)
    for term_no, value in enumerate(summed_terms(sums_ref)):
        high = value[own_blocks : own_blocks + 1]
        low = value[own_blocks + 1 : own_blocks + 2]
        inner_ref[term_no : term_no + 1, :] = jnp.where(even, high, low)
        outer_ref[term_no : term_no + 1, :] = jnp.where(even, low, high)


def backward_kernel(
    items_ref, table_ref, basis_ref, grad_ref, edge_sums_ref, *refs
):
    saved, own_ref, sums_ref, scratch = refs[:3], refs[3], refs[4], refs[5:]
    sums_ref[...] = edge_sums_ref[...]
    early, pairs = early_pairs(items_ref, basis_ref.shape[0])
    pull_items(
        early, pairs, items_ref, table_ref, basis_ref, grad_ref, sums_ref, saved, scratch
    )
    for term_no, value in enumerate(summed_terms(sums_ref)):
        own_ref[term_no] = value[: own_ref.shape[1]]


def update_kernel(
    params_ref,
    first_ref,
    second_ref,
    own_ref,
    inner_ref,
    outer_ref,
    gradient_ref,
    new_params_ref,
    new_first_ref,
    new_second_ref,
    rows_ref,
    grads_ref,
):
    own_blocks = own_ref.shape[1]
    for block in range(own_blocks):
        rows_ref[pl.ds(block, PARAMS, stride=own_blocks), :] = params_ref[
            :, block * BLOCK : (block + 1) * BLOCK
        ]
    rows = [rows_ref[i * own_blocks : (i + 1) * own_blocks, :] for i in range(PARAMS)]
    slot = lax.broadcasted_iota(jnp.int32, (own_blocks, LANES), 0)
    even = lax.axis_index("region") % 2 == 0
    from_low = jnp.where(even, outer_ref[...], inner_ref[...])
    from_high = jnp.where(even, inner_ref[...], outer_ref[...])
    cots = []
    for term_no in range(9):
        low = jnp.where(slot == 0, from_low[term_no : term_no + 1, :], 0.0)
        high = jnp.where(slot == own_blocks - 1, from_high[term_no : term_no + 1, :], 0.0)
        cots.append(own_ref[term_no] + low + high)
    _, pull_back = jax.vjp(splat_rows, rows)
    pulled = pull_back((cots[:6], cots[6:]))[0]
    for i in range(PARAMS):
        grads_ref[i * own_blocks : (i + 1) * own_blocks, :] = pulled[i]
    for block in range(own_blocks):
        span = slice(block * BLOCK, (block + 1) * BLOCK)
        gradient = grads_ref[pl.ds(block, PARAMS, stride=own_blocks), :]
        new_first = beta_one * first_ref[:, span] + (1 - beta_one) * gradient
        new_second = beta_two * second_ref[:, span] + (1 - beta_two) * gradient * gradient
        update = (
            new_first
            / (1 - beta_one**adam_step)
            / (jnp.sqrt(new_second / (1 - beta_two**adam_step)) + tiny)
        )
        gradient_ref[:, span] = gradient
        new_params_ref[:, span] = params_ref[:, span] - rate * update
        new_first_ref[:, span] = new_first
        new_second_ref[:, span] = new_second


def exchange(to_inner, to_outer):
    count = lax.axis_size("region")
    inner = [(i, i ^ 1) for i in range(count) if (i ^ 1) < count]
    outer = [(i, i + 1) for i in range(1, count - 1, 2)]
    outer += [(target, source) for source, target in outer]
    near = lax.ppermute(to_inner, "region", inner)
    far = lax.ppermute(to_outer, "region", outer)
    return near, far


def on_device(
    params,
    first_moment,
    second_moment,
    piece_blocks,
    piece_live,
    piece_owner,
    piece_cell,
    target,
    background,
):
    own_blocks = params.shape[1] // BLOCK
    doms = lax.axis_size("dom")
    pieces = piece_live.shape[1]
    tiles = target.shape[1]
    even = lax.axis_index("region") % 2 == 0
    low, high = params[:, :BLOCK], params[:, -BLOCK:]
    inner, outer = exchange(jnp.where(even, high, low), jnp.where(even, low, high))
    basis = jnp.asarray(pixel_basis(pieces))
    smem = pl.BlockSpec(memory_space=pltpu.SMEM)
    vmem = pl.BlockSpec(memory_space=pltpu.VMEM)
    plane = pltpu.VMEM((2 * BLOCK, PIX), f32)
    strip = pltpu.VMEM((2 * SUBL, PIX), f32)
    piece_rows = (PIX // LANES * (pieces + 1) * SUBL, LANES)
    sums_shape = (3 * SLOTS * SUBL, LANES)
    table_shape = jax.ShapeDtypeStruct(((own_blocks + 3) * BLOCK, KT), bf16)
    colour_shape = jax.ShapeDtypeStruct((own_blocks + 3, TOP, LANES), bf16)
    result_shape = jax.ShapeDtypeStruct(piece_rows, f32)
    forward_scratch = [
        pltpu.VMEM((64 * SUBL, LANES), f32),
        pltpu.VMEM(((KT // SUBL + 1) * SUBL * SUBL, LANES), f32),
        [plane] * 2,
        [strip] * 2,
        [strip] * 2,
    ]
    backward_scratch = [[plane] * 2, [strip] * 2]
    saved_shapes = tuple(
        jax.ShapeDtypeStruct((pieces + 4, rows, PIX), f32)
        for rows in (2 * BLOCK, 2 * BLOCK, 2 * SUBL)
    )
    params_limit = pltpu.CompilerParams(vmem_limit_bytes=vmem_limit)
    table, colour, result, basis, aimed, *saved, items = pl.pallas_call(
        forward_kernel,
        out_shape=(
            table_shape,
            colour_shape,
            result_shape,
            jax.ShapeDtypeStruct(basis.shape, bf16),
            jax.ShapeDtypeStruct((doms, tiles, LANES), f32),
            *saved_shapes,
            jax.ShapeDtypeStruct((2 * (3 * (pieces + SUBL) + 2),), jnp.int32),
        ),
        in_specs=[pl.BlockSpec(memory_space=pltpu.HBM)] * 7,
        out_specs=(vmem,) * 8 + (smem,),
        scratch_shapes=[
            pltpu.SMEM((2, pieces), jnp.int32),
            pltpu.SMEM((1, pieces), jnp.int32),
            pltpu.VMEM(params.shape, f32),
            pltpu.VMEM((1, pieces), jnp.int32),
            pltpu.VMEM((1, pieces), jnp.int32),
            pltpu.VMEM((3, tiles, PIX), f32),
            pltpu.SemaphoreType.DMA((7,)),
        ]
        + forward_scratch,
        compiler_params=params_limit,
        name="forward",
    )(
        *[
            pltpu.with_memory_space_constraint(value, pltpu.HBM)
            for value in (
                piece_blocks[0].T,
                piece_live,
                params,
                basis,
                piece_owner,
                piece_cell,
                jnp.transpose(target[0], (1, 0, 2)),
            )
        ]
    )
    table, _, _, *saved, payload = pl.pallas_call(
        forward_edge_kernel,
        out_shape=(
            table_shape,
            colour_shape,
            result_shape,
            *saved_shapes,
            jax.ShapeDtypeStruct((doms, pieces + tiles, LANES), f32),
        ),
        in_specs=[smem] + [vmem] * 10,
        out_specs=(vmem,) * 7,
        scratch_shapes=forward_scratch,
        input_output_aliases={5 + i: i for i in range(6)},
        compiler_params=params_limit,
        name="forward_edge",
    )(
        items,
        inner,
        outer,
        aimed,
        basis,
        table,
        colour,
        result,
        *saved,
    )
    arrived = lax.all_to_all(payload, "dom", split_axis=0, concat_axis=0, tiled=True)
    back = pl.pallas_call(
        composite_kernel,
        out_shape=jax.ShapeDtypeStruct((doms, pieces, LANES), f32),
        in_specs=[smem, vmem],
        out_specs=vmem,
        compiler_params=params_limit,
        name="composite",
    )(background, arrived)
    returned = lax.all_to_all(back, "dom", split_axis=0, concat_axis=0, tiled=True)
    grads, edge_sums, to_inner, to_outer = pl.pallas_call(
        backward_edge_kernel,
        out_shape=(
            result_shape,
            jax.ShapeDtypeStruct(sums_shape, f32),
            jax.ShapeDtypeStruct((SLOTS, LANES), f32),
            jax.ShapeDtypeStruct((SLOTS, LANES), f32),
        ),
        in_specs=[smem] + [vmem] * 6,
        out_specs=(vmem,) * 4,
        scratch_shapes=backward_scratch,
        compiler_params=params_limit,
        name="backward_edge",
    )(items, returned, table, basis, *saved)
    inner, outer = exchange(to_inner, to_outer)
    own = pl.pallas_call(
        backward_kernel,
        out_shape=jax.ShapeDtypeStruct((9, own_blocks, LANES), f32),
        in_specs=[smem] + [vmem] * 7,
        out_specs=vmem,
        scratch_shapes=[pltpu.VMEM(sums_shape, f32)] + backward_scratch,
        compiler_params=params_limit,
        name="backward",
    )(items, table, basis, grads, edge_sums, *saved)
    shape = jax.ShapeDtypeStruct(params.shape, f32)
    return pl.pallas_call(
        update_kernel,
        out_shape=(shape, shape, shape, shape),
        in_specs=[vmem] * 6,
        out_specs=(vmem,) * 4,
        scratch_shapes=[
            pltpu.VMEM((64 * own_blocks, LANES), f32),
            pltpu.VMEM((64 * own_blocks, LANES), f32),
        ],
        name="update",
        compiler_params=pltpu.CompilerParams(vmem_limit_bytes=vmem_limit),
    )(params, first_moment, second_moment, own, inner, outer)


def solution(mesh):
    in_specs = (
        P(None, ("region", "dom")),
        P(None, ("region", "dom")),
        P(None, ("region", "dom")),
        P(("region", "dom"), None, None),
        P(("region", "dom"), None),
        P(("region", "dom"), None),
        P(("region", "dom"), None),
        P(("region", "dom"), None, None, None),
        P(),
    )
    out_specs = (P(None, ("region", "dom")),) * 4
    return jax.shard_map(
        on_device, mesh=mesh, in_specs=in_specs, out_specs=out_specs, check_vma=False
    )
```

```python
import math

import numpy as np
import jax
import jax.numpy as jnp
from jax import lax
from jax.experimental import pallas as pl
from jax.experimental.pallas import tpu as pltpu
from jax.sharding import PartitionSpec as P

PARAMS = 59
TSIDE = 16
WIN = 8
BLOCK = 128
MAXD = 8
PIX = 256

harmonic_zero = 0.28209479177387814
harmonic_one = 0.4886025119029199
harmonic_two = (
    1.0925484305920792,
    -1.0925484305920792,
    0.31539156525252005,
    -1.0925484305920792,
    0.5462742152960396,
)
harmonic_three = (
    -0.5900435899266435,
    2.890611442640554,
    -0.4570457994644658,
    0.3731763325901154,
    -0.4570457994644658,
    1.445305721320277,
    -0.5900435899266435,
)
beta_one = 0.9
beta_two = 0.999
rate = 0.001
adam_step = 100
tiny = 1e-08
log2_e = math.log2(math.e)
ln_2 = math.log(2.0)

LANES = 128
SUBL = 8
ROWS = BLOCK // SUBL
FORWARD_STEPS = 4
BACKWARD_STEPS = 3
GROUP = LANES // 4
BASIS = 9
KE = 32
KC = 2 * SUBL
KT = KE + KC
TOP = 16
SLOTS = 16
vmem_limit = 12 * 2**20
f32 = jnp.float32
bf16 = jnp.bfloat16


def splat_rows(rows):
    mean_x, mean_y, mean_z = rows[0], rows[1], rows[2]
    scales = [jnp.exp(rows[3]), jnp.exp(rows[4]), jnp.exp(rows[5])]
    norm_sq = rows[6] * rows[6] + rows[7] * rows[7] + rows[8] * rows[8] + rows[9] * rows[9]
    inv_norm = 1.0 / jnp.sqrt(norm_sq)
    quat_w, quat_x, quat_y, quat_z = [rows[6 + i] * inv_norm for i in range(4)]
    rotation = [
        [
            1 - 2 * (quat_y * quat_y + quat_z * quat_z),
            2 * (quat_x * quat_y - quat_w * quat_z),
            2 * (quat_x * quat_z + quat_w * quat_y),
        ],
        [
            2 * (quat_x * quat_y + quat_w * quat_z),
            1 - 2 * (quat_x * quat_x + quat_z * quat_z),
            2 * (quat_y * quat_z - quat_w * quat_x),
        ],
        [
            2 * (quat_x * quat_z - quat_w * quat_y),
            2 * (quat_y * quat_z + quat_w * quat_x),
            1 - 2 * (quat_x * quat_x + quat_y * quat_y),
        ],
    ]
    focal_px = 0.3125 * float(WIN * TSIDE)
    inv_z = 1.0 / mean_z
    scale_z = focal_px * inv_z
    off_u = scale_z * mean_x
    off_v = scale_z * mean_y
    slope_u = off_u * inv_z
    slope_v = off_v * inv_z
    proj_u = [(scale_z * rotation[0][i] - slope_u * rotation[2][i]) * scales[i] for i in range(3)]
    proj_v = [(scale_z * rotation[1][i] - slope_v * rotation[2][i]) * scales[i] for i in range(3)]
    sigma_xx = proj_u[0] * proj_u[0] + proj_u[1] * proj_u[1] + proj_u[2] * proj_u[2] + 0.3
    sigma_xy = proj_u[0] * proj_v[0] + proj_u[1] * proj_v[1] + proj_u[2] * proj_v[2]
    sigma_yy = proj_v[0] * proj_v[0] + proj_v[1] * proj_v[1] + proj_v[2] * proj_v[2] + 0.3
    determinant = sigma_xx * sigma_yy - sigma_xy * sigma_xy
    inv_det = log2_e / determinant
    con_xx = sigma_yy * inv_det
    con_xy = -sigma_xy * inv_det
    con_yy = sigma_xx * inv_det
    lin_x = con_xx * off_u + con_xy * off_v
    lin_y = con_xy * off_u + con_yy * off_v
    logit = rows[10]
    log_opacity = (logit - jnp.log(1.0 + jnp.exp(logit))) * log2_e
    const = log_opacity - 0.5 * (lin_x * off_u + lin_y * off_v)
    coefs = [const, lin_x, lin_y, -0.5 * con_xx, -con_xy, -0.5 * con_yy]
    inv_len = 1.0 / jnp.sqrt(mean_x * mean_x + mean_y * mean_y + mean_z * mean_z)
    dir_x, dir_y, dir_z = mean_x * inv_len, mean_y * inv_len, mean_z * inv_len
    sq_x, sq_y, sq_z = dir_x * dir_x, dir_y * dir_y, dir_z * dir_z
    harmonics = [
        None,
        -harmonic_one * dir_y,
        harmonic_one * dir_z,
        -harmonic_one * dir_x,
        harmonic_two[0] * dir_x * dir_y,
        harmonic_two[1] * dir_y * dir_z,
        harmonic_two[2] * (2 * sq_z - sq_x - sq_y),
        harmonic_two[3] * dir_x * dir_z,
        harmonic_two[4] * (sq_x - sq_y),
        harmonic_three[0] * dir_y * (3 * sq_x - sq_y),
        harmonic_three[1] * dir_x * dir_y * dir_z,
        harmonic_three[2] * dir_y * (4 * sq_z - sq_x - sq_y),
        harmonic_three[3] * dir_z * (2 * sq_z - 3 * sq_x - 3 * sq_y),
        harmonic_three[4] * dir_x * (4 * sq_z - sq_x - sq_y),
        harmonic_three[5] * dir_z * (sq_x - sq_y),
        harmonic_three[6] * dir_x * (sq_x - 3 * sq_y),
    ]
    colours = []
    for colour_no in range(3):
        base = 11 + 16 * colour_no
        total = rows[base] * harmonic_zero
        for k in range(1, 16):
            total = total + rows[base + k] * harmonics[k]
        colours.append(jnp.maximum(total + 0.5, 0.0))
    return coefs, colours


def split3(value):
    high = value.astype(bf16).astype(f32)
    rest = value - high
    middle = rest.astype(bf16).astype(f32)
    return high, middle, rest - middle


def split2(value):
    high = value.astype(bf16)
    return high, (value - high.astype(f32)).astype(bf16)


def pixel_basis(pieces):
    tiles = np.arange(pieces)[:, None]
    pixels = np.arange(PIX)[None, :]
    half = WIN * TSIDE / 2
    pos_x = TSIDE * (tiles % WIN) + pixels % TSIDE + 0.5 - half
    pos_y = TSIDE * (tiles // WIN) + pixels // TSIDE + 0.5 - half
    rows = [np.ones_like(pos_x), pos_x, pos_y]
    for product in (pos_x * pos_x, pos_x * pos_y, pos_y * pos_y):
        high = product.astype(bf16).astype(np.float64)
        rows += [high, product - high]
    table = np.zeros((pieces, KE, PIX))
    for row_no, row in enumerate(rows * 3):
        table[:, row_no] = row
    return table.astype(bf16)


def basis_coefs(coefs):
    return [coefs[i] for i in (0, 1, 2, 3, 3, 4, 4, 5, 5)]


def lane_order(shape, inverse):
    lane = lax.broadcasted_iota(jnp.int32, shape, 1)
    if inverse:
        return (lane % ROWS) * SUBL + lane // ROWS
    return (lane % SUBL) * ROWS + lane // SUBL


def prefix_product(total):
    sub = lax.broadcasted_iota(jnp.int32, total.shape, 0)
    run = total
    for step in (1, 2, 4):
        run = jnp.where(sub >= step, run * pltpu.roll(run, step, 0), run)
    before = jnp.where(sub >= 1, pltpu.roll(run, 1, 0), 1.0)
    return before, run[SUBL - 1 :]


def suffix_sum(total, behind):
    sub = lax.broadcasted_iota(jnp.int32, total.shape, 0)
    value = total
    for step in (1, 2, 4):
        later = pltpu.roll(value, SUBL - step, 0)
        value = value + jnp.where(sub < SUBL - step, later, 0.0)
    whole = value + behind
    after = jnp.where(sub < SUBL - 1, pltpu.roll(whole, SUBL - 1, 0), behind)
    return after, whole[:1]


def list_items(blocks_ref, live_ref, items_ref, pieces, own_blocks):
    room = pieces + SUBL
    size = 3 * room + 2
    doubles = [jnp.int32(0), jnp.int32(size)]
    singles = [jnp.int32(2 * room), jnp.int32(size + 2 * room)]
    for piece in range(pieces):
        places = []
        for slot in range(2):
            block = blocks_ref[slot, piece]
            places.append(jnp.where(block == 0, own_blocks + 1, block - 1))
        second = live_ref[0, piece] - 1
        edge = jnp.where(second > 0, jnp.maximum(places[0], places[1]), places[0]) >= own_blocks
        double = jnp.where(edge, doubles[1], doubles[0])
        single = jnp.where(edge, singles[1], singles[0])
        entry = places[0] * 64 + piece
        items_ref[double] = entry
        items_ref[room + double] = places[1] * 64 + piece
        items_ref[single] = entry
        edge_second = jnp.where(edge, second, 0)
        edge_first = jnp.where(edge, 1 - second, 0)
        doubles = [doubles[0] + second - edge_second, doubles[1] + edge_second]
        singles = [singles[0] + 1 - second - edge_first, singles[1] + edge_first]
    counts, sizes = [], []
    for which in range(2):
        for spare in range(6):
            items_ref[singles[which] + spare] = (own_blocks + 2) * 64 + pieces
        counts.append(doubles[which] - which * size)
        sizes.append(counts[which] + (singles[which] - which * size - 2 * room + 1) // 2)
    items_ref[size - 2] = counts[0]
    items_ref[size - 1] = counts[1]
    items_ref[2 * size - 2] = sizes[1]
    items_ref[2 * size - 1] = sizes[0] + sizes[1]


def item_ranges(items_ref, pieces):
    size = 3 * (pieces + SUBL) + 2
    return (items_ref[2 * size - 2] + 1) // 2, (items_ref[2 * size - 1] + 1) // 2


def item_slots(items_ref, item, pieces):
    room = pieces + SUBL
    size = 3 * room + 2
    edges = items_ref[2 * size - 2]
    raw = item
    edge = item < edges
    doubles = jnp.where(edge, items_ref[size - 1], items_ref[size - 2])
    base = jnp.where(edge, size, 0)
    item = jnp.where(edge, item, item - edges)
    chained = item < doubles
    single = base + 2 * (room + item - doubles)
    first = items_ref[jnp.where(chained, base + item, single)]
    second = items_ref[jnp.where(chained, base + room + item, single + 1)]
    found = [chained.astype(jnp.int32)]
    for entry in (first, second):
        found += [entry & 63, lax.shift_right_logical(entry, 6)]
    return (*found, raw)


def pipelined(items_ref, pieces, begin, end, steps, multiply, front, back):
    def slots_of(item):
        return item_slots(items_ref, item, pieces)

    first = slots_of(2 * begin)
    front(first, multiply(first), 0)

    def step(pair, carry):
        this, middle, last = carry
        ahead = multiply(middle)
        further = multiply(last)
        back(this, 0)
        front(middle, ahead, 1)
        back(middle, 1)
        front(last, further, 0)
        return last, slots_of(2 * pair + 3), slots_of(2 * pair + 4)

    def long_step(number, carry):
        for inner in range(steps):
            carry = step(begin + steps * number + inner, carry)
        return carry

    longs = (end - begin) // steps
    carry = (first, slots_of(2 * begin + 1), slots_of(2 * begin + 2))
    carry = lax.fori_loop(0, longs, long_step, carry)
    lax.fori_loop(begin + steps * longs, end, step, carry)


def block_rows(block):
    return pl.ds(pl.multiple_of(block * BLOCK, BLOCK), BLOCK)


def exponents(table_ref, basis_ref, piece, block, pieces):
    unit = basis_ref[jnp.minimum(piece, pieces - 1)]
    rhs = jnp.concatenate([unit, jnp.zeros((KC, PIX), bf16)], axis=0)
    return jnp.dot(table_ref[block_rows(block), :], rhs, preferred_element_type=f32)


def fill_tables(rows, present, places, stage_ref, table_ref, colour_ref):
    coefs, colours = splat_rows(rows)
    shape = (SUBL, LANES)
    order = lane_order(shape, False)

    def settled(value, absent):
        if present is not None:
            value = jnp.where(present, value, absent)
        return jnp.take_along_axis(value, order, axis=1)

    coefs = [settled(value, -1e9 if i == 0 else 0.0) for i, value in enumerate(coefs)]
    colours = [settled(value, 0.0) for value in colours]
    nothing = jnp.zeros(shape, f32)
    parts = basis_coefs([split3(value) for value in coefs])
    lines = [parts[row % BASIS][row // BASIS] for row in range(3 * BASIS)]
    lines += [nothing] * (KE - 3 * BASIS)
    triples = [split3(value) for value in colours]
    for level in (0, 0, 1, 0, 0, 1):
        lines += [triple[level] for triple in triples] + [nothing]
    for row, value in enumerate(lines):
        group, place = divmod(row, SUBL)
        stage_ref[pl.ds(group * SUBL * SUBL + place, SUBL, stride=SUBL), :] = value
    for sublane, block in enumerate(places):
        tiles = [
            stage_ref[(group * SUBL + sublane) * SUBL : (group * SUBL + sublane + 1) * SUBL, :]
            for group in range(len(lines) // SUBL)
        ]
        span = slice(block * BLOCK, (block + 1) * BLOCK)
        table_ref[span, :] = jnp.concatenate(tiles[: KT // SUBL], axis=0).T.astype(bf16)
        colour_ref[block] = jnp.concatenate(tiles[KT // SUBL :] * 2, axis=0).astype(bf16)


def render_items(
    begin, end, items_ref, table_ref, colour_ref, basis_ref, result_ref, saved_refs, scratch
):
    local_refs, before_refs, left_refs = scratch
    alpha_all_ref, weight_all_ref, ends_all_ref = saved_refs
    pieces = basis_ref.shape[0]

    def multiply(found):
        return [
            exponents(table_ref, basis_ref, found[1 + 2 * slot], found[2 + 2 * slot], pieces)
            for slot in range(2)
        ]

    def front(found, powers, side):
        chained = found[0] > 0
        carry = None
        for slot in range(2):
            alphas = jnp.exp2(powers[slot])
            keep = None
            alpha_all_ref[found[5], slot * BLOCK : (slot + 1) * BLOCK, :] = alphas
            for row in range(ROWS):
                alpha = alphas[row * SUBL : (row + 1) * SUBL]
                weight = alpha if keep is None else alpha * keep
                keep = 1.0 - alpha if keep is None else keep - weight
                first = slot * BLOCK + row * SUBL
                local_refs[side][first : first + SUBL, :] = weight
            before, total = prefix_product(keep)
            if slot == 1:
                carry = jnp.where(chained, carry, 1.0)
                before, total = before * carry, total * carry
            carry = total
            before_refs[side][slot * SUBL : (slot + 1) * SUBL, :] = before
            left_refs[side][slot : slot + 1, :] = total
            ends_all_ref[found[5], slot * SUBL : (slot + 1) * SUBL, :] = before * keep

    def back(found, side):
        chained = found[0] > 0
        sums = None
        for slot in range(2):
            piece, block = found[1 + 2 * slot], found[2 + 2 * slot]
            before = before_refs[side][slot * SUBL : (slot + 1) * SUBL, :]
            weights = []
            for row in range(ROWS):
                first = slot * BLOCK + row * SUBL
                weight = local_refs[side][first : first + SUBL, :] * before
                weight_all_ref[found[5], first : first + SUBL, :] = weight
                weights.append(weight)
            high, low = split2(jnp.concatenate(weights, axis=0))
            left = colour_ref[block]
            wide = jnp.dot(left, high, preferred_element_type=f32)
            wide = (wide + jnp.dot(left, low, preferred_element_type=f32))[:SUBL]
            wide = wide + pltpu.roll(wide, 4, 0)
            sums = wide + jnp.where(chained, sums, 0.0) if slot else wide
            row_no = lax.broadcasted_iota(jnp.int32, sums.shape, 0)
            value = jnp.where(row_no == 3, 1.0 - left_refs[side][slot : slot + 1, :], sums)
            for half in range(PIX // LANES):
                first = pl.multiple_of((half * (pieces + 1) + piece) * SUBL, SUBL)
                result_ref[pl.ds(first, SUBL), :] = value[:, half * LANES : (half + 1) * LANES]

    pipelined(items_ref, pieces, begin, end, FORWARD_STEPS, multiply, front, back)


def forward_kernel(
    far_blocks_ref,
    far_live_ref,
    far_params_ref,
    far_basis_ref,
    far_owner_ref,
    far_cell_ref,
    far_target_ref,
    table_ref,
    colour_ref,
    result_ref,
    basis_ref,
    aimed_ref,
    alpha_all_ref,
    weight_all_ref,
    ends_all_ref,
    items_ref,
    blocks_ref,
    live_ref,
    params_ref,
    owner_ref,
    cell_ref,
    target_ref,
    arrivals,
    rows_ref,
    stage_ref,
    *scratch,
):
    pieces = basis_ref.shape[0]
    own_blocks = params_ref.shape[1] // BLOCK
    moves = (
        (far_blocks_ref, blocks_ref),
        (far_live_ref, live_ref),
        (far_params_ref, params_ref),
        (far_owner_ref, owner_ref),
        (far_cell_ref, cell_ref),
        (far_target_ref, target_ref),
        (far_basis_ref, basis_ref),
    )
    fetches = [
        pltpu.make_async_copy(far, near, arrivals.at[i]) for i, (far, near) in enumerate(moves)
    ]
    for fetch in fetches:
        fetch.start()
    for fetch in fetches[:3]:
        fetch.wait()
    list_items(blocks_ref, live_ref, items_ref, pieces, own_blocks)
    for block in range(own_blocks):
        rows_ref[pl.ds(block, PARAMS, stride=SUBL), :] = params_ref[
            :, block * BLOCK : (block + 1) * BLOCK
        ]
    rows = [rows_ref[i * SUBL : (i + 1) * SUBL, :] for i in range(PARAMS)]
    fill_tables(rows, None, range(own_blocks), stage_ref, table_ref, colour_ref)
    empty = own_blocks + 2
    column = lax.broadcasted_iota(jnp.int32, (BLOCK, KT), 1)
    table_ref[empty * BLOCK : (empty + 1) * BLOCK, :] = jnp.where(column == 0, -1e9, 0.0).astype(
        bf16
    )
    colour_ref[empty] = jnp.zeros((TOP, LANES), bf16)
    for fetch in fetches[3:]:
        fetch.wait()
    doms = aimed_ref.shape[0]
    width, tiles = PIX // doms, target_ref.shape[1]
    tile_lane = lax.broadcasted_iota(jnp.int32, (SUBL, LANES), 1)
    cell = cell_ref[...]
    labels = (cell % MAXD) * (doms * tiles) + owner_ref[...] * tiles + cell // MAXD
    labels = jnp.concatenate(
        [jnp.zeros((1, LANES - pieces), f32), labels.astype(f32)], axis=1
    )
    labels = jnp.broadcast_to(labels, (SUBL, LANES))
    for dom in range(doms):
        half, offset = divmod(dom * width, LANES)
        span = slice(half * LANES, (half + 1) * LANES)
        aimed = labels
        for channel in (2, 1, 0):
            shift = (channel * GROUP - offset) % LANES
            value = target_ref[channel, :, span]
            value = pltpu.roll(value, shift, 1) if shift else value
            aimed = jnp.where(tile_lane < (channel + 1) * GROUP, value, aimed)
        aimed_ref[dom] = aimed
    edge_pairs, pairs = item_ranges(items_ref, pieces)
    saved = (alpha_all_ref, weight_all_ref, ends_all_ref)
    render_items(edge_pairs, pairs, items_ref, table_ref, colour_ref, basis_ref, result_ref, saved, scratch)


def forward_edge_kernel(
    items_ref,
    inner_ref,
    outer_ref,
    aimed_ref,
    basis_ref,
    *refs,
):
    table_ref, colour_ref, result_ref, *saved, out_ref, rows_ref, stage_ref = refs[6:15]
    scratch = refs[15:]
    doms, pieces = out_ref.shape[0], basis_ref.shape[0]
    own_blocks = table_ref.shape[0] // BLOCK - 3
    region_idx, regions = lax.axis_index("region"), lax.axis_size("region")
    even = region_idx % 2 == 0
    inner, outer = inner_ref[...], outer_ref[...]
    rows_ref[pl.ds(0, PARAMS, stride=SUBL), :] = jnp.where(even, inner, outer)
    rows_ref[pl.ds(1, PARAMS, stride=SUBL), :] = jnp.where(even, outer, inner)
    rows = [rows_ref[i * SUBL : (i + 1) * SUBL, :] for i in range(PARAMS)]
    sublane = lax.broadcasted_iota(jnp.int32, (SUBL, LANES), 0)
    present = ((sublane == 0) & (region_idx < regions - 1)) | ((sublane == 1) & (region_idx > 0))
    places = (own_blocks, own_blocks + 1)
    fill_tables(rows, present, places, stage_ref, table_ref, colour_ref)
    render_items(0, item_ranges(items_ref, pieces)[0], items_ref, table_ref, colour_ref, basis_ref, result_ref, saved, scratch)
    width = PIX // doms
    lane = lax.broadcasted_iota(jnp.int32, (pieces, LANES), 1)
    tiles = aimed_ref.shape[1]
    for dom in range(doms):
        half, offset = divmod(dom * width, LANES)
        packed = None
        for channel in range(4):
            shift = (channel * GROUP - offset) % LANES
            first = half * (pieces + 1) * SUBL + channel
            value = result_ref[pl.ds(first, pieces, stride=SUBL), :]
            value = pltpu.roll(value, shift, 1) if shift else value
            packed = value if packed is None else jnp.where(lane >= channel * GROUP, value, packed)
        out_ref[dom, :pieces, :] = packed
        out_ref[dom, pieces : pieces + tiles, :] = aimed_ref[dom]


def composite_kernel(background_ref, arrived_ref, out_ref):
    doms, pieces = out_ref.shape[0], out_ref.shape[1]
    tiles = arrived_ref.shape[1] - pieces
    all_pieces, all_tiles = doms * pieces, doms * tiles
    per_row = LANES // GROUP
    lane = lax.broadcasted_iota(jnp.int32, (1, LANES), 1)
    label_rows = []
    for dom in range(doms):
        place = dom % per_row
        value = arrived_ref[dom, pieces : pieces + 1, :]
        shift = ((place - 3) * GROUP) % LANES
        value = pltpu.roll(value, shift, 1) if shift else value
        if place == 0:
            label_rows.append(value)
        else:
            label_rows[-1] = jnp.where(lane >= place * GROUP, value, label_rows[-1])
    cells_all = MAXD * all_tiles
    cell_no = lax.broadcasted_iota(jnp.int32, (cells_all, LANES), 0).astype(f32)
    to_cells = jnp.concatenate(
        [jnp.where(cell_no == row, 1.0, 0.0).astype(bf16) for row in label_rows], axis=1
    )
    upright = jnp.concatenate([jnp.broadcast_to(row, (SUBL, LANES)).T for row in label_rows], axis=0)
    cell_no = lax.broadcasted_iota(jnp.int32, (all_pieces, cells_all), 1).astype(f32)
    to_pieces = jnp.where(cell_no == upright[:, :1], 1.0, 0.0).astype(bf16)

    def moved(matrix, values):
        wide = jnp.dot(
            matrix, jnp.concatenate(split2(values), axis=1), preferred_element_type=f32
        )
        return wide[:, :LANES] + wide[:, LANES:]

    data = arrived_ref[:, :pieces, :].reshape(all_pieces, LANES)
    cells = moved(to_cells, data)
    goal = arrived_ref[:, pieces:, :].reshape(all_tiles, LANES)
    lane = lax.broadcasted_iota(jnp.int32, (all_tiles, LANES), 1)
    last = lane >= 3 * GROUP
    backdrop = jnp.where(
        lane < GROUP,
        background_ref[0],
        jnp.where(lane < 2 * GROUP, background_ref[1], background_ref[2]),
    )

    def spread(value):
        return pltpu.roll(value, GROUP, 1) + pltpu.roll(value, 2 * GROUP, 1) + pltpu.roll(
            value, 3 * GROUP, 1
        )

    fronts, through, layers = [], [], []
    front = jnp.ones((all_tiles, LANES), f32)
    composite = jnp.zeros((all_tiles, LANES), f32)
    for depth in range(MAXD):
        layer = cells[depth * all_tiles : (depth + 1) * all_tiles]
        passed = jnp.where(last, 1.0 - layer, 0.0)
        passed = passed + spread(passed)
        fronts.append(front)
        through.append(passed)
        layers.append(layer)
        composite = composite + front * layer
        front = front * passed
    residual = jnp.where(last, 0.0, composite + front * backdrop - goal)
    behind = backdrop
    grads = [None] * MAXD
    for depth in reversed(range(MAXD)):
        grads[depth] = fronts[depth] * jnp.where(last, spread(residual * behind), residual)
        behind = layers[depth] + through[depth] * behind
    back = moved(to_pieces, jnp.concatenate(grads, axis=0))
    out_ref[...] = back.reshape(out_ref.shape)


def pull_items(
    begin, end, items_ref, table_ref, basis_ref, grad_ref, sums_ref, saved_refs, scratch
):
    shade_refs, hidden_refs = scratch
    alpha_all_ref, weight_all_ref, ends_all_ref = saved_refs
    pieces = basis_ref.shape[0]

    def grads_of(piece):
        halves = []
        for half in range(PIX // LANES):
            first = pl.multiple_of((half * (pieces + 1) + piece) * SUBL, SUBL)
            halves.append(grad_ref[pl.ds(first, SUBL), :])
        grads = jnp.concatenate(halves, axis=1)
        upper = lax.broadcasted_iota(jnp.int32, grads.shape, 0) < 4
        high, middle, low = split3(grads)
        first = jnp.where(upper, high, pltpu.roll(middle, 4, 0))
        return grads, first, jnp.where(upper, high, pltpu.roll(low, 4, 0))

    def multiply(found):
        products = []
        for slot in range(2):
            piece, block = found[1 + 2 * slot], found[2 + 2 * slot]
            grads, first, second = grads_of(piece)
            rhs = jnp.concatenate([first, second], axis=0).astype(bf16)
            rhs = jnp.concatenate([jnp.zeros((KE, PIX), bf16), rhs], axis=0)
            shades = jnp.dot(table_ref[block_rows(block), :], rhs, preferred_element_type=f32)
            products.append((shades, grads[3:4]))
        return products

    def front(found, products, side):
        chained, item = found[0] > 0, found[5]
        ends = []
        for slot, (shades, final) in enumerate(products):
            span = slice(slot * BLOCK, (slot + 1) * BLOCK)
            shade_refs[side][span, :] = shades
            total = None
            for row in range(ROWS):
                first = slot * BLOCK + row * SUBL
                value = weight_all_ref[item, first : first + SUBL, :] * shades[
                    row * SUBL : (row + 1) * SUBL
                ]
                total = value if total is None else total + value
            left = ends_all_ref[item, slot * SUBL : (slot + 1) * SUBL, :]
            ends.append((total, left, final * left[SUBL - 1 :]))
        behind = None
        for slot in (1, 0):
            total, left, final = ends[slot]
            behind = jnp.where(chained, behind, final) if slot == 0 else final
            hidden, behind = suffix_sum(total, behind)
            hidden = hidden / left
            hidden_refs[side][slot * SUBL : (slot + 1) * SUBL, :] = hidden

    def back(found, side):
        along = (((1,), (1,)), ((), ()))
        for slot in range(2):
            piece, block = found[1 + 2 * slot], found[2 + 2 * slot]
            hidden = hidden_refs[side][slot * SUBL : (slot + 1) * SUBL, :]
            pulls, weights = [None] * ROWS, [None] * ROWS
            for row in reversed(range(ROWS)):
                first = slot * BLOCK + row * SUBL
                span = slice(first, first + SUBL)
                weight = weight_all_ref[found[5], span, :]
                gap = shade_refs[side][span, :] - hidden
                weights[row] = weight
                pulls[row] = weight * gap
                hidden = hidden + alpha_all_ref[found[5], span, :] * gap
            unit = basis_ref[jnp.minimum(piece, pieces - 1)][:TOP]
            _, first, second = grads_of(piece)
            g_lhs = jnp.concatenate([first, second], axis=0).astype(bf16)
            for base, left, values in ((0, unit, pulls), (2, g_lhs, weights)):
                part = None
                for value in split2(jnp.concatenate(values, axis=0)):
                    product = lax.dot_general(left, value, along, preferred_element_type=f32)
                    part = product if part is None else part + product
                for group in range(2 if base == 0 else 1):
                    row = (base + group) * SLOTS * SUBL + block * SUBL
                    rows = pl.ds(pl.multiple_of(row, SUBL), SUBL)
                    sums_ref[rows, :] = (
                        sums_ref[rows, :] + part[group * SUBL : (group + 1) * SUBL]
                    )

    pipelined(items_ref, pieces, begin, end, BACKWARD_STEPS, multiply, front, back)


def early_pairs(items_ref, pieces):
    edge_pairs, pairs = item_ranges(items_ref, pieces)
    return jnp.minimum(jnp.maximum(edge_pairs, pieces * 9 // 32), pairs), pairs


def summed_terms(sums_ref):
    def rows_of(row):
        group, place = divmod(row, SUBL)
        return sums_ref[pl.ds(group * SLOTS * SUBL + place, SLOTS, stride=SUBL), :]

    moments = [rows_of(0), rows_of(1), rows_of(2)]
    moments += [rows_of(3 + 2 * i) + rows_of(4 + 2 * i) for i in range(3)]
    terms = [value * ln_2 for value in moments]
    terms += [rows_of(TOP + i) + rows_of(TOP + 4 + i) for i in range(3)]
    order = lane_order((SLOTS, LANES), True)
    return [jnp.take_along_axis(value, order, axis=1) for value in terms]


def backward_edge_kernel(
    items_ref,
    back_ref,
    table_ref,
    basis_ref,
    alpha_all_ref,
    weight_all_ref,
    ends_all_ref,
    grad_ref,
    sums_ref,
    inner_ref,
    outer_ref,
    *scratch,
):
    doms, pieces = back_ref.shape[0], back_ref.shape[1]
    own_blocks = table_ref.shape[0] // BLOCK - 3
    width = PIX // doms
    lane = lax.broadcasted_iota(jnp.int32, (pieces, LANES), 1)
    grad_ref[...] = jnp.zeros_like(grad_ref)
    sums_ref[...] = jnp.zeros_like(sums_ref)
    for half in range(PIX // LANES):
        for channel in range(4):
            gathered = None
            for dom in range(half * LANES // width, (half + 1) * LANES // width):
                offset = dom * width - half * LANES
                shift = (offset - channel * GROUP) % LANES
                value = back_ref[dom]
                value = pltpu.roll(value, shift, 1) if shift else value
                gathered = value if gathered is None else jnp.where(lane >= offset, value, gathered)
            first = half * (pieces + 1) * SUBL + channel
            grad_ref[pl.ds(first, pieces, stride=SUBL), :] = gathered

    early, _ = early_pairs(items_ref, pieces)
    saved = (alpha_all_ref, weight_all_ref, ends_all_ref)
    pull_items(0, early, items_ref, table_ref, basis_ref, grad_ref, sums_ref, saved, scratch)
    even = lax.axis_index("region") % 2 == 0
    inner_ref[...] = jnp.zeros_like(inner_ref)
    outer_ref[...] = jnp.zeros_like(outer_ref)
    for term_no, value in enumerate(summed_terms(sums_ref)):
        high = value[own_blocks : own_blocks + 1]
        low = value[own_blocks + 1 : own_blocks + 2]
        inner_ref[term_no : term_no + 1, :] = jnp.where(even, high, low)
        outer_ref[term_no : term_no + 1, :] = jnp.where(even, low, high)


def backward_kernel(
    items_ref, table_ref, basis_ref, grad_ref, edge_sums_ref, *refs
):
    saved, own_ref, sums_ref, scratch = refs[:3], refs[3], refs[4], refs[5:]
    sums_ref[...] = edge_sums_ref[...]
    early, pairs = early_pairs(items_ref, basis_ref.shape[0])
    pull_items(
        early, pairs, items_ref, table_ref, basis_ref, grad_ref, sums_ref, saved, scratch
    )
    for term_no, value in enumerate(summed_terms(sums_ref)):
        own_ref[term_no] = value[: own_ref.shape[1]]


def update_kernel(
    params_ref,
    first_ref,
    second_ref,
    own_ref,
    inner_ref,
    outer_ref,
    gradient_ref,
    new_params_ref,
    new_first_ref,
    new_second_ref,
    rows_ref,
    grads_ref,
):
    own_blocks = own_ref.shape[1]
    for block in range(own_blocks):
        rows_ref[pl.ds(block, PARAMS, stride=own_blocks), :] = params_ref[
            :, block * BLOCK : (block + 1) * BLOCK
        ]
    rows = [rows_ref[i * own_blocks : (i + 1) * own_blocks, :] for i in range(PARAMS)]
    slot = lax.broadcasted_iota(jnp.int32, (own_blocks, LANES), 0)
    even = lax.axis_index("region") % 2 == 0
    from_low = jnp.where(even, outer_ref[...], inner_ref[...])
    from_high = jnp.where(even, inner_ref[...], outer_ref[...])
    cots = []
    for term_no in range(9):
        low = jnp.where(slot == 0, from_low[term_no : term_no + 1, :], 0.0)
        high = jnp.where(slot == own_blocks - 1, from_high[term_no : term_no + 1, :], 0.0)
        cots.append(own_ref[term_no] + low + high)
    _, pull_back = jax.vjp(splat_rows, rows)
    pulled = pull_back((cots[:6], cots[6:]))[0]
    for i in range(PARAMS):
        grads_ref[i * own_blocks : (i + 1) * own_blocks, :] = pulled[i]
    for block in range(own_blocks):
        span = slice(block * BLOCK, (block + 1) * BLOCK)
        gradient = grads_ref[pl.ds(block, PARAMS, stride=own_blocks), :]
        new_first = beta_one * first_ref[:, span] + (1 - beta_one) * gradient
        new_second = beta_two * second_ref[:, span] + (1 - beta_two) * gradient * gradient
        update = (
            new_first
            / (1 - beta_one**adam_step)
            / (jnp.sqrt(new_second / (1 - beta_two**adam_step)) + tiny)
        )
        gradient_ref[:, span] = gradient
        new_params_ref[:, span] = params_ref[:, span] - rate * update
        new_first_ref[:, span] = new_first
        new_second_ref[:, span] = new_second


def exchange(to_inner, to_outer):
    count = lax.axis_size("region")
    inner = [(i, i ^ 1) for i in range(count) if (i ^ 1) < count]
    outer = [(i, i + 1) for i in range(1, count - 1, 2)]
    outer += [(target, source) for source, target in outer]
    near = lax.ppermute(to_inner, "region", inner)
    far = lax.ppermute(to_outer, "region", outer)
    return near, far


def on_device(
    params,
    first_moment,
    second_moment,
    piece_blocks,
    piece_live,
    piece_owner,
    piece_cell,
    target,
    background,
):
    own_blocks = params.shape[1] // BLOCK
    doms = lax.axis_size("dom")
    pieces = piece_live.shape[1]
    tiles = target.shape[1]
    even = lax.axis_index("region") % 2 == 0
    low, high = params[:, :BLOCK], params[:, -BLOCK:]
    inner, outer = exchange(jnp.where(even, high, low), jnp.where(even, low, high))
    basis = jnp.asarray(pixel_basis(pieces))
    smem = pl.BlockSpec(memory_space=pltpu.SMEM)
    vmem = pl.BlockSpec(memory_space=pltpu.VMEM)
    plane = pltpu.VMEM((2 * BLOCK, PIX), f32)
    strip = pltpu.VMEM((2 * SUBL, PIX), f32)
    piece_rows = (PIX // LANES * (pieces + 1) * SUBL, LANES)
    sums_shape = (3 * SLOTS * SUBL, LANES)
    table_shape = jax.ShapeDtypeStruct(((own_blocks + 3) * BLOCK, KT), bf16)
    colour_shape = jax.ShapeDtypeStruct((own_blocks + 3, TOP, LANES), bf16)
    result_shape = jax.ShapeDtypeStruct(piece_rows, f32)
    forward_scratch = [
        pltpu.VMEM((64 * SUBL, LANES), f32),
        pltpu.VMEM(((KT // SUBL + 1) * SUBL * SUBL, LANES), f32),
        [plane] * 2,
        [strip] * 2,
        [strip] * 2,
    ]
    backward_scratch = [[plane] * 2, [strip] * 2]
    saved_shapes = tuple(
        jax.ShapeDtypeStruct((pieces + 4, rows, PIX), f32)
        for rows in (2 * BLOCK, 2 * BLOCK, 2 * SUBL)
    )
    params_limit = pltpu.CompilerParams(vmem_limit_bytes=vmem_limit)
    table, colour, result, basis, aimed, *saved, items = pl.pallas_call(
        forward_kernel,
        out_shape=(
            table_shape,
            colour_shape,
            result_shape,
            jax.ShapeDtypeStruct(basis.shape, bf16),
            jax.ShapeDtypeStruct((doms, tiles, LANES), f32),
            *saved_shapes,
            jax.ShapeDtypeStruct((2 * (3 * (pieces + SUBL) + 2),), jnp.int32),
        ),
        in_specs=[pl.BlockSpec(memory_space=pltpu.HBM)] * 7,
        out_specs=(vmem,) * 8 + (smem,),
        scratch_shapes=[
            pltpu.SMEM((2, pieces), jnp.int32),
            pltpu.SMEM((1, pieces), jnp.int32),
            pltpu.VMEM(params.shape, f32),
            pltpu.VMEM((1, pieces), jnp.int32),
            pltpu.VMEM((1, pieces), jnp.int32),
            pltpu.VMEM((3, tiles, PIX), f32),
            pltpu.SemaphoreType.DMA((7,)),
        ]
        + forward_scratch,
        compiler_params=params_limit,
        name="forward",
    )(
        *[
            pltpu.with_memory_space_constraint(value, pltpu.HBM)
            for value in (
                piece_blocks[0].T,
                piece_live,
                params,
                basis,
                piece_owner,
                piece_cell,
                jnp.transpose(target[0], (1, 0, 2)),
            )
        ]
    )
    table, _, _, *saved, payload = pl.pallas_call(
        forward_edge_kernel,
        out_shape=(
            table_shape,
            colour_shape,
            result_shape,
            *saved_shapes,
            jax.ShapeDtypeStruct((doms, pieces + tiles, LANES), f32),
        ),
        in_specs=[smem] + [vmem] * 10,
        out_specs=(vmem,) * 7,
        scratch_shapes=forward_scratch,
        input_output_aliases={5 + i: i for i in range(6)},
        compiler_params=params_limit,
        name="forward_edge",
    )(
        items,
        inner,
        outer,
        aimed,
        basis,
        table,
        colour,
        result,
        *saved,
    )
    arrived = lax.all_to_all(payload, "dom", split_axis=0, concat_axis=0, tiled=True)
    back = pl.pallas_call(
        composite_kernel,
        out_shape=jax.ShapeDtypeStruct((doms, pieces, LANES), f32),
        in_specs=[smem, vmem],
        out_specs=vmem,
        compiler_params=params_limit,
        name="composite",
    )(background, arrived)
    returned = lax.all_to_all(back, "dom", split_axis=0, concat_axis=0, tiled=True)
    grads, edge_sums, to_inner, to_outer = pl.pallas_call(
        backward_edge_kernel,
        out_shape=(
            result_shape,
            jax.ShapeDtypeStruct(sums_shape, f32),
            jax.ShapeDtypeStruct((SLOTS, LANES), f32),
            jax.ShapeDtypeStruct((SLOTS, LANES), f32),
        ),
        in_specs=[smem] + [vmem] * 6,
        out_specs=(vmem,) * 4,
        scratch_shapes=backward_scratch,
        compiler_params=params_limit,
        name="backward_edge",
    )(items, returned, table, basis, *saved)
    inner, outer = exchange(to_inner, to_outer)
    own = pl.pallas_call(
        backward_kernel,
        out_shape=jax.ShapeDtypeStruct((9, own_blocks, LANES), f32),
        in_specs=[smem] + [vmem] * 7,
        out_specs=vmem,
        scratch_shapes=[pltpu.VMEM(sums_shape, f32)] + backward_scratch,
        compiler_params=params_limit,
        name="backward",
    )(items, table, basis, grads, edge_sums, *saved)
    shape = jax.ShapeDtypeStruct(params.shape, f32)
    return pl.pallas_call(
        update_kernel,
        out_shape=(shape, shape, shape, shape),
        in_specs=[vmem] * 6,
        out_specs=(vmem,) * 4,
        scratch_shapes=[
            pltpu.VMEM((64 * own_blocks, LANES), f32),
            pltpu.VMEM((64 * own_blocks, LANES), f32),
        ],
        name="update",
        compiler_params=pltpu.CompilerParams(vmem_limit_bytes=vmem_limit),
    )(params, first_moment, second_moment, own, inner, outer)


def solution(mesh):
    in_specs = (
        P(None, ("region", "dom")),
        P(None, ("region", "dom")),
        P(None, ("region", "dom")),
        P(("region", "dom"), None, None),
        P(("region", "dom"), None),
        P(("region", "dom"), None),
        P(("region", "dom"), None),
        P(("region", "dom"), None, None, None),
        P(),
    )
    out_specs = (P(None, ("region", "dom")),) * 4
    return jax.shard_map(
        on_device, mesh=mesh, in_specs=in_specs, out_specs=out_specs, check_vma=False
    )
```
